32 devices in a mesh: ma: 8 (over z, y), row: 4 (over x, core).
Axes of the slice: x: 2, y: 2, z: 4, core: 2. Of those that a mesh axis runs over, the one named last changes fastest.
Arguments:
- velocity: bfloat16 [3, 2, 16, 32, 65], P(None, None, 'row', 'ma'), may hold values from -6 to 6
- vorticity: bfloat16 [3, 2, 16, 32, 65], P(None, None, 'row', 'ma'), may hold values from -6 to 6
- legendre: bfloat16 [32, 65, 384], P('ma'), may hold values from -0.75 to 0.75
- pair_order: int32 [32], P('ma'), may hold values from 0 to 31, each once
- lat_weight: float32 [384], replicated, may hold values from 0.5 to 2
- diffusivity: float32 [16], replicated, may hold values from 0.25 to 2.5
Outputs:
- new_velocity: float32 [3, 2, 16, 32, 65], P(None, None, 'row', 'ma')
The draws below stay inside these ranges and needn't reach their ends.
Inputs may be any that keep to these rules, and one draw needn't show every extreme that they name: pair_order holds each of 0 to 31 exactly once.
All inputs are finite; a program needn't handle non-finite values.
Results may differ from the reference program's by a relative error of at most 0.0095.
Values may be sent and summed in bfloat16 or wider, within the bound.
A program may use at most 128 MiB of HBM per device.

```python
import math
import jax
import jax.numpy as jnp
from jax import lax

ORDERS = 64
PAIRS = 32
PACK = 65
NLAT = 768
NH = 384
NLON = 2048
LEVELS = 16


def shard_levels(rng, dims, cuts, least, largest):
    def one(position, shards_of):
        heights = jax.random.uniform(jax.random.fold_in(jax.random.fold_in(rng, 6), position), (shards_of,), jnp.float32, least / len(cuts), largest / len(cuts))
        return jnp.repeat(jnp.exp(heights), dims[position] // shards_of).reshape((-1,) + (1,) * (len(dims) - position - 1))

    gain = one(*cuts[0])
    for cut in cuts[1:]:
        gain = gain * one(*cut)
    return gain


def bell_draw(own_key, extent, scale, bound, cuts=(), kind=jnp.bfloat16):
    drawn = jax.random.normal(own_key, extent, jnp.float32) * scale
    if len(cuts) > 0:
        drawn = shard_levels(own_key, extent, cuts, -0.22, 0.18) * drawn
    return jnp.clip(drawn, min=-bound, max=bound).astype(kind)


def setup_inputs(seed: int = 0) -> dict:
    splits = jax.random.split(jax.random.key(seed), 7)
    velocity = bell_draw(splits[0], (3, 2, LEVELS, PAIRS, PACK), 1.0, 6.0, ((2, 4), (3, 8)))
    vorticity = bell_draw(splits[1], (3, 2, LEVELS, PAIRS, PACK), 1.0, 6.0, ((2, 4), (3, 8)))
    legendre = bell_draw(splits[2], (PAIRS, PACK, NH), ORDERS ** -0.5, 0.75, ((0, 8),))
    pair_order = jax.random.permutation(splits[3], PAIRS).astype(jnp.int32)
    lat_weight = jnp.clip(jnp.exp(jax.random.uniform(splits[4], (NH,), jnp.float32, math.log(0.5), math.log(2.0))), 0.5, 2.0)
    diffusivity = jnp.clip(jnp.exp(jax.random.uniform(splits[5], (LEVELS,), jnp.float32, math.log(0.25), math.log(2.5))), 0.25, 2.5)
    return {"velocity": velocity, "vorticity": vorticity, "legendre": legendre, "pair_order": pair_order, "lat_weight": lat_weight, "diffusivity": diffusivity}


STEP_SIZE = 1.0

def row_masks(low_order):
    row_index = jnp.arange(PACK, dtype=jnp.int32)[None, :]
    low_column = low_order[:, None]
    is_lower = row_index < ORDERS - low_column
    not_lower = jnp.logical_not(is_lower)
    even_low = row_index % 2 == 0
    even_high = (row_index + low_column) % 2 == 0
    low_pair = jnp.stack([is_lower & even_low, is_lower & jnp.logical_not(even_low)])
    high_pair = jnp.stack([not_lower & even_high, not_lower & jnp.logical_not(even_high)])
    return jnp.stack([low_pair, high_pair]).astype(jnp.float32)

def cross_product(velocity_grid, vorticity_grid):
    return jnp.stack([velocity_grid[1] * vorticity_grid[2] - velocity_grid[2] * vorticity_grid[1], velocity_grid[2] * vorticity_grid[0] - velocity_grid[0] * vorticity_grid[2], velocity_grid[0] * vorticity_grid[1] - velocity_grid[1] * vorticity_grid[0]])

def synth_pair(packed):
    coeffs, legendre_rows, low_order = packed
    mask_table = row_masks(low_order[None])[:, :, 0]
    masked = coeffs.astype(jnp.float32)[None, None] * mask_table[:, :, None, None, None, :]
    halves = jnp.einsum('oqfilr,rj->qflioj', masked, legendre_rows.astype(jnp.float32))
    north_part = halves[0] + halves[1]
    south_part = halves[0] - halves[1]
    return jnp.concatenate([north_part, south_part], axis=-1).astype(jnp.bfloat16)

def grid_level(spectra):
    values = lax.optimization_barrier(spectra).astype(jnp.float32)
    doubled = jnp.where(jnp.arange(ORDERS) == 0, 2.0, 1.0).astype(values.dtype)
    coefficient = lax.complex(values[:, 0] * doubled, values[:, 1] * doubled)
    coefficient = jnp.pad(coefficient, ((0, 0), (0, 0), (0, NLON // 2 + 1 - ORDERS)))
    fields = jnp.fft.irfft(coefficient, n=NLON, axis=-1) * (NLON / (2.0 * math.sqrt(ORDERS)))
    lamb_vector = cross_product(fields[:3], fields[3:])
    spectrum = jnp.fft.rfft(lamb_vector, axis=-1)[..., :ORDERS] / math.sqrt(NLON)
    return jnp.stack([jnp.real(spectrum), jnp.imag(spectrum)], axis=1).astype(jnp.bfloat16)

def jacobi_sweep(current, source, coupling):
    padded = jnp.pad(current, ((0, 0), (0, 0), (1, 1), (0, 0), (0, 0)))
    return (source + coupling * (padded[:, :, :-2] + padded[:, :, 2:])) / (1.0 + 2.0 * coupling)

def reference(velocity, vorticity, legendre, pair_order, lat_weight, diffusivity):
    fields = jnp.concatenate([velocity, vorticity], axis=0)
    by_pair = jnp.transpose(fields, (3, 0, 1, 2, 4))
    synthesized = lax.map(synth_pair, (by_pair, legendre, pair_order))
    low_part = synthesized[:, :, :, :, 0]
    high_part = synthesized[:, :, :, :, 1]
    by_order = jnp.zeros((ORDERS, 6, LEVELS, 2, NLAT), jnp.bfloat16)
    by_order = by_order.at[pair_order].set(low_part).at[ORDERS - 1 - pair_order].set(high_part)
    by_level = jnp.transpose(by_order, (2, 1, 3, 4, 0))
    lamb_spectra = lax.map(grid_level, by_level)
    lamb_by_order = jnp.transpose(lamb_spectra, (4, 0, 1, 2, 3))

    def analyse_pair(packed):
        legendre_rows, low_order = packed
        mask_table = row_masks(low_order[None])[:, :, 0]
        chosen = jnp.stack([lamb_by_order[low_order], lamb_by_order[ORDERS - 1 - low_order]])
        chosen = lax.optimization_barrier(chosen).astype(jnp.float32)
        north_part = chosen[..., :NH]
        south_part = chosen[..., NH:]
        weighted = jnp.stack([lat_weight * (north_part + south_part), lat_weight * (north_part - south_part)])
        weighted = lax.optimization_barrier(weighted.astype(jnp.bfloat16)).astype(jnp.float32)
        projected = jnp.einsum('qolfij,rj->qolfir', weighted, legendre_rows.astype(jnp.float32))
        selector = jnp.transpose(mask_table, (1, 0, 2))[:, :, None, None, None, :]
        picked = lax.optimization_barrier(jnp.sum(projected * selector, axis=(0, 1)))
        return jnp.transpose(picked, (1, 2, 0, 3))
    tendency = lax.map(analyse_pair, (legendre, pair_order))
    tendency = jnp.transpose(tendency, (1, 2, 3, 0, 4))
    source = velocity.astype(jnp.float32) + STEP_SIZE * tendency
    coupling = diffusivity[None, None, :, None, None]
    first_pass = jacobi_sweep(source, source, coupling)
    return jacobi_sweep(first_pass, source, coupling)
```

```python
import functools
import math

import jax
import jax.numpy as jnp
import numpy as np
from jax import lax
from jax.experimental import pallas as pl
from jax.experimental.pallas import tpu as pltpu
from jax.sharding import PartitionSpec as P

NLON = 2048


STEP_SIZE = 1.0


def with_halo(cells, sides, width):
    for axis, dim in sides:
        count = lax.axis_size(axis)
        ends = count - 1
        head = lax.slice_in_dim(cells, 0, width, axis=dim)
        tail = lax.slice_in_dim(cells, cells.shape[dim] - width, cells.shape[dim], axis=dim)
        cells = jnp.concatenate(
            [
                lax.ppermute(tail, axis, [(i, (i + 1) % count) for i in range(ends)]),
                cells,
                lax.ppermute(head, axis, [((i + 1) % count, i) for i in range(ends)]),
            ],
            axis=dim,
        )
    return cells


def row_masks(low_order, pack_rows):
    orders_all = pack_rows - 1
    row_index = jnp.arange(pack_rows, dtype=jnp.int32)[None, :]
    low_column = low_order[:, None]
    is_lower = row_index < orders_all - low_column
    not_lower = jnp.logical_not(is_lower)
    even_low = row_index % 2 == 0
    even_high = (row_index + low_column) % 2 == 0
    low_pair = jnp.stack([is_lower & even_low, is_lower & jnp.logical_not(even_low)])
    high_pair = jnp.stack([not_lower & even_high, not_lower & jnp.logical_not(even_high)])
    return jnp.stack([low_pair, high_pair])


def cross_product(velocity_grid, vorticity_grid):
    return jnp.stack(
        [
            velocity_grid[1] * vorticity_grid[2] - velocity_grid[2] * vorticity_grid[1],
            velocity_grid[2] * vorticity_grid[0] - velocity_grid[0] * vorticity_grid[2],
            velocity_grid[0] * vorticity_grid[1] - velocity_grid[1] * vorticity_grid[0],
        ]
    )


def lon_table(column_order, is_imag, lon_start, lon_count):
    lon_index = lon_start + jnp.arange(lon_count, dtype=jnp.int32)
    angle_index = column_order[:, None] * lon_index[None, :] % NLON
    angle_value = angle_index.astype(jnp.float32) * (2.0 * math.pi / NLON)
    return jnp.where(is_imag[:, None], -jnp.sin(angle_value), jnp.cos(angle_value))


def local(velocity, vorticity, legendre, pair_order, lat_weight, diffusivity):
    pair_count = pair_order.shape[0]
    pack_rows = legendre.shape[1]
    half_lat = legendre.shape[2]
    nlat_all = 2 * half_lat
    levels_dev = velocity.shape[2]
    orders_all = pack_rows - 1
    inv_orders = 1.0 / math.sqrt(orders_all)
    inv_lon = 1.0 / math.sqrt(NLON)
    lon_width = NLON // 4
    mask_bool = row_masks(pair_order, pack_rows)
    fields = jnp.concatenate([velocity, vorticity], axis=0)
    masked = fields[None, None] * mask_bool.astype(jnp.bfloat16)[:, :, None, None, None]
    halves = jnp.einsum(
        "oqfilsr,srj->qfliosj", masked, legendre, preferred_element_type=jnp.float32
    )
    north_part = halves[0] + halves[1]
    south_part = halves[0] - halves[1]
    both_parts = jnp.concatenate([north_part, south_part], axis=-1)
    spectral = jnp.transpose(both_parts, (0, 1, 5, 2, 3, 4))
    spectral = spectral.reshape(6, levels_dev, nlat_all, 4 * pair_count).astype(jnp.bfloat16)
    gathered_ids = lax.all_gather(pair_order, "ma", axis=0, tiled=True)
    pair_slots = gathered_ids.reshape(-1, 1, 1, pair_count)
    both_orders = jnp.concatenate([pair_slots, orders_all - 1 - pair_slots], axis=2)
    full_shape = (both_orders.shape[0], 2, 2, pair_count)
    column_order = jnp.broadcast_to(both_orders, full_shape).reshape(-1)
    part_index = jnp.arange(2, dtype=jnp.int32)[None, :, None, None]
    is_imag = jnp.broadcast_to(part_index, full_shape).reshape(-1) == 1
    tables = [
        lon_table(column_order, is_imag, lon_block * lon_width, lon_width).astype(jnp.bfloat16)
        for lon_block in range(4)
    ]
    spec_block = lax.all_to_all(spectral, "ma", split_axis=2, concat_axis=3, tiled=True)
    accumulated = jnp.zeros((3,) + spec_block.shape[1:], jnp.float32)
    for lon_block in range(4):
        table_block = tables[lon_block]
        grid_values = (
            jnp.einsum("flac,cb->flab", spec_block, table_block, preferred_element_type=jnp.float32)
            * inv_orders
        )
        lamb_vector = cross_product(grid_values[:3], grid_values[3:])
        accumulated = accumulated + jnp.einsum(
            "flab,cb->flac",
            lamb_vector,
            table_block.astype(jnp.float32),
            precision=lax.Precision.HIGH,
            preferred_element_type=jnp.float32,
        )
    lamb_spec = (accumulated * inv_lon).astype(jnp.bfloat16)
    selector = jnp.transpose(mask_bool.astype(jnp.float32), (1, 0, 2, 3))[:, None, None, None]
    lamb_block = lax.all_to_all(lamb_spec, "ma", split_axis=3, concat_axis=2, tiled=True)
    item_count = lamb_block.shape[0]
    shaped = lamb_block.astype(jnp.float32).reshape(
        item_count, levels_dev, nlat_all, 2, 2, pair_count
    )
    shaped = jnp.transpose(shaped, (0, 1, 3, 4, 5, 2))
    north_side = shaped[..., :half_lat]
    south_side = shaped[..., half_lat:]
    weighted = jnp.stack(
        [lat_weight * (north_side + south_side), lat_weight * (north_side - south_side)]
    )
    weighted = weighted.astype(jnp.bfloat16)
    projected = jnp.einsum(
        "qfliosj,srj->qfliosr", weighted, legendre, preferred_element_type=jnp.float32
    )
    picked = jnp.sum(projected * selector, axis=(0, 4))
    tendency = jnp.transpose(picked, (0, 2, 1, 3, 4))
    source = velocity.astype(jnp.float32) + STEP_SIZE * tendency
    row_start = lax.axis_index("row") * levels_dev
    level_total = levels_dev * lax.axis_size("row")
    extended = with_halo(source.astype(jnp.bfloat16), (("row", 2),), 2).astype(source.dtype)
    padded_coupling = jnp.pad(diffusivity, (2, 2))
    wide_coupling = lax.dynamic_slice_in_dim(padded_coupling, row_start, levels_dev + 4)[
        None, None, :, None, None
    ]
    inner_coupling = wide_coupling[:, :, 1:-1]
    first_wide = (
        extended[:, :, 1:-1] + inner_coupling * (extended[:, :, :-2] + extended[:, :, 2:])
    ) / (1.0 + 2.0 * inner_coupling)
    global_level = row_start - 1 + jnp.arange(levels_dev + 2, dtype=jnp.int32)
    inside = ((global_level >= 0) & (global_level < level_total)).astype(jnp.float32)
    first_wide = first_wide * inside[None, None, :, None, None]
    own_coupling = wide_coupling[:, :, 2:-2]
    return (source + own_coupling * (first_wide[:, :, :-2] + first_wide[:, :, 2:])) / (
        1.0 + 2.0 * own_coupling
    )

def lon_count(orders_all):
    need = 3 * (orders_all - 1) + 1
    return min(NLON, -(-need // 64) * 64)


def remote(src, dst, send_sem, recv_sem, device_id):
    return pltpu.make_async_remote_copy(
        src_ref=src,
        dst_ref=dst,
        send_sem=send_sem,
        recv_sem=recv_sem,
        device_id=device_id,
        device_id_type=pl.DeviceIdType.MESH,
    )


def fused_kernel(
    n_ma, n_row, pairs, rows, levels, scale,
    velocity_hbm, vorticity_hbm, legendre_hbm, order_hbm, weight_hbm, dif_hbm, tab_hbm, tab_t_hbm,
    out_ref,
    velocity_ref, vorticity_ref, legendre_ref, order_ref, weight_ref, dif_ref, tab_ref, tab_t_ref, load_sem,
    leg_rows, leg_ref, rest_ref, coef_all, leg_all, rest_all, rest_t, onehot, ops, spec, wgt, part, part_in, ext, halo,
    coef_send, coef_recv, leg_send, leg_recv, swap_send, swap_recv, rest_send, rest_recv, part_send, part_recv, halo_send, halo_recv,
):
    me = lax.axis_index("ma")
    row = lax.axis_index("row")
    _, chunks, groups, wide = coef_all.shape
    coef_ref = coef_all.at[0]
    lanes = (chunks + 1) * wide
    fields2 = groups // 2
    orders = rows - 1
    slots = 2 * pairs
    full = n_ma * slots
    lat = leg_ref.shape[2]
    side = wide // 2
    main = pairs * orders
    per_chunk = pairs // chunks
    f32 = jnp.float32
    bf16 = jnp.bfloat16
    n_z = n_ma // 2
    z, y = me // 2, lax.rem(me, 2)
    half = lax.rem(row, 2)
    mate_row = row + 1 - 2 * half

    def target(s):
        return lax.rem(z + s // 2, n_z) * 2 + lax.rem(y + lax.rem(s, 2), 2)

    def origin(s):
        return lax.rem(z + n_z - s // 2, n_z) * 2 + lax.rem(y + lax.rem(s, 2), 2)

    left = lax.rem(row + n_row - 1, n_row)
    right = lax.rem(row + 1, n_row)

    barrier = pltpu.get_barrier_semaphore()
    for d in range(1, n_ma):
        pl.semaphore_signal(
            barrier, inc=1, device_id=(lax.rem(me + d, n_ma), row), device_id_type=pl.DeviceIdType.MESH
        )
    for beside in (left, right):
        pl.semaphore_signal(barrier, inc=1, device_id=(me, beside), device_id_type=pl.DeviceIdType.MESH)

    loads = [
        pltpu.make_async_copy(src, dst, load_sem.at[i])
        for i, (src, dst) in enumerate(
            [
                (legendre_hbm, legendre_ref),
                (velocity_hbm, velocity_ref),
                (vorticity_hbm, vorticity_ref),
                (order_hbm, order_ref),
                (weight_hbm, weight_ref),
                (dif_hbm, dif_ref),
                (tab_hbm, tab_ref),
                (tab_t_hbm, tab_t_ref),
            ]
        )
    ]
    for load in loads:
        load.start()
    for load in loads[:4]:
        load.wait()

    for r in range(rows):
        values = legendre_ref[r].astype(f32)
        for t in range(leg_rows.shape[0]):
            leg_rows[t, r * pairs : (r + 1) * pairs, :] = values[:, t * wide : (t + 1) * wide]
    packs = [
        jnp.concatenate([velocity_ref[...].astype(f32)[:, p], vorticity_ref[...].astype(f32)[:, p]], axis=0)
        for p in range(pairs)
    ]
    column = lax.broadcasted_iota(jnp.int32, (groups, wide), 1)
    ends = jnp.zeros((groups, wide), f32)
    for p in range(pairs):
        ends = jnp.where(column == p, packs[p][:, orders:], ends)
    ends = jnp.concatenate([ends, jnp.zeros((wide - groups, wide), f32)], axis=0)
    ends = jnp.transpose(ends)[0:pairs, 0:side]
    tails = jnp.concatenate([leg_rows[t, main : main + pairs, :] for t in range(leg_rows.shape[0])], axis=1)
    order_rows = [jnp.full((1, wide), order_ref[p].astype(f32)) for p in range(pairs)]
    filler = jnp.zeros((pairs, side - lat), f32)
    for b in range(n_ma):
        data_rows = jnp.concatenate([ends, tails[:, b * lat : (b + 1) * lat], filler], axis=1)
        rest_ref[b] = jnp.concatenate([data_rows] + order_rows, axis=0).astype(bf16)
    for c in range(chunks):
        members = range(c * per_chunk, (c + 1) * per_chunk)
        coef_all[0, c] = jnp.concatenate([packs[p][:, :orders] for p in members], axis=1).astype(bf16)
        turned = jnp.concatenate(
            [
                jnp.transpose(
                    jnp.concatenate([leg_rows[t, pl.ds(p, orders, stride=pairs), :] for p in members], axis=0)
                )
                for t in range(leg_rows.shape[0])
            ],
            axis=0,
        ).astype(bf16)
        for b in range(n_ma):
            leg_ref[b, c] = turned[b * lat : (b + 1) * lat]

    pl.semaphore_wait(barrier, n_ma + 1)

    def coef_copy(s):
        return remote(coef_ref, coef_all.at[s], coef_send.at[s], coef_recv.at[s], (target(s), row))

    def leg_copy(s):
        peer = target(s)
        return remote(
            leg_ref.at[peer, half], leg_all.at[s, half], leg_send.at[s], leg_recv.at[s], (peer, row)
        )

    def swap_copy(s):
        return remote(
            leg_all.at[s, half], leg_all.at[s, half], swap_send.at[s], swap_recv.at[s], (me, mate_row)
        )

    def swap_arrival(s):
        return remote(
            leg_all.at[s, half], leg_all.at[s, 1 - half], swap_send.at[s], swap_recv.at[s], (me, mate_row)
        )

    def rest_copy(s):
        peer = target(s)
        return remote(rest_ref.at[peer], rest_all.at[s], rest_send.at[s], rest_recv.at[s], (peer, row))

    far_first = sorted(range(1, n_ma), key=lambda s: (-min(s // 2, n_z - s // 2), -(s % 2)))
    near_first = far_first[::-1]
    for s in far_first:
        rest_copy(s).start()
    for s in far_first:
        leg_copy(s).start()
    for s in far_first:
        coef_copy(s).start()

    leg_all[0] = leg_ref[me]
    rest_all[0] = rest_ref[me]

    def clear(d, carry):
        ops[d] = jnp.zeros(ops.shape[1:], bf16)
        return carry

    lax.fori_loop(0, n_ma, clear, 0)
    for load in loads[4:]:
        load.wait()
    weight = jnp.zeros((1, lat), f32)
    for b in range(n_ma):
        weight = jnp.where(me == b, weight_ref[...].reshape(1, -1)[:, b * lat : (b + 1) * lat], weight)
    weight = weight * scale
    gap = jnp.zeros((1, side - lat), f32)
    weight = jnp.concatenate([weight, gap, weight, gap] * 2, axis=1)

    lane = lax.broadcasted_iota(jnp.int32, (pairs, wide), 1)
    sub = lax.broadcasted_iota(jnp.int32, (pairs, wide), 0)
    m_lane = lax.broadcasted_iota(jnp.int32, (slots, orders), 1)
    m_sub = lax.broadcasted_iota(jnp.int32, (slots, orders), 0)
    lane_row = lane % orders
    own = lane // orders == sub % per_chunk

    def low_orders(d):
        return rest_all[d].astype(f32)[pairs:].astype(jnp.int32)

    def place(d):
        low = low_orders(d)
        order = jnp.zeros((slots, orders), jnp.int32)
        for p in range(pairs):
            value = low[p : p + 1, 0:1]
            order = jnp.where(m_sub == 2 * p, value, order)
            order = jnp.where(m_sub == 2 * p + 1, orders - 1 - value, order)
        onehot[d * slots : (d + 1) * slots, :] = (m_lane == order).astype(f32)

    def synth(d):
        low = low_orders(d)
        lower = lane_row < orders - low
        north_low = (own & lower).astype(f32)
        north_high = (own & jnp.logical_not(lower)).astype(f32)
        south_low = north_low * (1 - 2 * (lane_row & 1)).astype(f32)
        south_high = north_high * (1 - 2 * ((lane_row + low) & 1)).astype(f32)
        north_end = (lane == 8 * d + sub).astype(f32)
        south_end = north_end * (1 - 2 * (low & 1)).astype(f32)
        end_leg = rest_t[side : side + lat, :]
        end_coef = rest_t[0:groups, :].astype(bf16)
        for p in range(pairs):
            c = p // per_chunk
            table = leg_all[d, c].astype(f32)
            at = p * 2 * wide
            for i, factor in enumerate((north_low, south_low, north_high, south_high)):
                ops[d, at + i * side : at + i * side + lat, 0:wide] = (table * factor[p : p + 1]).astype(bf16)
            for i, factor in enumerate((north_end, south_end)):
                first = at + wide + i * side
                ops[d, first : first + lat, wide : 2 * wide] = (end_leg * factor[p : p + 1]).astype(bf16)
            lhs = jnp.concatenate([coef_all[d, c], end_coef], axis=1)
            made = lax.dot_general(
                lhs, ops[d, at : at + 2 * wide, :], (((1,), (1,)), ((), ())), preferred_element_type=f32
            )
            for i in range(2):
                spec[pl.ds(d * slots + 2 * p + i, groups, stride=full), :] = made[:, i * wide : (i + 1) * wide]

    for s in near_first:
        rest_copy(s).wait_recv()
    rest = rest_all[...].astype(f32).reshape(n_ma * 8, wide)
    rest = jnp.concatenate([rest, jnp.zeros((wide - n_ma * 8, wide), f32)], axis=0)
    rest_t[...] = jnp.transpose(rest)
    for d in range(n_ma):
        place(d)
    hot = onehot[...].astype(bf16)
    to_grid = jnp.concatenate(
        [
            lax.dot_general(tab_t_ref[c], hot, (((1,), (1,)), ((), ())), preferred_element_type=f32)
            for c in range(2)
        ],
        axis=1,
    ).astype(bf16)
    to_spec = jnp.concatenate(
        [jnp.dot(hot, tab_ref[c], preferred_element_type=f32) for c in range(2)], axis=0
    ).astype(bf16)
    synth(0)
    for s in near_first:
        leg_copy(s).wait_recv()
        swap_copy(s).start()
    for s in near_first:
        coef_copy(s).wait_recv()
        swap_arrival(s).wait_recv()
        synth(s)

    def middle(j, carry):
        grids = []
        for f in range(6):
            blocks = []
            for i in range(2):
                k = 2 * j + i
                parts = [
                    spec[pl.ds(pl.multiple_of(((f * 2 + c) * levels + k) * full, full), full), :] for c in range(2)
                ]
                blocks.append(jnp.concatenate(parts, axis=0))
            block = jnp.concatenate(blocks, axis=1).astype(bf16)
            grids.append(jnp.dot(to_grid, block, preferred_element_type=f32))
        u, w = grids[:3], grids[3:]
        lamb = [
            u[1] * w[2] - u[2] * w[1],
            u[2] * w[0] - u[0] * w[2],
            u[0] * w[1] - u[1] * w[0],
        ]
        for f in range(3):
            made = jnp.dot(to_spec, lamb[f].astype(bf16), preferred_element_type=f32) * weight
            for i in range(2):
                k = 2 * j + i
                for c in range(2):
                    at = pl.multiple_of(((f * 2 + c) * levels + k) * full, full)
                    wgt[pl.ds(at, full), :] = made[c * full : (c + 1) * full, i * wide : (i + 1) * wide]
        return carry

    lax.fori_loop(0, levels // 2, middle, 0)

    def part_copy(d):
        return remote(part.at[d], part_in.at[d], part_send.at[d], part_recv.at[d], (origin(d), row))

    def analyse(d):
        heads = []
        tail = None
        for c in range(chunks):
            picked = []
            for p in range(c * per_chunk, (c + 1) * per_chunk):
                for i in range(2):
                    picked.append(wgt[pl.ds(d * slots + 2 * p + i, fields2, stride=full), :])
            lhs = jnp.concatenate(picked, axis=1).astype(bf16)
            first = c * per_chunk * 2 * wide
            made = jnp.dot(lhs, ops[d, first : first + per_chunk * 2 * wide, :], preferred_element_type=f32)
            heads.append(made[:, :wide])
            tail = made[:, wide:] if tail is None else tail + made[:, wide:]
        return jnp.concatenate(heads + [tail], axis=1)

    def project(i, carry):
        d = n_ma - i
        part[d] = analyse(d).astype(bf16)
        part_copy(d).start()
        return carry

    lax.fori_loop(1, n_ma, project, 0)
    source = analyse(0)

    def gather(i, total):
        d = n_ma - i
        part_copy(d).wait_recv()
        return total + part_in[d].astype(f32)

    source = lax.fori_loop(1, n_ma, gather, source)
    tail = source[:, main:]
    for shift in (8, 16, 32):
        tail = tail + pltpu.roll(tail, wide - shift, 1)
    own_tail = rest_t[0:fields2, :]
    heads = [source[:, c * wide : (c + 1) * wide] + coef_ref[c, 0:fields2].astype(f32) for c in range(chunks)]
    source = jnp.concatenate(heads + [tail + own_tail], axis=1)
    source = source.reshape(fields2 // levels, levels, lanes)
    own_levels = [source[:, k, :] for k in range(levels)]
    for i in range(2):
        halo[0, i] = own_levels[i].astype(bf16)
        halo[1, i] = own_levels[levels - 2 + i].astype(bf16)
    to_left = remote(halo.at[0], ext.at[1], halo_send.at[0], halo_recv.at[1], (me, left))
    to_right = remote(halo.at[1], ext.at[0], halo_send.at[1], halo_recv.at[0], (me, right))
    from_left = remote(halo.at[1], ext.at[0], halo_send.at[1], halo_recv.at[0], (me, left))
    from_right = remote(halo.at[0], ext.at[1], halo_send.at[0], halo_recv.at[1], (me, right))

    @pl.when(row > 0)
    def _():
        to_left.start()

    @pl.when(row < n_row - 1)
    def _():
        to_right.start()

    for s in range(1, n_ma):
        coef_copy(s).wait_send()
        leg_copy(s).wait_send()
        swap_copy(s).wait_send()
        rest_copy(s).wait_send()
        part_copy(s).wait_send()

    @pl.when(row > 0)
    def _():
        to_left.wait_send()
        from_left.wait_recv()

    @pl.when(row == 0)
    def _():
        ext[0] = jnp.zeros(ext.shape[1:], bf16)

    @pl.when(row < n_row - 1)
    def _():
        to_right.wait_send()
        from_right.wait_recv()

    @pl.when(row == n_row - 1)
    def _():
        ext[1] = jnp.zeros(ext.shape[1:], bf16)

    shape = (fields2 // levels, lanes)
    has_left = (row > 0).astype(f32)
    has_right = (row < n_row - 1).astype(f32)
    wide_levels = [ext[0, i].astype(f32) for i in range(2)] + own_levels + [ext[1, i].astype(f32) for i in range(2)]
    coupling = [jnp.full(shape, dif_ref[lax.rem((row + n_row) * levels + i - 2, n_row * levels)]) for i in range(levels + 4)]
    inverse = [1.0 / (1.0 + 2.0 * c) for c in coupling]
    first = [
        (wide_levels[i] + coupling[i] * (wide_levels[i - 1] + wide_levels[i + 1])) * inverse[i]
        for i in range(1, levels + 3)
    ]
    first[0] = first[0] * has_left
    first[-1] = first[-1] * has_right
    for k in range(levels):
        done = (wide_levels[k + 2] + coupling[k + 2] * (first[k] + first[k + 2])) * inverse[k + 2]
        for p in range(pairs):
            line = jnp.concatenate(
                [done[:, p * orders : (p + 1) * orders], done[:, main + p : main + p + 1]], axis=1
            )
            for i in range(fields2 // levels):
                out_ref[i * levels + k, p : p + 1, :] = line[i : i + 1]


def fused(velocity, vorticity, legendre, pair_order, lat_weight, diffusivity):
    n_ma = lax.axis_size("ma")
    n_row = lax.axis_size("row")
    pairs, rows, half_lat = legendre.shape
    levels = velocity.shape[2]
    orders = rows - 1
    main = pairs * orders
    chunks = main // 128
    lanes = main + 128
    lat = half_lat // n_ma
    slots = 2 * pairs
    full = n_ma * slots
    points = lon_count(orders)
    bf16 = jnp.bfloat16
    f32 = jnp.float32
    groups = 12 * levels
    scale = (NLON / points) / math.sqrt(NLON) / orders
    angle = np.outer(np.arange(orders), np.arange(points)) % points * (2.0 * math.pi / points)
    table = np.stack([np.cos(angle), -np.sin(angle)])
    tab = jnp.asarray(table, bf16)
    tab_t = jnp.asarray(np.transpose(table, (0, 2, 1)), bf16)
    vmem = pl.BlockSpec(memory_space=pltpu.VMEM)
    away = pl.BlockSpec(memory_space=pltpu.HBM)
    operands = (
        velocity.reshape(6 * levels, pairs, rows),
        vorticity.reshape(6 * levels, pairs, rows),
        jnp.transpose(legendre, (1, 0, 2)),
        pair_order,
        lat_weight,
        diffusivity,
        tab,
        tab_t,
    )
    out = pl.pallas_call(
        functools.partial(fused_kernel, n_ma, n_row, pairs, rows, levels, scale),
        out_shape=jax.ShapeDtypeStruct((6 * levels, pairs, rows), f32),
        in_specs=[away] * 8,
        out_specs=vmem,
        scratch_shapes=[
            pltpu.VMEM((6 * levels, pairs, rows), bf16),
            pltpu.VMEM((6 * levels, pairs, rows), bf16),
            pltpu.VMEM((rows, pairs, half_lat), bf16),
            pltpu.SMEM((pairs,), jnp.int32),
            pltpu.VMEM((half_lat,), f32),
            pltpu.SMEM(diffusivity.shape, f32),
            pltpu.VMEM(tab.shape, bf16),
            pltpu.VMEM(tab_t.shape, bf16),
            pltpu.SemaphoreType.DMA((8,)),
            pltpu.VMEM((half_lat // 128, rows * pairs + 4, 128), f32),
            pltpu.VMEM((n_ma, chunks, lat, 128), bf16),
            pltpu.VMEM((n_ma, 8, 128), bf16),
            pltpu.VMEM((n_ma, chunks, groups, 128), bf16),
            pltpu.VMEM((n_ma, chunks, lat, 128), bf16),
            pltpu.VMEM((n_ma, 8, 128), bf16),
            pltpu.VMEM((128, 128), f32),
            pltpu.VMEM((full, orders), f32),
            pltpu.VMEM((n_ma, pairs * 256, 256), bf16),
            pltpu.VMEM((groups * full, 128), f32),
            pltpu.VMEM((groups // 2 * full, 128), f32),
            pltpu.VMEM((n_ma, groups // 2, lanes), bf16),
            pltpu.VMEM((n_ma, groups // 2, lanes), bf16),
            pltpu.VMEM((2, 2, 6, lanes), bf16),
            pltpu.VMEM((2, 2, 6, lanes), bf16),
        ]
        + [pltpu.SemaphoreType.DMA((n_ma,))] * 10
        + [pltpu.SemaphoreType.DMA((2,))] * 2,
        compiler_params=pltpu.CompilerParams(
            collective_id=0, has_side_effects=True, vmem_limit_bytes=48 * 1024 * 1024
        ),
    )(*(pltpu.with_memory_space_constraint(x, pltpu.HBM) for x in operands))
    return out.reshape(velocity.shape)


def fits(velocity, legendre):
    n_ma = lax.axis_size("ma")
    n_row = lax.axis_size("row")
    pairs, rows, half_lat = legendre.shape
    levels = velocity.shape[2]
    lat = half_lat // n_ma
    tiles = pairs == 4 and pairs * (rows - 1) == 256 and n_ma % 2 == 0 and n_ma <= 8 and n_row % 2 == 0
    whole = half_lat % n_ma == 0 and half_lat % 128 == 0 and lat % 16 == 0 and lat <= 64 and levels == 4
    return tiles and whole and n_row > 2 and n_ma > 1


def step(velocity, vorticity, legendre, pair_order, lat_weight, diffusivity):
    chosen = fused if fits(velocity, legendre) else local
    return chosen(velocity, vorticity, legendre, pair_order, lat_weight, diffusivity)


def solution(mesh):
    in_specs = (
        P(None, None, "row", "ma", None),
        P(None, None, "row", "ma", None),
        P("ma", None, None),
        P("ma"),
        P(),
        P(),
    )
    out_specs = P(None, None, "row", "ma", None)
    return jax.shard_map(step, mesh=mesh, in_specs=in_specs, out_specs=out_specs, check_vma=False)
```

```python
import functools
import math

import jax
import jax.numpy as jnp
import numpy as np
from jax import lax
from jax.experimental import pallas as pl
from jax.experimental.pallas import tpu as pltpu
from jax.sharding import PartitionSpec as P

NLON = 2048


STEP_SIZE = 1.0


def with_halo(cells, sides, width):
    for axis, dim in sides:
        count = lax.axis_size(axis)
        ends = count - 1
        head = lax.slice_in_dim(cells, 0, width, axis=dim)
        tail = lax.slice_in_dim(cells, cells.shape[dim] - width, cells.shape[dim], axis=dim)
        cells = jnp.concatenate(
            [
                lax.ppermute(tail, axis, [(i, (i + 1) % count) for i in range(ends)]),
                cells,
                lax.ppermute(head, axis, [((i + 1) % count, i) for i in range(ends)]),
            ],
            axis=dim,
        )
    return cells


def row_masks(low_order, pack_rows):
    orders_all = pack_rows - 1
    row_index = jnp.arange(pack_rows, dtype=jnp.int32)[None, :]
    low_column = low_order[:, None]
    is_lower = row_index < orders_all - low_column
    not_lower = jnp.logical_not(is_lower)
    even_low = row_index % 2 == 0
    even_high = (row_index + low_column) % 2 == 0
    low_pair = jnp.stack([is_lower & even_low, is_lower & jnp.logical_not(even_low)])
    high_pair = jnp.stack([not_lower & even_high, not_lower & jnp.logical_not(even_high)])
    return jnp.stack([low_pair, high_pair])


def cross_product(velocity_grid, vorticity_grid):
    return jnp.stack(
        [
            velocity_grid[1] * vorticity_grid[2] - velocity_grid[2] * vorticity_grid[1],
            velocity_grid[2] * vorticity_grid[0] - velocity_grid[0] * vorticity_grid[2],
            velocity_grid[0] * vorticity_grid[1] - velocity_grid[1] * vorticity_grid[0],
        ]
    )


def lon_table(column_order, is_imag, lon_start, lon_count):
    lon_index = lon_start + jnp.arange(lon_count, dtype=jnp.int32)
    angle_index = column_order[:, None] * lon_index[None, :] % NLON
    angle_value = angle_index.astype(jnp.float32) * (2.0 * math.pi / NLON)
    return jnp.where(is_imag[:, None], -jnp.sin(angle_value), jnp.cos(angle_value))


def local(velocity, vorticity, legendre, pair_order, lat_weight, diffusivity):
    pair_count = pair_order.shape[0]
    pack_rows = legendre.shape[1]
    half_lat = legendre.shape[2]
    nlat_all = 2 * half_lat
    levels_dev = velocity.shape[2]
    orders_all = pack_rows - 1
    inv_orders = 1.0 / math.sqrt(orders_all)
    inv_lon = 1.0 / math.sqrt(NLON)
    lon_width = NLON // 4
    mask_bool = row_masks(pair_order, pack_rows)
    fields = jnp.concatenate([velocity, vorticity], axis=0)
    masked = fields[None, None] * mask_bool.astype(jnp.bfloat16)[:, :, None, None, None]
    halves = jnp.einsum(
        "oqfilsr,srj->qfliosj", masked, legendre, preferred_element_type=jnp.float32
    )
    north_part = halves[0] + halves[1]
    south_part = halves[0] - halves[1]
    both_parts = jnp.concatenate([north_part, south_part], axis=-1)
    spectral = jnp.transpose(both_parts, (0, 1, 5, 2, 3, 4))
    spectral = spectral.reshape(6, levels_dev, nlat_all, 4 * pair_count).astype(jnp.bfloat16)
    gathered_ids = lax.all_gather(pair_order, "ma", axis=0, tiled=True)
    pair_slots = gathered_ids.reshape(-1, 1, 1, pair_count)
    both_orders = jnp.concatenate([pair_slots, orders_all - 1 - pair_slots], axis=2)
    full_shape = (both_orders.shape[0], 2, 2, pair_count)
    column_order = jnp.broadcast_to(both_orders, full_shape).reshape(-1)
    part_index = jnp.arange(2, dtype=jnp.int32)[None, :, None, None]
    is_imag = jnp.broadcast_to(part_index, full_shape).reshape(-1) == 1
    tables = [
        lon_table(column_order, is_imag, lon_block * lon_width, lon_width).astype(jnp.bfloat16)
        for lon_block in range(4)
    ]
    spec_block = lax.all_to_all(spectral, "ma", split_axis=2, concat_axis=3, tiled=True)
    accumulated = jnp.zeros((3,) + spec_block.shape[1:], jnp.float32)
    for lon_block in range(4):
        table_block = tables[lon_block]
        grid_values = (
            jnp.einsum("flac,cb->flab", spec_block, table_block, preferred_element_type=jnp.float32)
            * inv_orders
        )
        lamb_vector = cross_product(grid_values[:3], grid_values[3:])
        accumulated = accumulated + jnp.einsum(
            "flab,cb->flac",
            lamb_vector,
            table_block.astype(jnp.float32),
            precision=lax.Precision.HIGH,
            preferred_element_type=jnp.float32,
        )
    lamb_spec = (accumulated * inv_lon).astype(jnp.bfloat16)
    selector = jnp.transpose(mask_bool.astype(jnp.float32), (1, 0, 2, 3))[:, None, None, None]
    lamb_block = lax.all_to_all(lamb_spec, "ma", split_axis=3, concat_axis=2, tiled=True)
    item_count = lamb_block.shape[0]
    shaped = lamb_block.astype(jnp.float32).reshape(
        item_count, levels_dev, nlat_all, 2, 2, pair_count
    )
    shaped = jnp.transpose(shaped, (0, 1, 3, 4, 5, 2))
    north_side = shaped[..., :half_lat]
    south_side = shaped[..., half_lat:]
    weighted = jnp.stack(
        [lat_weight * (north_side + south_side), lat_weight * (north_side - south_side)]
    )
    weighted = weighted.astype(jnp.bfloat16)
    projected = jnp.einsum(
        "qfliosj,srj->qfliosr", weighted, legendre, preferred_element_type=jnp.float32
    )
    picked = jnp.sum(projected * selector, axis=(0, 4))
    tendency = jnp.transpose(picked, (0, 2, 1, 3, 4))
    source = velocity.astype(jnp.float32) + STEP_SIZE * tendency
    row_start = lax.axis_index("row") * levels_dev
    level_total = levels_dev * lax.axis_size("row")
    extended = with_halo(source.astype(jnp.bfloat16), (("row", 2),), 2).astype(source.dtype)
    padded_coupling = jnp.pad(diffusivity, (2, 2))
    wide_coupling = lax.dynamic_slice_in_dim(padded_coupling, row_start, levels_dev + 4)[
        None, None, :, None, None
    ]
    inner_coupling = wide_coupling[:, :, 1:-1]
    first_wide = (
        extended[:, :, 1:-1] + inner_coupling * (extended[:, :, :-2] + extended[:, :, 2:])
    ) / (1.0 + 2.0 * inner_coupling)
    global_level = row_start - 1 + jnp.arange(levels_dev + 2, dtype=jnp.int32)
    inside = ((global_level >= 0) & (global_level < level_total)).astype(jnp.float32)
    first_wide = first_wide * inside[None, None, :, None, None]
    own_coupling = wide_coupling[:, :, 2:-2]
    return (source + own_coupling * (first_wide[:, :, :-2] + first_wide[:, :, 2:])) / (
        1.0 + 2.0 * own_coupling
    )

def lon_count(orders_all):
    need = 3 * (orders_all - 1) + 1
    return min(NLON, -(-need // 64) * 64)


def remote(src, dst, send_sem, recv_sem, device_id):
    return pltpu.make_async_remote_copy(
        src_ref=src,
        dst_ref=dst,
        send_sem=send_sem,
        recv_sem=recv_sem,
        device_id=device_id,
        device_id_type=pl.DeviceIdType.MESH,
    )


def fused_kernel(
    n_ma, n_row, pairs, rows, levels, scale,
    velocity_hbm, vorticity_hbm, legendre_hbm, order_hbm, weight_hbm, dif_hbm, tab_hbm, tab_t_hbm,
    out_ref,
    velocity_ref, vorticity_ref, legendre_ref, order_ref, weight_ref, dif_ref, tab_ref, tab_t_ref, load_sem,
    leg_rows, leg_ref, rest_ref, coef_all, leg_all, rest_all, rest_t, end_op, end_spec, onehot, ops, spec, wgt, part, part_in, far_in, far_sum, near_out, near_in,
    coef_send, coef_recv, leg_send, leg_recv, swap_send, swap_recv, rest_send, rest_recv, part_send, part_recv, far_send, far_recv, near_send, near_recv, ready,
):
    me = lax.axis_index("ma")
    row = lax.axis_index("row")
    _, chunks, groups, wide = coef_all.shape
    coef_ref = coef_all.at[0]
    fields2 = groups // 2
    orders = rows - 1
    slots = 2 * pairs
    full = n_ma * slots
    lat = leg_ref.shape[2]
    side = wide // 2
    main = pairs * orders
    per_chunk = pairs // chunks
    f32 = jnp.float32
    bf16 = jnp.bfloat16
    n_z = n_ma // 2
    z, y = me // 2, lax.rem(me, 2)
    mate = me + 1 - 2 * y
    half = lax.rem(row, 2)
    mate_row = row + 1 - 2 * half

    def target(s):
        return lax.rem(z + s // 2, n_z) * 2 + lax.rem(y + lax.rem(s, 2), 2)

    def origin(s):
        return lax.rem(z + n_z - s // 2, n_z) * 2 + lax.rem(y + lax.rem(s, 2), 2)

    far_row = row + 2 * half - 1
    has_far = (far_row >= 0) & (far_row < n_row)

    barrier = pltpu.get_barrier_semaphore()
    for d in range(1, n_ma):
        pl.semaphore_signal(
            barrier, inc=1, device_id=(lax.rem(me + d, n_ma), row), device_id_type=pl.DeviceIdType.MESH
        )
    pl.semaphore_signal(barrier, inc=1, device_id=(me, mate_row), device_id_type=pl.DeviceIdType.MESH)

    @pl.when(has_far)
    def _():
        pl.semaphore_signal(barrier, inc=1, device_id=(me, far_row), device_id_type=pl.DeviceIdType.MESH)

    loads = [
        pltpu.make_async_copy(src, dst, load_sem.at[i])
        for i, (src, dst) in enumerate(
            [
                (legendre_hbm, legendre_ref),
                (velocity_hbm, velocity_ref),
                (vorticity_hbm, vorticity_ref),
                (order_hbm, order_ref),
                (weight_hbm, weight_ref),
                (dif_hbm, dif_ref),
                (tab_hbm, tab_ref),
                (tab_t_hbm, tab_t_ref),
            ]
        )
    ]
    for load in loads:
        load.start()
    for load in loads[:4]:
        load.wait()

    for r in range(rows):
        values = legendre_ref[r].astype(f32)
        for t in range(leg_rows.shape[0]):
            leg_rows[t, r * pairs : (r + 1) * pairs, :] = values[:, t * wide : (t + 1) * wide]
    packs = [
        jnp.concatenate([velocity_ref[...].astype(f32)[:, p], vorticity_ref[...].astype(f32)[:, p]], axis=0)
        for p in range(pairs)
    ]
    column = lax.broadcasted_iota(jnp.int32, (groups, wide), 1)
    ends = jnp.zeros((groups, wide), f32)
    for p in range(pairs):
        ends = jnp.where(column == p, packs[p][:, orders:], ends)
    ends = jnp.concatenate([ends, jnp.zeros((wide - groups, wide), f32)], axis=0)
    ends = jnp.transpose(ends)[0:pairs, 0:side]
    tails = jnp.concatenate([leg_rows[t, main : main + pairs, :] for t in range(leg_rows.shape[0])], axis=1)
    order_rows = [jnp.full((1, wide), order_ref[p].astype(f32)) for p in range(pairs)]
    filler = jnp.zeros((pairs, side - lat), f32)
    for b in range(n_ma):
        data_rows = jnp.concatenate([ends, tails[:, b * lat : (b + 1) * lat], filler], axis=1)
        rest_ref[b] = jnp.concatenate([data_rows] + order_rows, axis=0).astype(bf16)
    for c in range(chunks):
        members = range(c * per_chunk, (c + 1) * per_chunk)
        coef_all[0, c] = jnp.concatenate([packs[p][:, :orders] for p in members], axis=1).astype(bf16)
        turned = jnp.concatenate(
            [
                jnp.transpose(
                    jnp.concatenate([leg_rows[t, pl.ds(p, orders, stride=pairs), :] for p in members], axis=0)
                )
                for t in range(leg_rows.shape[0])
            ],
            axis=0,
        ).astype(bf16)
        for b in range(n_ma):
            leg_ref[b, c] = turned[b * lat : (b + 1) * lat]

    pl.semaphore_wait(barrier, n_ma + has_far.astype(jnp.int32))

    relayed = n_ma // 2

    def coef_copy(s):
        if s == relayed + 1:
            return remote(coef_all.at[relayed], coef_all.at[s], coef_send.at[s], coef_recv.at[s], (mate, row))
        return remote(coef_ref, coef_all.at[s], coef_send.at[s], coef_recv.at[s], (target(s), row))

    def leg_copy(s):
        peer = target(s)
        return remote(leg_ref.at[peer], leg_all.at[s], leg_send.at[s], leg_recv.at[s], (peer, row))

    def share_copy(s):
        return remote(leg_all.at[s], leg_all.at[s], swap_send.at[s], swap_recv.at[s], (me, mate_row))

    def rest_copy(s):
        peer = target(s)
        return remote(rest_ref.at[peer], rest_all.at[s], rest_send.at[s], rest_recv.at[s], (peer, row))

    far_first = sorted(range(1, n_ma), key=lambda s: (-min(s // 2, n_z - s // 2), -(s // 2), s % 2))
    direct = sorted((s for s in far_first if s // 2 * 2 != relayed), key=lambda s: (s < 2, -(s % 2), -s))
    for s in far_first:
        rest_copy(s).start()
    coef_copy(relayed).start()

    @pl.when(half == 1)
    def _():
        for s in far_first:
            leg_copy(s).start()

    for s in direct:
        coef_copy(s).start()

    @pl.when(has_far)
    def _():
        pl.semaphore_signal(ready, inc=1, device_id=(me, far_row), device_id_type=pl.DeviceIdType.MESH)

    leg_all[0] = leg_ref[me]
    rest_all[0] = rest_ref[me]

    def clear(d, carry):
        ops[d] = jnp.zeros(ops.shape[1:], bf16)
        return carry

    lax.fori_loop(0, n_ma, clear, 0)
    for load in loads[4:]:
        load.wait()
    weight = jnp.zeros((1, lat), f32)
    for b in range(n_ma):
        weight = jnp.where(me == b, weight_ref[...].reshape(1, -1)[:, b * lat : (b + 1) * lat], weight)
    weight = weight * scale
    gap = jnp.zeros((1, side - lat), f32)
    weight = jnp.concatenate([weight, gap, weight, gap] * 2, axis=1)

    lane = lax.broadcasted_iota(jnp.int32, (pairs, wide), 1)
    sub = lax.broadcasted_iota(jnp.int32, (pairs, wide), 0)
    m_lane = lax.broadcasted_iota(jnp.int32, (slots, orders), 1)
    m_sub = lax.broadcasted_iota(jnp.int32, (slots, orders), 0)
    lane_row = lane % orders
    own = lane // orders == sub % per_chunk

    def low_orders(d):
        return rest_all[d].astype(f32)[pairs:].astype(jnp.int32)

    def place(d):
        low = low_orders(d)
        order = jnp.zeros((slots, orders), jnp.int32)
        for p in range(pairs):
            value = low[p : p + 1, 0:1]
            order = jnp.where(m_sub == 2 * p, value, order)
            order = jnp.where(m_sub == 2 * p + 1, orders - 1 - value, order)
        onehot[d * slots : (d + 1) * slots, :] = (m_lane == order).astype(f32)

    def build(d):
        low = low_orders(d)
        lower = lane_row < orders - low
        north_low = (own & lower).astype(f32)
        north_high = (own & jnp.logical_not(lower)).astype(f32)
        south_low = north_low * (1 - 2 * (lane_row & 1)).astype(f32)
        south_high = north_high * (1 - 2 * ((lane_row + low) & 1)).astype(f32)
        for p in range(pairs):
            c = p // per_chunk
            table = leg_all[d, c].astype(f32)
            at = p * 2 * wide
            for i, factor in enumerate((north_low, south_low, north_high, south_high)):
                ops[d, at + i * side : at + i * side + lat, :] = (table * factor[p : p + 1]).astype(bf16)

    def synth(d):
        for p in range(pairs):
            at = p * 2 * wide
            made = lax.dot_general(
                coef_all[d, p // per_chunk],
                ops[d, at : at + 2 * wide, :],
                (((1,), (1,)), ((), ())),
                preferred_element_type=f32,
            )
            spec[pl.ds(d * slots + 2 * p, groups, stride=full), :] = made[:, :wide]
            spec[pl.ds(d * slots + 2 * p + 1, groups, stride=full), :] = made[:, wide:] + end_spec[d * pairs + p]

    for s in far_first:
        rest_copy(s).wait_recv()
    coef_copy(relayed).wait_recv()
    coef_copy(relayed + 1).start()

    def legs(ids):
        @pl.when(half == 1)
        def _():
            for s in ids:
                leg_copy(s).wait_recv()
                share_copy(s).start()

        @pl.when(half == 0)
        def _():
            for s in ids:
                share_copy(s).wait_recv()

    rest = rest_all[...].astype(f32).reshape(n_ma * 8, wide)
    rest_t[...] = jnp.transpose(jnp.concatenate([rest, jnp.zeros((wide - n_ma * 8, wide), f32)], axis=0))
    end_lane = lax.broadcasted_iota(jnp.int32, rest.shape, 1)
    end_sign = (1 - 2 * (pltpu.roll(rest, n_ma * 8 - pairs, 0).astype(jnp.int32) & 1)).astype(f32)
    north_end = jnp.where(end_lane < lat, pltpu.roll(rest, side, 1), 0.0)
    south_end = jnp.where((end_lane >= side) & (end_lane < side + lat), rest * end_sign, 0.0)
    end_op[...] = north_end + south_end
    for d in range(n_ma):
        place(d)
    hot = onehot[...].astype(bf16)
    to_grid = jnp.concatenate(
        [
            lax.dot_general(tab_t_ref[c], hot, (((1,), (1,)), ((), ())), preferred_element_type=f32)
            for c in range(2)
        ],
        axis=1,
    ).astype(bf16)
    to_spec = jnp.concatenate(
        [jnp.dot(hot, tab_ref[c], preferred_element_type=f32) for c in range(2)], axis=0
    ).astype(bf16)
    for d in range(n_ma):
        for p in range(pairs):
            i = 8 * d + p
            end_spec[d * pairs + p] = rest_t[0:groups, i : i + 1] * end_op[i : i + 1, :]
    held = [coef_ref[c, 0:fields2].astype(f32) for c in range(chunks)]
    held = jnp.concatenate(held + [rest_t[0:fields2, :]], axis=1)
    held = held.reshape(6, levels, held.shape[1])
    held = [held[:, k, :] for k in range(levels)]
    block = 6 * levels // 2
    lower = jnp.concatenate([held[k][:, c * wide : (c + 1) * wide] for c in range(chunks) for k in (0, 1)], axis=0)
    upper = jnp.concatenate([held[k][:, c * wide : (c + 1) * wide] for c in range(chunks) for k in (2, 3)], axis=0)
    own_end = jnp.concatenate([h[:, main:] for h in held] + [jnp.zeros((wide - fields2, wide), f32)], axis=0)
    own_end = jnp.where(lax.broadcasted_iota(jnp.int32, own_end.shape, 1) < pairs, own_end, 0.0)
    own_velocity = jnp.concatenate([lower, jnp.transpose(own_end)[0:8], upper], axis=0)
    build(0)
    synth(0)
    legs(far_first[:4])
    for s in far_first[:4]:
        build(s)
    synth(relayed)
    legs(far_first[4:])
    for s in far_first[4:]:
        build(s)
    for s in direct[:2]:
        coef_copy(s).wait_recv()
    for s in direct[:2]:
        synth(s)
    for s in direct[2:] + [relayed + 1]:
        coef_copy(s).wait_recv()
    for s in direct[2:] + [relayed + 1]:
        synth(s)

    def middle(j, carry):
        grids = []
        for f in range(6):
            blocks = []
            for i in range(2):
                k = 2 * j + i
                parts = [
                    spec[pl.ds(pl.multiple_of(((f * 2 + c) * levels + k) * full, full), full), :] for c in range(2)
                ]
                blocks.append(jnp.concatenate(parts, axis=0))
            block = jnp.concatenate(blocks, axis=1).astype(bf16)
            grids.append(jnp.dot(to_grid, block, preferred_element_type=f32))
        u, w = grids[:3], grids[3:]
        lamb = [
            u[1] * w[2] - u[2] * w[1],
            u[2] * w[0] - u[0] * w[2],
            u[0] * w[1] - u[1] * w[0],
        ]
        for f in range(3):
            made = jnp.dot(to_spec, lamb[f].astype(bf16), preferred_element_type=f32) * weight
            for i in range(2):
                k = 2 * j + i
                for c in range(2):
                    at = pl.multiple_of((k * 6 + f * 2 + c) * full, full)
                    wgt[pl.ds(at, full), :] = made[c * full : (c + 1) * full, i * wide : (i + 1) * wide]
        return carry

    lax.fori_loop(0, levels // 2, middle, 0)

    def part_copy(d):
        return remote(part.at[d], part_in.at[d], part_send.at[d], part_recv.at[d], (origin(d), row))

    def rows_of(slot):
        return wgt[pl.ds(slot, fields2, stride=full), :]

    def analyse(d):
        heads = []
        for c in range(chunks):
            picked = [rows_of(d * slots + i) for i in range(2 * c * per_chunk, 2 * (c + 1) * per_chunk)]
            lhs = jnp.concatenate(picked, axis=1).astype(bf16)
            first = c * per_chunk * 2 * wide
            heads.append(
                jnp.dot(lhs, ops[d, first : first + per_chunk * 2 * wide, :], preferred_element_type=f32)
            )
        lower = jnp.concatenate([h[:block] for h in heads], axis=0)
        upper = jnp.concatenate([h[block:] for h in heads], axis=0)
        return lower, upper

    highs = jnp.concatenate([rows_of(2 * i + 1).astype(bf16) for i in range(n_ma * pairs)], axis=0)
    ends = lax.dot_general(
        highs, end_op[...].astype(bf16), (((1,), (1,)), ((), ())), preferred_element_type=f32
    )
    end_column = lax.broadcasted_iota(jnp.int32, (fields2, n_ma * 8), 1)
    end_sum = jnp.zeros((fields2, n_ma * 8), f32)
    for i in range(n_ma * pairs):
        at = i // pairs * 8 + i % pairs
        end_sum = jnp.where(end_column == at, ends[i * fields2 : (i + 1) * fields2], end_sum)
    end_sum = jnp.concatenate([end_sum, jnp.zeros((fields2, wide - n_ma * 8), f32)], axis=1)
    end_sum = jnp.transpose(jnp.concatenate([end_sum, jnp.zeros((wide - fields2, wide), f32)], axis=0))
    body = chunks * block
    for d in range(n_ma):
        part[d, body : body + 8] = end_sum[8 * d : 8 * (d + 1)].astype(bf16)

    sent = pl.ds(pl.multiple_of(half * body, 8), body + 8)

    def far_copy(d):
        return remote(part.at[d, sent], far_in.at[d], far_send.at[d], far_recv.at[d], (origin(d), far_row))

    @pl.when(has_far)
    def _():
        pl.semaphore_wait(ready, 1)

    def project(i, carry):
        d = n_ma - i
        lower, upper = analyse(d)
        part[d, 0:body] = lower.astype(bf16)
        part[d, body + 8 :] = upper.astype(bf16)
        part_copy(d).start()

        @pl.when(has_far)
        def _():
            far_copy(d).start()

        return carry

    lax.fori_loop(1, n_ma, project, 0)
    lower, upper = analyse(0)
    source = jnp.concatenate([lower, end_sum[0:8], upper], axis=0) + own_velocity
    part[0] = source.astype(bf16)

    @pl.when(has_far)
    def _():
        far_copy(0).start()

    def gather(i, total):
        d = n_ma - i
        part_copy(d).wait_recv()
        return total + part_in[d].astype(f32)

    source = lax.fori_loop(1, n_ma, gather, source)

    def end_rows(values):
        turned = jnp.transpose(jnp.concatenate([values, jnp.zeros((wide - 8, wide), f32)], axis=0))[0:fields2]
        return jnp.where(lax.broadcasted_iota(jnp.int32, turned.shape, 1) < pairs, turned, 0.0)

    def level_pair(values, ends):
        made = []
        for k in range(2):
            heads = [values[c * block + 6 * k : c * block + 6 * (k + 1)] for c in range(chunks)]
            made.append(jnp.concatenate(heads + [ends[6 * k : 6 * (k + 1)]], axis=1))
        return made

    turned = end_rows(source[body : body + 8])
    own_levels = level_pair(source[0:body], turned[0:block]) + level_pair(source[body + 8 :], turned[block:fields2])
    for i in range(2):
        near_out[i] = jnp.where(half == 0, own_levels[levels - 2 + i], own_levels[i]).astype(bf16)
    near_copy = remote(near_out, near_in, near_send.at[0], near_recv.at[0], (me, mate_row))
    near_copy.start()

    @pl.when(has_far)
    def _():
        def collect(d, total):
            far_copy(d).wait_recv()
            return total + far_in[d].astype(f32)

        far_sum[...] = lax.fori_loop(0, n_ma, collect, jnp.zeros(far_sum.shape, f32))

    @pl.when(jnp.logical_not(has_far))
    def _():
        far_sum[...] = jnp.zeros(far_sum.shape, f32)

    far_body = far_sum[pl.ds(pl.multiple_of((1 - half) * 8, 8), body), :]
    turned = end_rows(far_sum[pl.ds(pl.multiple_of(half * body, 8), 8), :])
    far_levels = level_pair(far_body, jnp.where(half == 0, turned[block:fields2], turned[0:block]))

    for s in range(1, n_ma):
        coef_copy(s).wait_send()
        rest_copy(s).wait_send()
        part_copy(s).wait_send()

    @pl.when(half == 1)
    def _():
        for s in range(1, n_ma):
            leg_copy(s).wait_send()
            share_copy(s).wait_send()

    @pl.when(has_far)
    def _():
        for s in range(n_ma):
            far_copy(s).wait_send()

    near_copy.wait()

    shape = own_levels[0].shape
    has_left = (row > 0).astype(f32)
    has_right = (row < n_row - 1).astype(f32)
    near_levels = [near_in[i].astype(f32) for i in range(2)]
    before = [jnp.where(half == 0, a, b) for a, b in zip(far_levels, near_levels)]
    after = [jnp.where(half == 0, b, a) for a, b in zip(far_levels, near_levels)]
    wide_levels = before + own_levels + after
    coupling = [jnp.full(shape, dif_ref[lax.rem((row + n_row) * levels + i - 2, n_row * levels)]) for i in range(levels + 4)]
    inverse = [1.0 / (1.0 + 2.0 * c) for c in coupling]
    first = [
        (wide_levels[i] + coupling[i] * (wide_levels[i - 1] + wide_levels[i + 1])) * inverse[i]
        for i in range(1, levels + 3)
    ]
    first[0] = first[0] * has_left
    first[-1] = first[-1] * has_right
    for k in range(levels):
        done = (wide_levels[k + 2] + coupling[k + 2] * (first[k] + first[k + 2])) * inverse[k + 2]
        for p in range(pairs):
            line = jnp.concatenate(
                [done[:, p * orders : (p + 1) * orders], done[:, main + p : main + p + 1]], axis=1
            )
            for i in range(fields2 // levels):
                out_ref[i * levels + k, p : p + 1, :] = line[i : i + 1]


def fused(velocity, vorticity, legendre, pair_order, lat_weight, diffusivity):
    n_ma = lax.axis_size("ma")
    n_row = lax.axis_size("row")
    pairs, rows, half_lat = legendre.shape
    levels = velocity.shape[2]
    orders = rows - 1
    main = pairs * orders
    chunks = main // 128
    lanes = main + 128
    lat = half_lat // n_ma
    slots = 2 * pairs
    full = n_ma * slots
    points = lon_count(orders)
    bf16 = jnp.bfloat16
    f32 = jnp.float32
    groups = 12 * levels
    scale = (NLON / points) / math.sqrt(NLON) / orders
    angle = np.outer(np.arange(orders), np.arange(points)) % points * (2.0 * math.pi / points)
    table = np.stack([np.cos(angle), -np.sin(angle)])
    tab = jnp.asarray(table, bf16)
    tab_t = jnp.asarray(np.transpose(table, (0, 2, 1)), bf16)
    vmem = pl.BlockSpec(memory_space=pltpu.VMEM)
    away = pl.BlockSpec(memory_space=pltpu.HBM)
    operands = (
        velocity.reshape(6 * levels, pairs, rows),
        vorticity.reshape(6 * levels, pairs, rows),
        jnp.transpose(legendre, (1, 0, 2)),
        pair_order,
        lat_weight,
        diffusivity,
        tab,
        tab_t,
    )
    out = pl.pallas_call(
        functools.partial(fused_kernel, n_ma, n_row, pairs, rows, levels, scale),
        out_shape=jax.ShapeDtypeStruct((6 * levels, pairs, rows), f32),
        in_specs=[away] * 8,
        out_specs=vmem,
        scratch_shapes=[
            pltpu.VMEM((6 * levels, pairs, rows), bf16),
            pltpu.VMEM((6 * levels, pairs, rows), bf16),
            pltpu.VMEM((rows, pairs, half_lat), bf16),
            pltpu.SMEM((pairs,), jnp.int32),
            pltpu.VMEM((half_lat,), f32),
            pltpu.SMEM(diffusivity.shape, f32),
            pltpu.VMEM(tab.shape, bf16),
            pltpu.VMEM(tab_t.shape, bf16),
            pltpu.SemaphoreType.DMA((8,)),
            pltpu.VMEM((half_lat // 128, rows * pairs + 4, 128), f32),
            pltpu.VMEM((n_ma, chunks, lat, 128), bf16),
            pltpu.VMEM((n_ma, 8, 128), bf16),
            pltpu.VMEM((n_ma, chunks, groups, 128), bf16),
            pltpu.VMEM((n_ma, chunks, lat, 128), bf16),
            pltpu.VMEM((n_ma, 8, 128), bf16),
            pltpu.VMEM((128, 128), f32),
            pltpu.VMEM((n_ma * 8, 128), f32),
            pltpu.VMEM((n_ma * pairs, groups, 128), f32),
            pltpu.VMEM((full, orders), f32),
            pltpu.VMEM((n_ma, pairs * 256, 128), bf16),
            pltpu.VMEM((groups * full, 128), f32),
            pltpu.VMEM((groups // 2 * full, 128), f32),
            pltpu.VMEM((n_ma, chunks * groups // 2 + 8, 128), bf16),
            pltpu.VMEM((n_ma, chunks * groups // 2 + 8, 128), bf16),
            pltpu.VMEM((n_ma, chunks * groups // 4 + 8, 128), bf16),
            pltpu.VMEM((chunks * groups // 4 + 8, 128), f32),
            pltpu.VMEM((2, 6, lanes), bf16),
            pltpu.VMEM((2, 6, lanes), bf16),
        ]
        + [pltpu.SemaphoreType.DMA((n_ma,))] * 12
        + [pltpu.SemaphoreType.DMA((1,))] * 2
        + [pltpu.SemaphoreType.REGULAR],
        compiler_params=pltpu.CompilerParams(
            collective_id=0, has_side_effects=True, vmem_limit_bytes=48 * 1024 * 1024
        ),
    )(*(pltpu.with_memory_space_constraint(x, pltpu.HBM) for x in operands))
    return out.reshape(velocity.shape)


def fits(velocity, legendre):
    n_ma = lax.axis_size("ma")
    n_row = lax.axis_size("row")
    pairs, rows, half_lat = legendre.shape
    levels = velocity.shape[2]
    lat = half_lat // n_ma
    tiles = pairs == 4 and pairs * (rows - 1) == 256 and n_ma % 2 == 0 and n_ma <= 8 and n_row % 2 == 0
    whole = half_lat % n_ma == 0 and half_lat % 128 == 0 and lat % 16 == 0 and lat <= 64 and levels == 4
    return tiles and whole and n_row > 2 and n_ma > 1


def step(velocity, vorticity, legendre, pair_order, lat_weight, diffusivity):
    chosen = fused if fits(velocity, legendre) else local
    return chosen(velocity, vorticity, legendre, pair_order, lat_weight, diffusivity)


def solution(mesh):
    in_specs = (
        P(None, None, "row", "ma", None),
        P(None, None, "row", "ma", None),
        P("ma", None, None),
        P("ma"),
        P(),
        P(),
    )
    out_specs = P(None, None, "row", "ma", None)
    return jax.shard_map(step, mesh=mesh, in_specs=in_specs, out_specs=out_specs, check_vma=False)
```

```python
import functools
import math

import jax
import jax.numpy as jnp
import numpy as np
from jax import lax
from jax.experimental import pallas as pl
from jax.experimental.pallas import tpu as pltpu
from jax.sharding import PartitionSpec as P

NLON = 2048


STEP_SIZE = 1.0


def with_halo(cells, sides, width):
    for axis, dim in sides:
        count = lax.axis_size(axis)
        ends = count - 1
        head = lax.slice_in_dim(cells, 0, width, axis=dim)
        tail = lax.slice_in_dim(cells, cells.shape[dim] - width, cells.shape[dim], axis=dim)
        cells = jnp.concatenate(
            [
                lax.ppermute(tail, axis, [(i, (i + 1) % count) for i in range(ends)]),
                cells,
                lax.ppermute(head, axis, [((i + 1) % count, i) for i in range(ends)]),
            ],
            axis=dim,
        )
    return cells


def row_masks(low_order, pack_rows):
    orders_all = pack_rows - 1
    row_index = jnp.arange(pack_rows, dtype=jnp.int32)[None, :]
    low_column = low_order[:, None]
    is_lower = row_index < orders_all - low_column
    not_lower = jnp.logical_not(is_lower)
    even_low = row_index % 2 == 0
    even_high = (row_index + low_column) % 2 == 0
    low_pair = jnp.stack([is_lower & even_low, is_lower & jnp.logical_not(even_low)])
    high_pair = jnp.stack([not_lower & even_high, not_lower & jnp.logical_not(even_high)])
    return jnp.stack([low_pair, high_pair])


def cross_product(velocity_grid, vorticity_grid):
    return jnp.stack(
        [
            velocity_grid[1] * vorticity_grid[2] - velocity_grid[2] * vorticity_grid[1],
            velocity_grid[2] * vorticity_grid[0] - velocity_grid[0] * vorticity_grid[2],
            velocity_grid[0] * vorticity_grid[1] - velocity_grid[1] * vorticity_grid[0],
        ]
    )


def lon_table(column_order, is_imag, lon_start, lon_count):
    lon_index = lon_start + jnp.arange(lon_count, dtype=jnp.int32)
    angle_index = column_order[:, None] * lon_index[None, :] % NLON
    angle_value = angle_index.astype(jnp.float32) * (2.0 * math.pi / NLON)
    return jnp.where(is_imag[:, None], -jnp.sin(angle_value), jnp.cos(angle_value))


def local(velocity, vorticity, legendre, pair_order, lat_weight, diffusivity):
    pair_count = pair_order.shape[0]
    pack_rows = legendre.shape[1]
    half_lat = legendre.shape[2]
    nlat_all = 2 * half_lat
    levels_dev = velocity.shape[2]
    orders_all = pack_rows - 1
    inv_orders = 1.0 / math.sqrt(orders_all)
    inv_lon = 1.0 / math.sqrt(NLON)
    lon_width = NLON // 4
    mask_bool = row_masks(pair_order, pack_rows)
    fields = jnp.concatenate([velocity, vorticity], axis=0)
    masked = fields[None, None] * mask_bool.astype(jnp.bfloat16)[:, :, None, None, None]
    halves = jnp.einsum(
        "oqfilsr,srj->qfliosj", masked, legendre, preferred_element_type=jnp.float32
    )
    north_part = halves[0] + halves[1]
    south_part = halves[0] - halves[1]
    both_parts = jnp.concatenate([north_part, south_part], axis=-1)
    spectral = jnp.transpose(both_parts, (0, 1, 5, 2, 3, 4))
    spectral = spectral.reshape(6, levels_dev, nlat_all, 4 * pair_count).astype(jnp.bfloat16)
    gathered_ids = lax.all_gather(pair_order, "ma", axis=0, tiled=True)
    pair_slots = gathered_ids.reshape(-1, 1, 1, pair_count)
    both_orders = jnp.concatenate([pair_slots, orders_all - 1 - pair_slots], axis=2)
    full_shape = (both_orders.shape[0], 2, 2, pair_count)
    column_order = jnp.broadcast_to(both_orders, full_shape).reshape(-1)
    part_index = jnp.arange(2, dtype=jnp.int32)[None, :, None, None]
    is_imag = jnp.broadcast_to(part_index, full_shape).reshape(-1) == 1
    tables = [
        lon_table(column_order, is_imag, lon_block * lon_width, lon_width).astype(jnp.bfloat16)
        for lon_block in range(4)
    ]
    spec_block = lax.all_to_all(spectral, "ma", split_axis=2, concat_axis=3, tiled=True)
    accumulated = jnp.zeros((3,) + spec_block.shape[1:], jnp.float32)
    for lon_block in range(4):
        table_block = tables[lon_block]
        grid_values = (
            jnp.einsum("flac,cb->flab", spec_block, table_block, preferred_element_type=jnp.float32)
            * inv_orders
        )
        lamb_vector = cross_product(grid_values[:3], grid_values[3:])
        accumulated = accumulated + jnp.einsum(
            "flab,cb->flac",
            lamb_vector,
            table_block.astype(jnp.float32),
            precision=lax.Precision.HIGH,
            preferred_element_type=jnp.float32,
        )
    lamb_spec = (accumulated * inv_lon).astype(jnp.bfloat16)
    selector = jnp.transpose(mask_bool.astype(jnp.float32), (1, 0, 2, 3))[:, None, None, None]
    lamb_block = lax.all_to_all(lamb_spec, "ma", split_axis=3, concat_axis=2, tiled=True)
    item_count = lamb_block.shape[0]
    shaped = lamb_block.astype(jnp.float32).reshape(
        item_count, levels_dev, nlat_all, 2, 2, pair_count
    )
    shaped = jnp.transpose(shaped, (0, 1, 3, 4, 5, 2))
    north_side = shaped[..., :half_lat]
    south_side = shaped[..., half_lat:]
    weighted = jnp.stack(
        [lat_weight * (north_side + south_side), lat_weight * (north_side - south_side)]
    )
    weighted = weighted.astype(jnp.bfloat16)
    projected = jnp.einsum(
        "qfliosj,srj->qfliosr", weighted, legendre, preferred_element_type=jnp.float32
    )
    picked = jnp.sum(projected * selector, axis=(0, 4))
    tendency = jnp.transpose(picked, (0, 2, 1, 3, 4))
    source = velocity.astype(jnp.float32) + STEP_SIZE * tendency
    row_start = lax.axis_index("row") * levels_dev
    level_total = levels_dev * lax.axis_size("row")
    extended = with_halo(source.astype(jnp.bfloat16), (("row", 2),), 2).astype(source.dtype)
    padded_coupling = jnp.pad(diffusivity, (2, 2))
    wide_coupling = lax.dynamic_slice_in_dim(padded_coupling, row_start, levels_dev + 4)[
        None, None, :, None, None
    ]
    inner_coupling = wide_coupling[:, :, 1:-1]
    first_wide = (
        extended[:, :, 1:-1] + inner_coupling * (extended[:, :, :-2] + extended[:, :, 2:])
    ) / (1.0 + 2.0 * inner_coupling)
    global_level = row_start - 1 + jnp.arange(levels_dev + 2, dtype=jnp.int32)
    inside = ((global_level >= 0) & (global_level < level_total)).astype(jnp.float32)
    first_wide = first_wide * inside[None, None, :, None, None]
    own_coupling = wide_coupling[:, :, 2:-2]
    return (source + own_coupling * (first_wide[:, :, :-2] + first_wide[:, :, 2:])) / (
        1.0 + 2.0 * own_coupling
    )

def lon_count(orders_all):
    need = 3 * (orders_all - 1) + 1
    return min(NLON, -(-need // 64) * 64)


def remote(src, dst, send_sem, recv_sem, device_id):
    return pltpu.make_async_remote_copy(
        src_ref=src,
        dst_ref=dst,
        send_sem=send_sem,
        recv_sem=recv_sem,
        device_id=device_id,
        device_id_type=pl.DeviceIdType.MESH,
    )


def fused_kernel(
    n_ma, n_row, pairs, rows, levels, scale,
    velocity_hbm, vorticity_hbm, legendre_hbm, order_hbm, weight_hbm, dif_hbm, tab_hbm, tab_t_hbm,
    out_ref,
    velocity_ref, vorticity_ref, legendre_ref, order_ref, weight_ref, dif_ref, tab_ref, tab_t_ref, load_sem,
    leg_rows, leg_ref, rest_ref, coef_all, leg_all, rest_all, rest_t, end_op, end_spec, onehot, ops, spec, wgt, part, part_in, far_in, far_sum, near_out, near_in,
    coef_send, coef_recv, leg_send, leg_recv, swap_send, swap_recv, rest_send, rest_recv, part_send, part_recv, far_send, far_recv, near_send, near_recv, ready,
):
    me = lax.axis_index("ma")
    row = lax.axis_index("row")
    _, chunks, groups, wide = coef_all.shape
    coef_ref = coef_all.at[0]
    fields2 = groups // 2
    orders = rows - 1
    slots = 2 * pairs
    full = n_ma * slots
    lat = leg_ref.shape[2]
    side = wide // 2
    main = pairs * orders
    per_chunk = pairs // chunks
    f32 = jnp.float32
    bf16 = jnp.bfloat16
    n_z = n_ma // 2
    z, y = me // 2, lax.rem(me, 2)
    mate = me + 1 - 2 * y
    half = lax.rem(row, 2)
    mate_row = row + 1 - 2 * half

    def target(s):
        return lax.rem(z + s // 2, n_z) * 2 + lax.rem(y + lax.rem(s, 2), 2)

    def origin(s):
        return lax.rem(z + n_z - s // 2, n_z) * 2 + lax.rem(y + lax.rem(s, 2), 2)

    far_row = row + 2 * half - 1
    has_far = (far_row >= 0) & (far_row < n_row)

    barrier = pltpu.get_barrier_semaphore()
    for d in range(1, n_ma):
        pl.semaphore_signal(
            barrier, inc=1, device_id=(lax.rem(me + d, n_ma), row), device_id_type=pl.DeviceIdType.MESH
        )
    pl.semaphore_signal(barrier, inc=1, device_id=(me, mate_row), device_id_type=pl.DeviceIdType.MESH)

    @pl.when(has_far)
    def _():
        pl.semaphore_signal(barrier, inc=1, device_id=(me, far_row), device_id_type=pl.DeviceIdType.MESH)

    loads = [
        pltpu.make_async_copy(src, dst, load_sem.at[i])
        for i, (src, dst) in enumerate(
            [
                (legendre_hbm, legendre_ref),
                (velocity_hbm, velocity_ref),
                (vorticity_hbm, vorticity_ref),
                (order_hbm, order_ref),
                (weight_hbm, weight_ref),
                (dif_hbm, dif_ref),
                (tab_hbm, tab_ref),
                (tab_t_hbm, tab_t_ref),
            ]
        )
    ]
    for load in loads:
        load.start()
    for load in loads[:4]:
        load.wait()

    for r in range(rows):
        values = legendre_ref[r].astype(f32)
        for t in range(leg_rows.shape[0]):
            leg_rows[t, r * pairs : (r + 1) * pairs, :] = values[:, t * wide : (t + 1) * wide]
    packs = [
        jnp.concatenate([velocity_ref[...].astype(f32)[:, p], vorticity_ref[...].astype(f32)[:, p]], axis=0)
        for p in range(pairs)
    ]
    column = lax.broadcasted_iota(jnp.int32, (groups, wide), 1)
    ends = jnp.zeros((groups, wide), f32)
    for p in range(pairs):
        ends = jnp.where(column == p, packs[p][:, orders:], ends)
    ends = jnp.concatenate([ends, jnp.zeros((wide - groups, wide), f32)], axis=0)
    ends = jnp.transpose(ends)[0:pairs, 0:side]
    tails = jnp.concatenate([leg_rows[t, main : main + pairs, :] for t in range(leg_rows.shape[0])], axis=1)
    order_rows = [jnp.full((1, wide), order_ref[p].astype(f32)) for p in range(pairs)]
    filler = jnp.zeros((pairs, side - lat), f32)
    for b in range(n_ma):
        data_rows = jnp.concatenate([ends, tails[:, b * lat : (b + 1) * lat], filler], axis=1)
        rest_ref[b] = jnp.concatenate([data_rows] + order_rows, axis=0).astype(bf16)
    for c in range(chunks):
        members = range(c * per_chunk, (c + 1) * per_chunk)
        coef_all[0, c] = jnp.concatenate([packs[p][:, :orders] for p in members], axis=1).astype(bf16)
        turned = jnp.concatenate(
            [
                jnp.transpose(
                    jnp.concatenate([leg_rows[t, pl.ds(p, orders, stride=pairs), :] for p in members], axis=0)
                )
                for t in range(leg_rows.shape[0])
            ],
            axis=0,
        ).astype(bf16)
        for b in range(n_ma):
            leg_ref[b, c] = turned[b * lat : (b + 1) * lat]

    pl.semaphore_wait(barrier, n_ma + has_far.astype(jnp.int32))

    passed = [s for s in (4,) if s < n_ma]
    gained = [s + 1 for s in passed]
    far_first = sorted(range(1, n_ma), key=lambda s: (-min(s // 2, n_z - s // 2), -(s // 2), s % 2))
    direct = [s for s in (7, 3, 6, 2, 1) if s < n_ma]
    coef_groups = [[s] for s in passed] + [direct[:2], direct[2:], gained]
    leg_groups = [far_first[: n_ma // 2], far_first[n_ma // 2 :]]

    def wait_blocks(ref, count, sem):
        blocks = ref.at[pl.ds(0, count)]
        pltpu.make_async_copy(blocks, blocks, sem).wait()

    def coef_copy(s):
        group = [s in g for g in coef_groups].index(True)
        if s in gained:
            return remote(coef_all.at[s - 1], coef_all.at[s], coef_send.at[0], coef_recv.at[group], (mate, row))
        return remote(coef_ref, coef_all.at[s], coef_send.at[0], coef_recv.at[group], (target(s), row))

    def leg_copy(s):
        peer = target(s)
        return remote(leg_ref.at[peer], leg_all.at[s], leg_send.at[0], leg_recv.at[s - 1], (peer, row))

    def share_copy(s):
        group = [s in g for g in leg_groups].index(True)
        return remote(leg_all.at[s], leg_all.at[s], swap_send.at[0], swap_recv.at[group], (me, mate_row))

    def rest_copy(s):
        peer = target(s)
        return remote(rest_ref.at[peer], rest_all.at[s], rest_send.at[0], rest_recv.at[0], (peer, row))

    for s in far_first:
        rest_copy(s).start()
    for s in passed:
        coef_copy(s).start()

    @pl.when(half == 1)
    def _():
        for s in far_first:
            leg_copy(s).start()

    for s in direct:
        coef_copy(s).start()

    @pl.when(has_far)
    def _():
        pl.semaphore_signal(ready, inc=1, device_id=(me, far_row), device_id_type=pl.DeviceIdType.MESH)

    leg_all[0] = leg_ref[me]
    rest_all[0] = rest_ref[me]

    def clear(d, carry):
        ops[d] = jnp.zeros(ops.shape[1:], bf16)
        return carry

    lax.fori_loop(0, n_ma, clear, 0)
    for load in loads[4:]:
        load.wait()
    weight = jnp.zeros((1, lat), f32)
    for b in range(n_ma):
        weight = jnp.where(me == b, weight_ref[...].reshape(1, -1)[:, b * lat : (b + 1) * lat], weight)
    weight = weight * scale
    gap = jnp.zeros((1, side - lat), f32)
    weight = jnp.concatenate([weight, gap, weight, gap] * 2, axis=1)

    lane = lax.broadcasted_iota(jnp.int32, (pairs, wide), 1)
    sub = lax.broadcasted_iota(jnp.int32, (pairs, wide), 0)
    m_lane = lax.broadcasted_iota(jnp.int32, (slots, orders), 1)
    m_sub = lax.broadcasted_iota(jnp.int32, (slots, orders), 0)
    lane_row = lane % orders
    own = lane // orders == sub % per_chunk

    def low_orders(d):
        return rest_all[d].astype(f32)[pairs:].astype(jnp.int32)

    def place(d):
        low = low_orders(d)
        order = jnp.zeros((slots, orders), jnp.int32)
        for p in range(pairs):
            value = low[p : p + 1, 0:1]
            order = jnp.where(m_sub == 2 * p, value, order)
            order = jnp.where(m_sub == 2 * p + 1, orders - 1 - value, order)
        onehot[d * slots : (d + 1) * slots, :] = (m_lane == order).astype(f32)

    def build(d):
        low = low_orders(d)
        lower = lane_row < orders - low
        north_low = (own & lower).astype(f32)
        north_high = (own & jnp.logical_not(lower)).astype(f32)
        south_low = north_low * (1 - 2 * (lane_row & 1)).astype(f32)
        south_high = north_high * (1 - 2 * ((lane_row + low) & 1)).astype(f32)
        for p in range(pairs):
            c = p // per_chunk
            table = leg_all[d, c].astype(f32)
            at = p * 2 * wide
            for i, factor in enumerate((north_low, south_low, north_high, south_high)):
                ops[d, at + i * side : at + i * side + lat, :] = (table * factor[p : p + 1]).astype(bf16)

    def synth(d):
        for p in range(pairs):
            at = p * 2 * wide
            made = lax.dot_general(
                coef_all[d, p // per_chunk],
                ops[d, at : at + 2 * wide, :],
                (((1,), (1,)), ((), ())),
                preferred_element_type=f32,
            )
            spec[pl.ds(d * slots + 2 * p, groups, stride=full), :] = made[:, :wide]
            spec[pl.ds(d * slots + 2 * p + 1, groups, stride=full), :] = made[:, wide:] + end_spec[d * pairs + p]

    for i, s in enumerate(passed):
        wait_blocks(coef_all, 1, coef_recv.at[i])
        coef_copy(s + 1).start()
    wait_blocks(rest_all, n_ma - 1, rest_recv.at[0])

    def legs(group):
        @pl.when(half == 1)
        def _():
            for s in leg_groups[group]:
                leg_copy(s).wait_recv()
                share_copy(s).start()

        @pl.when(half == 0)
        def _():
            wait_blocks(leg_all, len(leg_groups[group]), swap_recv.at[group])

    rest = rest_all[...].astype(f32).reshape(n_ma * 8, wide)
    rest_t[...] = jnp.transpose(jnp.concatenate([rest, jnp.zeros((wide - n_ma * 8, wide), f32)], axis=0))
    end_lane = lax.broadcasted_iota(jnp.int32, rest.shape, 1)
    end_sign = (1 - 2 * (pltpu.roll(rest, n_ma * 8 - pairs, 0).astype(jnp.int32) & 1)).astype(f32)
    north_end = jnp.where(end_lane < lat, pltpu.roll(rest, side, 1), 0.0)
    south_end = jnp.where((end_lane >= side) & (end_lane < side + lat), rest * end_sign, 0.0)
    end_op[...] = north_end + south_end
    for d in range(n_ma):
        place(d)
    hot = onehot[...].astype(bf16)
    to_grid = jnp.concatenate(
        [
            lax.dot_general(tab_t_ref[c], hot, (((1,), (1,)), ((), ())), preferred_element_type=f32)
            for c in range(2)
        ],
        axis=1,
    ).astype(bf16)
    to_spec = jnp.concatenate(
        [jnp.dot(hot, tab_ref[c], preferred_element_type=f32) for c in range(2)], axis=0
    ).astype(bf16)
    for d in range(n_ma):
        for p in range(pairs):
            i = 8 * d + p
            end_spec[d * pairs + p] = rest_t[0:groups, i : i + 1] * end_op[i : i + 1, :]
    held = [coef_ref[c, 0:fields2].astype(f32) for c in range(chunks)]
    held = jnp.concatenate(held + [rest_t[0:fields2, :]], axis=1)
    held = held.reshape(6, levels, held.shape[1])
    held = [held[:, k, :] for k in range(levels)]
    block = 6 * levels // 2
    lower = jnp.concatenate([held[k][:, c * wide : (c + 1) * wide] for c in range(chunks) for k in (0, 1)], axis=0)
    upper = jnp.concatenate([held[k][:, c * wide : (c + 1) * wide] for c in range(chunks) for k in (2, 3)], axis=0)
    own_end = jnp.concatenate([h[:, main:] for h in held] + [jnp.zeros((wide - fields2, wide), f32)], axis=0)
    own_end = jnp.where(lax.broadcasted_iota(jnp.int32, own_end.shape, 1) < pairs, own_end, 0.0)
    own_velocity = jnp.concatenate([lower, jnp.transpose(own_end)[0:8], upper], axis=0)
    build(0)
    synth(0)
    legs(0)
    for s in leg_groups[0]:
        build(s)
    for s in passed:
        synth(s)
    legs(1)
    for s in leg_groups[1]:
        build(s)
    for group in range(len(passed), len(coef_groups)):
        wait_blocks(coef_all, len(coef_groups[group]), coef_recv.at[group])
        for s in coef_groups[group]:
            synth(s)

    def middle(j, carry):
        grids = []
        for f in range(6):
            blocks = []
            for i in range(2):
                k = 2 * j + i
                parts = [
                    spec[pl.ds(pl.multiple_of(((f * 2 + c) * levels + k) * full, full), full), :] for c in range(2)
                ]
                blocks.append(jnp.concatenate(parts, axis=0))
            block = jnp.concatenate(blocks, axis=1).astype(bf16)
            grids.append(jnp.dot(to_grid, block, preferred_element_type=f32))
        u, w = grids[:3], grids[3:]
        lamb = [
            u[1] * w[2] - u[2] * w[1],
            u[2] * w[0] - u[0] * w[2],
            u[0] * w[1] - u[1] * w[0],
        ]
        for f in range(3):
            made = jnp.dot(to_spec, lamb[f].astype(bf16), preferred_element_type=f32) * weight
            for i in range(2):
                k = 2 * j + i
                for c in range(2):
                    at = pl.multiple_of((k * 6 + f * 2 + c) * full, full)
                    wgt[pl.ds(at, full), :] = made[c * full : (c + 1) * full, i * wide : (i + 1) * wide]
        return carry

    lax.fori_loop(0, levels // 2, middle, 0)

    def part_copy(d):
        return remote(part.at[d], part_in.at[d], part_send.at[0], part_recv.at[0], (origin(d), row))

    def rows_of(slot):
        return wgt[pl.ds(slot, fields2, stride=full), :]

    def analyse(d):
        heads = []
        for c in range(chunks):
            picked = [rows_of(d * slots + i) for i in range(2 * c * per_chunk, 2 * (c + 1) * per_chunk)]
            lhs = jnp.concatenate(picked, axis=1).astype(bf16)
            first = c * per_chunk * 2 * wide
            heads.append(
                jnp.dot(lhs, ops[d, first : first + per_chunk * 2 * wide, :], preferred_element_type=f32)
            )
        lower = jnp.concatenate([h[:block] for h in heads], axis=0)
        upper = jnp.concatenate([h[block:] for h in heads], axis=0)
        return lower, upper

    highs = jnp.concatenate([rows_of(2 * i + 1) for i in range(n_ma * pairs)], axis=0).astype(bf16)
    ends = lax.dot_general(
        highs, end_op[...].astype(bf16), (((1,), (1,)), ((), ())), preferred_element_type=f32
    )
    end_column = lax.broadcasted_iota(jnp.int32, (fields2, n_ma * 8), 1)
    end_sum = jnp.zeros((fields2, n_ma * 8), f32)
    for i in range(n_ma * pairs):
        at = i // pairs * 8 + i % pairs
        end_sum = jnp.where(end_column == at, ends[i * fields2 : (i + 1) * fields2], end_sum)
    end_sum = jnp.concatenate([end_sum, jnp.zeros((fields2, wide - n_ma * 8), f32)], axis=1)
    end_sum = jnp.transpose(jnp.concatenate([end_sum, jnp.zeros((wide - fields2, wide), f32)], axis=0))
    body = chunks * block
    for d in range(n_ma):
        part[d, body : body + 8] = end_sum[8 * d : 8 * (d + 1)].astype(bf16)

    sent = pl.ds(pl.multiple_of(half * body, 8), body + 8)

    def far_copy(d):
        return remote(part.at[d, sent], far_in.at[d], far_send.at[0], far_recv.at[0], (origin(d), far_row))

    @pl.when(has_far)
    def _():
        pl.semaphore_wait(ready, 1)

    upper_z = z // (n_z // 2)

    def project(i, carry):
        d = upper_z * (n_ma - i) + (1 - upper_z) * (1 + lax.rem(i, n_ma - 1))
        lower, upper = analyse(d)
        part[d, 0:body] = lower.astype(bf16)
        part[d, body + 8 :] = upper.astype(bf16)
        part_copy(d).start()

        @pl.when(has_far)
        def _():
            far_copy(d).start()

        return carry

    lax.fori_loop(1, n_ma, project, 0)
    lower, upper = analyse(0)
    source = jnp.concatenate([lower, end_sum[0:8], upper], axis=0) + own_velocity
    part[0] = source.astype(bf16)

    @pl.when(has_far)
    def _():
        far_copy(0).start()

    wait_blocks(part_in, n_ma - 1, part_recv.at[0])
    for d in range(1, n_ma):
        source = source + part_in[d].astype(f32)

    def end_rows(values):
        turned = jnp.transpose(jnp.concatenate([values, jnp.zeros((wide - 8, wide), f32)], axis=0))[0:fields2]
        return jnp.where(lax.broadcasted_iota(jnp.int32, turned.shape, 1) < pairs, turned, 0.0)

    def level_pair(values, ends):
        made = []
        for k in range(2):
            heads = [values[c * block + 6 * k : c * block + 6 * (k + 1)] for c in range(chunks)]
            made.append(jnp.concatenate(heads + [ends[6 * k : 6 * (k + 1)]], axis=1))
        return made

    turned = end_rows(source[body : body + 8])
    own_levels = level_pair(source[0:body], turned[0:block]) + level_pair(source[body + 8 :], turned[block:fields2])
    for i in range(2):
        near_out[i] = jnp.where(half == 0, own_levels[levels - 2 + i], own_levels[i]).astype(bf16)
    near_copy = remote(near_out, near_in, near_send.at[0], near_recv.at[0], (me, mate_row))
    near_copy.start()

    @pl.when(has_far)
    def _():
        wait_blocks(far_in, n_ma, far_recv.at[0])
        total = far_in[0].astype(f32)
        for d in range(1, n_ma):
            total = total + far_in[d].astype(f32)
        far_sum[...] = total

    @pl.when(jnp.logical_not(has_far))
    def _():
        far_sum[...] = jnp.zeros(far_sum.shape, f32)

    far_body = far_sum[pl.ds(pl.multiple_of((1 - half) * 8, 8), body), :]
    turned = end_rows(far_sum[pl.ds(pl.multiple_of(half * body, 8), 8), :])
    far_levels = level_pair(far_body, jnp.where(half == 0, turned[block:fields2], turned[0:block]))

    wait_blocks(coef_all, n_ma - 1, coef_send.at[0])
    wait_blocks(rest_all, n_ma - 1, rest_send.at[0])
    wait_blocks(part_in, n_ma - 1, part_send.at[0])

    @pl.when(half == 1)
    def _():
        wait_blocks(leg_all, n_ma - 1, leg_send.at[0])
        wait_blocks(leg_all, n_ma - 1, swap_send.at[0])

    @pl.when(has_far)
    def _():
        wait_blocks(far_in, n_ma, far_send.at[0])

    near_copy.wait()

    shape = own_levels[0].shape
    has_left = (row > 0).astype(f32)
    has_right = (row < n_row - 1).astype(f32)
    near_levels = [near_in[i].astype(f32) for i in range(2)]
    before = [jnp.where(half == 0, a, b) for a, b in zip(far_levels, near_levels)]
    after = [jnp.where(half == 0, b, a) for a, b in zip(far_levels, near_levels)]
    wide_levels = before + own_levels + after
    coupling = [jnp.full(shape, dif_ref[lax.rem((row + n_row) * levels + i - 2, n_row * levels)]) for i in range(levels + 4)]
    inverse = [1.0 / (1.0 + 2.0 * c) for c in coupling]
    first = [
        (wide_levels[i] + coupling[i] * (wide_levels[i - 1] + wide_levels[i + 1])) * inverse[i]
        for i in range(1, levels + 3)
    ]
    first[0] = first[0] * has_left
    first[-1] = first[-1] * has_right
    for k in range(levels):
        done = (wide_levels[k + 2] + coupling[k + 2] * (first[k] + first[k + 2])) * inverse[k + 2]
        for p in range(pairs):
            line = jnp.concatenate(
                [done[:, p * orders : (p + 1) * orders], done[:, main + p : main + p + 1]], axis=1
            )
            for i in range(fields2 // levels):
                out_ref[i * levels + k, p : p + 1, :] = line[i : i + 1]


def fused(velocity, vorticity, legendre, pair_order, lat_weight, diffusivity):
    n_ma = lax.axis_size("ma")
    n_row = lax.axis_size("row")
    pairs, rows, half_lat = legendre.shape
    levels = velocity.shape[2]
    orders = rows - 1
    main = pairs * orders
    chunks = main // 128
    lanes = main + 128
    lat = half_lat // n_ma
    slots = 2 * pairs
    full = n_ma * slots
    points = lon_count(orders)
    bf16 = jnp.bfloat16
    f32 = jnp.float32
    groups = 12 * levels
    scale = (NLON / points) / math.sqrt(NLON) / orders
    angle = np.outer(np.arange(orders), np.arange(points)) % points * (2.0 * math.pi / points)
    table = np.stack([np.cos(angle), -np.sin(angle)])
    tab = jnp.asarray(table, bf16)
    tab_t = jnp.asarray(np.transpose(table, (0, 2, 1)), bf16)
    vmem = pl.BlockSpec(memory_space=pltpu.VMEM)
    away = pl.BlockSpec(memory_space=pltpu.HBM)
    operands = (
        velocity.reshape(6 * levels, pairs, rows),
        vorticity.reshape(6 * levels, pairs, rows),
        jnp.transpose(legendre, (1, 0, 2)),
        pair_order,
        lat_weight,
        diffusivity,
        tab,
        tab_t,
    )
    out = pl.pallas_call(
        functools.partial(fused_kernel, n_ma, n_row, pairs, rows, levels, scale),
        out_shape=jax.ShapeDtypeStruct((6 * levels, pairs, rows), f32),
        in_specs=[away] * 8,
        out_specs=vmem,
        scratch_shapes=[
            pltpu.VMEM((6 * levels, pairs, rows), bf16),
            pltpu.VMEM((6 * levels, pairs, rows), bf16),
            pltpu.VMEM((rows, pairs, half_lat), bf16),
            pltpu.SMEM((pairs,), jnp.int32),
            pltpu.VMEM((half_lat,), f32),
            pltpu.SMEM(diffusivity.shape, f32),
            pltpu.VMEM(tab.shape, bf16),
            pltpu.VMEM(tab_t.shape, bf16),
            pltpu.SemaphoreType.DMA((8,)),
            pltpu.VMEM((half_lat // 128, rows * pairs + 4, 128), f32),
            pltpu.VMEM((n_ma, chunks, lat, 128), bf16),
            pltpu.VMEM((n_ma, 8, 128), bf16),
            pltpu.VMEM((n_ma, chunks, groups, 128), bf16),
            pltpu.VMEM((n_ma, chunks, lat, 128), bf16),
            pltpu.VMEM((n_ma, 8, 128), bf16),
            pltpu.VMEM((128, 128), f32),
            pltpu.VMEM((n_ma * 8, 128), f32),
            pltpu.VMEM((n_ma * pairs, groups, 128), f32),
            pltpu.VMEM((full, orders), f32),
            pltpu.VMEM((n_ma, pairs * 256, 128), bf16),
            pltpu.VMEM((groups * full, 128), f32),
            pltpu.VMEM((groups // 2 * full, 128), f32),
            pltpu.VMEM((n_ma, chunks * groups // 2 + 8, 128), bf16),
            pltpu.VMEM((n_ma, chunks * groups // 2 + 8, 128), bf16),
            pltpu.VMEM((n_ma, chunks * groups // 4 + 8, 128), bf16),
            pltpu.VMEM((chunks * groups // 4 + 8, 128), f32),
            pltpu.VMEM((2, 6, lanes), bf16),
            pltpu.VMEM((2, 6, lanes), bf16),
        ]
        + [pltpu.SemaphoreType.DMA((count,)) for count in (1, 6, 1, n_ma - 1, 1, 2, 1, 1, 1, 1, 1, 1, 1, 1)]
        + [pltpu.SemaphoreType.REGULAR],
        compiler_params=pltpu.CompilerParams(
            collective_id=0, has_side_effects=True, vmem_limit_bytes=48 * 1024 * 1024
        ),
    )(*(pltpu.with_memory_space_constraint(x, pltpu.HBM) for x in operands))
    return out.reshape(velocity.shape)


def fits(velocity, legendre):
    n_ma = lax.axis_size("ma")
    n_row = lax.axis_size("row")
    pairs, rows, half_lat = legendre.shape
    levels = velocity.shape[2]
    lat = half_lat // n_ma
    tiles = pairs == 4 and pairs * (rows - 1) == 256 and n_ma % 2 == 0 and n_ma <= 8 and n_row % 2 == 0
    whole = half_lat % n_ma == 0 and half_lat % 128 == 0 and lat % 16 == 0 and lat <= 64 and levels == 4
    return tiles and whole and n_row > 2 and n_ma > 1


def step(velocity, vorticity, legendre, pair_order, lat_weight, diffusivity):
    chosen = fused if fits(velocity, legendre) else local
    return chosen(velocity, vorticity, legendre, pair_order, lat_weight, diffusivity)


def solution(mesh):
    in_specs = (
        P(None, None, "row", "ma", None),
        P(None, None, "row", "ma", None),
        P("ma", None, None),
        P("ma"),
        P(),
        P(),
    )
    out_specs = P(None, None, "row", "ma", None)
    return jax.shard_map(step, mesh=mesh, in_specs=in_specs, out_specs=out_specs, check_vma=False)
```

```python
import functools
import math

import jax
import jax.numpy as jnp
import numpy as np
from jax import lax
from jax.experimental import pallas as pl
from jax.experimental.pallas import tpu as pltpu
from jax.sharding import PartitionSpec as P

NLON = 2048


STEP_SIZE = 1.0


def with_halo(cells, sides, width):
    for axis, dim in sides:
        count = lax.axis_size(axis)
        ends = count - 1
        head = lax.slice_in_dim(cells, 0, width, axis=dim)
        tail = lax.slice_in_dim(cells, cells.shape[dim] - width, cells.shape[dim], axis=dim)
        cells = jnp.concatenate(
            [
                lax.ppermute(tail, axis, [(i, (i + 1) % count) for i in range(ends)]),
                cells,
                lax.ppermute(head, axis, [((i + 1) % count, i) for i in range(ends)]),
            ],
            axis=dim,
        )
    return cells


def row_masks(low_order, pack_rows):
    orders_all = pack_rows - 1
    row_index = jnp.arange(pack_rows, dtype=jnp.int32)[None, :]
    low_column = low_order[:, None]
    is_lower = row_index < orders_all - low_column
    not_lower = jnp.logical_not(is_lower)
    even_low = row_index % 2 == 0
    even_high = (row_index + low_column) % 2 == 0
    low_pair = jnp.stack([is_lower & even_low, is_lower & jnp.logical_not(even_low)])
    high_pair = jnp.stack([not_lower & even_high, not_lower & jnp.logical_not(even_high)])
    return jnp.stack([low_pair, high_pair])


def cross_product(velocity_grid, vorticity_grid):
    return jnp.stack(
        [
            velocity_grid[1] * vorticity_grid[2] - velocity_grid[2] * vorticity_grid[1],
            velocity_grid[2] * vorticity_grid[0] - velocity_grid[0] * vorticity_grid[2],
            velocity_grid[0] * vorticity_grid[1] - velocity_grid[1] * vorticity_grid[0],
        ]
    )


def lon_table(column_order, is_imag, lon_start, lon_count):
    lon_index = lon_start + jnp.arange(lon_count, dtype=jnp.int32)
    angle_index = column_order[:, None] * lon_index[None, :] % NLON
    angle_value = angle_index.astype(jnp.float32) * (2.0 * math.pi / NLON)
    return jnp.where(is_imag[:, None], -jnp.sin(angle_value), jnp.cos(angle_value))


def local(velocity, vorticity, legendre, pair_order, lat_weight, diffusivity):
    pair_count = pair_order.shape[0]
    pack_rows = legendre.shape[1]
    half_lat = legendre.shape[2]
    nlat_all = 2 * half_lat
    levels_dev = velocity.shape[2]
    orders_all = pack_rows - 1
    inv_orders = 1.0 / math.sqrt(orders_all)
    inv_lon = 1.0 / math.sqrt(NLON)
    lon_width = NLON // 4
    mask_bool = row_masks(pair_order, pack_rows)
    fields = jnp.concatenate([velocity, vorticity], axis=0)
    masked = fields[None, None] * mask_bool.astype(jnp.bfloat16)[:, :, None, None, None]
    halves = jnp.einsum(
        "oqfilsr,srj->qfliosj", masked, legendre, preferred_element_type=jnp.float32
    )
    north_part = halves[0] + halves[1]
    south_part = halves[0] - halves[1]
    both_parts = jnp.concatenate([north_part, south_part], axis=-1)
    spectral = jnp.transpose(both_parts, (0, 1, 5, 2, 3, 4))
    spectral = spectral.reshape(6, levels_dev, nlat_all, 4 * pair_count).astype(jnp.bfloat16)
    gathered_ids = lax.all_gather(pair_order, "ma", axis=0, tiled=True)
    pair_slots = gathered_ids.reshape(-1, 1, 1, pair_count)
    both_orders = jnp.concatenate([pair_slots, orders_all - 1 - pair_slots], axis=2)
    full_shape = (both_orders.shape[0], 2, 2, pair_count)
    column_order = jnp.broadcast_to(both_orders, full_shape).reshape(-1)
    part_index = jnp.arange(2, dtype=jnp.int32)[None, :, None, None]
    is_imag = jnp.broadcast_to(part_index, full_shape).reshape(-1) == 1
    tables = [
        lon_table(column_order, is_imag, lon_block * lon_width, lon_width).astype(jnp.bfloat16)
        for lon_block in range(4)
    ]
    spec_block = lax.all_to_all(spectral, "ma", split_axis=2, concat_axis=3, tiled=True)
    accumulated = jnp.zeros((3,) + spec_block.shape[1:], jnp.float32)
    for lon_block in range(4):
        table_block = tables[lon_block]
        grid_values = (
            jnp.einsum("flac,cb->flab", spec_block, table_block, preferred_element_type=jnp.float32)
            * inv_orders
        )
        lamb_vector = cross_product(grid_values[:3], grid_values[3:])
        accumulated = accumulated + jnp.einsum(
            "flab,cb->flac",
            lamb_vector,
            table_block.astype(jnp.float32),
            precision=lax.Precision.HIGH,
            preferred_element_type=jnp.float32,
        )
    lamb_spec = (accumulated * inv_lon).astype(jnp.bfloat16)
    selector = jnp.transpose(mask_bool.astype(jnp.float32), (1, 0, 2, 3))[:, None, None, None]
    lamb_block = lax.all_to_all(lamb_spec, "ma", split_axis=3, concat_axis=2, tiled=True)
    item_count = lamb_block.shape[0]
    shaped = lamb_block.astype(jnp.float32).reshape(
        item_count, levels_dev, nlat_all, 2, 2, pair_count
    )
    shaped = jnp.transpose(shaped, (0, 1, 3, 4, 5, 2))
    north_side = shaped[..., :half_lat]
    south_side = shaped[..., half_lat:]
    weighted = jnp.stack(
        [lat_weight * (north_side + south_side), lat_weight * (north_side - south_side)]
    )
    weighted = weighted.astype(jnp.bfloat16)
    projected = jnp.einsum(
        "qfliosj,srj->qfliosr", weighted, legendre, preferred_element_type=jnp.float32
    )
    picked = jnp.sum(projected * selector, axis=(0, 4))
    tendency = jnp.transpose(picked, (0, 2, 1, 3, 4))
    source = velocity.astype(jnp.float32) + STEP_SIZE * tendency
    row_start = lax.axis_index("row") * levels_dev
    level_total = levels_dev * lax.axis_size("row")
    extended = with_halo(source.astype(jnp.bfloat16), (("row", 2),), 2).astype(source.dtype)
    padded_coupling = jnp.pad(diffusivity, (2, 2))
    wide_coupling = lax.dynamic_slice_in_dim(padded_coupling, row_start, levels_dev + 4)[
        None, None, :, None, None
    ]
    inner_coupling = wide_coupling[:, :, 1:-1]
    first_wide = (
        extended[:, :, 1:-1] + inner_coupling * (extended[:, :, :-2] + extended[:, :, 2:])
    ) / (1.0 + 2.0 * inner_coupling)
    global_level = row_start - 1 + jnp.arange(levels_dev + 2, dtype=jnp.int32)
    inside = ((global_level >= 0) & (global_level < level_total)).astype(jnp.float32)
    first_wide = first_wide * inside[None, None, :, None, None]
    own_coupling = wide_coupling[:, :, 2:-2]
    return (source + own_coupling * (first_wide[:, :, :-2] + first_wide[:, :, 2:])) / (
        1.0 + 2.0 * own_coupling
    )

def lon_count(orders_all):
    need = 3 * (orders_all - 1) + 1
    return min(NLON, -(-need // 64) * 64)


def remote(src, dst, send_sem, recv_sem, device_id):
    return pltpu.make_async_remote_copy(
        src_ref=src,
        dst_ref=dst,
        send_sem=send_sem,
        recv_sem=recv_sem,
        device_id=device_id,
        device_id_type=pl.DeviceIdType.MESH,
    )


def fused_kernel(
    n_ma, n_row, pairs, rows, levels, scale,
    velocity_hbm, vorticity_hbm, legendre_hbm, order_hbm, weight_hbm, dif_hbm, tab_hbm, tab_t_hbm,
    out_ref,
    velocity_ref, vorticity_ref, legendre_ref, order_ref, weight_ref, dif_ref, tab_ref, tab_t_ref, load_sem,
    leg_rows, leg_ref, rest_ref, coef_all, leg_all, rest_all, rest_t, end_op, end_spec, onehot, ops, spec, wgt, part, part_in, far_in, far_sum, near_out, near_in,
    coef_send, coef_recv, leg_send, leg_recv, swap_send, swap_recv, rest_send, rest_recv, part_send, part_recv, far_send, far_recv, near_send, near_recv, ready,
):
    me = lax.axis_index("ma")
    row = lax.axis_index("row")
    _, chunks, groups, wide = coef_all.shape
    coef_ref = coef_all.at[0]
    fields2 = groups // 2
    orders = rows - 1
    slots = 2 * pairs
    full = n_ma * slots
    lat = leg_ref.shape[2]
    side = wide // 2
    main = pairs * orders
    per_chunk = pairs // chunks
    f32 = jnp.float32
    bf16 = jnp.bfloat16
    n_z = n_ma // 2
    z, y = me // 2, lax.rem(me, 2)
    mate = me + 1 - 2 * y
    half = lax.rem(row, 2)
    mate_row = row + 1 - 2 * half

    def target(s):
        return lax.rem(z + s // 2, n_z) * 2 + lax.rem(y + lax.rem(s, 2), 2)

    def origin(s):
        return lax.rem(z + n_z - s // 2, n_z) * 2 + lax.rem(y + lax.rem(s, 2), 2)

    far_row = row + 2 * half - 1
    has_far = (far_row >= 0) & (far_row < n_row)

    barrier = pltpu.get_barrier_semaphore()
    for d in range(1, n_ma):
        pl.semaphore_signal(
            barrier, inc=1, device_id=(lax.rem(me + d, n_ma), row), device_id_type=pl.DeviceIdType.MESH
        )
    pl.semaphore_signal(barrier, inc=1, device_id=(me, mate_row), device_id_type=pl.DeviceIdType.MESH)

    @pl.when(has_far)
    def _():
        pl.semaphore_signal(barrier, inc=1, device_id=(me, far_row), device_id_type=pl.DeviceIdType.MESH)

    loads = [
        pltpu.make_async_copy(src, dst, load_sem.at[i])
        for i, (src, dst) in enumerate(
            [
                (legendre_hbm, legendre_ref),
                (velocity_hbm, velocity_ref),
                (vorticity_hbm, vorticity_ref),
                (order_hbm, order_ref),
                (weight_hbm, weight_ref),
                (dif_hbm, dif_ref),
                (tab_hbm, tab_ref),
                (tab_t_hbm, tab_t_ref),
            ]
        )
    ]
    for load in loads:
        load.start()
    for load in loads[:4]:
        load.wait()

    for r in range(rows):
        values = legendre_ref[r].astype(f32)
        for t in range(leg_rows.shape[0]):
            leg_rows[t, r * pairs : (r + 1) * pairs, :] = values[:, t * wide : (t + 1) * wide]
    packs = [
        jnp.concatenate([velocity_ref[...].astype(f32)[:, p], vorticity_ref[...].astype(f32)[:, p]], axis=0)
        for p in range(pairs)
    ]
    column = lax.broadcasted_iota(jnp.int32, (groups, wide), 1)
    ends = jnp.zeros((groups, wide), f32)
    for p in range(pairs):
        ends = jnp.where(column == p, packs[p][:, orders:], ends)
    ends = jnp.concatenate([ends, jnp.zeros((wide - groups, wide), f32)], axis=0)
    ends = jnp.transpose(ends)[0:pairs, 0:side]
    tails = jnp.concatenate([leg_rows[t, main : main + pairs, :] for t in range(leg_rows.shape[0])], axis=1)
    order_rows = [jnp.full((1, wide), order_ref[p].astype(f32)) for p in range(pairs)]
    filler = jnp.zeros((pairs, side - lat), f32)
    for b in range(n_ma):
        data_rows = jnp.concatenate([ends, tails[:, b * lat : (b + 1) * lat], filler], axis=1)
        rest_ref[b] = jnp.concatenate([data_rows] + order_rows, axis=0).astype(bf16)
    for c in range(chunks):
        members = range(c * per_chunk, (c + 1) * per_chunk)
        coef_all[0, c] = jnp.concatenate([packs[p][:, :orders] for p in members], axis=1).astype(bf16)
        turned = jnp.concatenate(
            [
                jnp.transpose(
                    jnp.concatenate([leg_rows[t, pl.ds(p, orders, stride=pairs), :] for p in members], axis=0)
                )
                for t in range(leg_rows.shape[0])
            ],
            axis=0,
        ).astype(bf16)
        for b in range(n_ma):
            leg_ref[b, c] = turned[b * lat : (b + 1) * lat]

    pl.semaphore_wait(barrier, n_ma + has_far.astype(jnp.int32))

    passed = [s for s in (4,) if s < n_ma]
    gained = [s + 1 for s in passed]
    far_first = sorted(range(1, n_ma), key=lambda s: (-min(s // 2, n_z - s // 2), -(s // 2), s % 2))
    direct = [s for s in (7, 3, 6, 2, 1) if s < n_ma]
    coef_groups = [[s] for s in passed] + [direct[:2], direct[2:], gained]
    leg_groups = [far_first[: n_ma // 2], far_first[n_ma // 2 :]]

    def wait_blocks(ref, count, sem):
        blocks = ref.at[pl.ds(0, count)]
        pltpu.make_async_copy(blocks, blocks, sem).wait()

    def coef_copy(s):
        group = [s in g for g in coef_groups].index(True)
        if s in gained:
            return remote(coef_all.at[s - 1], coef_all.at[s], coef_send.at[0], coef_recv.at[group], (mate, row))
        return remote(coef_ref, coef_all.at[s], coef_send.at[0], coef_recv.at[group], (target(s), row))

    def leg_copy(s):
        peer = target(s)
        return remote(leg_ref.at[peer], leg_all.at[s], leg_send.at[0], leg_recv.at[s - 1], (peer, row))

    def share_copy(s):
        group = [s in g for g in leg_groups].index(True)
        return remote(leg_all.at[s], leg_all.at[s], swap_send.at[0], swap_recv.at[group], (me, mate_row))

    def rest_copy(s):
        peer = target(s)
        return remote(rest_ref.at[peer], rest_all.at[s], rest_send.at[0], rest_recv.at[0], (peer, row))

    for s in far_first:
        rest_copy(s).start()
    for s in passed:
        coef_copy(s).start()

    @pl.when(half == 1)
    def _():
        for s in far_first:
            leg_copy(s).start()

    for s in direct:
        coef_copy(s).start()

    @pl.when(has_far)
    def _():
        pl.semaphore_signal(ready, inc=1, device_id=(me, far_row), device_id_type=pl.DeviceIdType.MESH)

    leg_all[0] = leg_ref[me]
    rest_all[0] = rest_ref[me]

    def clear(d, carry):
        ops[d] = jnp.zeros(ops.shape[1:], bf16)
        return carry

    lax.fori_loop(0, n_ma, clear, 0)
    for load in loads[4:]:
        load.wait()
    weight = jnp.zeros((1, lat), f32)
    for b in range(n_ma):
        weight = jnp.where(me == b, weight_ref[...].reshape(1, -1)[:, b * lat : (b + 1) * lat], weight)
    weight = weight * scale
    gap = jnp.zeros((1, side - lat), f32)
    weight = jnp.concatenate([weight, gap, weight, gap] * 2, axis=1)

    lane = lax.broadcasted_iota(jnp.int32, (pairs, wide), 1)
    sub = lax.broadcasted_iota(jnp.int32, (pairs, wide), 0)
    m_lane = lax.broadcasted_iota(jnp.int32, (slots, orders), 1)
    m_sub = lax.broadcasted_iota(jnp.int32, (slots, orders), 0)
    lane_row = lane % orders
    own = lane // orders == sub % per_chunk

    def low_orders(d):
        return rest_all[d].astype(f32)[pairs:].astype(jnp.int32)

    def place(d):
        low = low_orders(d)
        order = jnp.zeros((slots, orders), jnp.int32)
        for p in range(pairs):
            value = low[p : p + 1, 0:1]
            order = jnp.where(m_sub == 2 * p, value, order)
            order = jnp.where(m_sub == 2 * p + 1, orders - 1 - value, order)
        onehot[d * slots : (d + 1) * slots, :] = (m_lane == order).astype(f32)

    def build(d):
        low = low_orders(d)
        lower = lane_row < orders - low
        north_low = (own & lower).astype(f32)
        north_high = (own & jnp.logical_not(lower)).astype(f32)
        south_low = north_low * (1 - 2 * (lane_row & 1)).astype(f32)
        south_high = north_high * (1 - 2 * ((lane_row + low) & 1)).astype(f32)
        for p in range(pairs):
            c = p // per_chunk
            table = leg_all[d, c].astype(f32)
            at = p * 2 * wide
            for i, factor in enumerate((north_low, south_low, north_high, south_high)):
                ops[d, at + i * side : at + i * side + lat, :] = (table * factor[p : p + 1]).astype(bf16)

    def synth(d):
        for p in range(pairs):
            at = p * 2 * wide
            made = lax.dot_general(
                coef_all[d, p // per_chunk],
                ops[d, at : at + 2 * wide, :],
                (((1,), (1,)), ((), ())),
                preferred_element_type=f32,
            )
            spec[pl.ds(d * slots + 2 * p, groups, stride=full), :] = made[:, :wide]
            spec[pl.ds(d * slots + 2 * p + 1, groups, stride=full), :] = made[:, wide:] + end_spec[d * pairs + p]

    for i, s in enumerate(passed):
        wait_blocks(coef_all, 1, coef_recv.at[i])
        coef_copy(s + 1).start()
    wait_blocks(rest_all, n_ma - 1, rest_recv.at[0])

    def legs(group):
        @pl.when(half == 1)
        def _():
            for s in leg_groups[group]:
                leg_copy(s).wait_recv()
                share_copy(s).start()

        @pl.when(half == 0)
        def _():
            wait_blocks(leg_all, len(leg_groups[group]), swap_recv.at[group])

    rest = rest_all[...].astype(f32).reshape(n_ma * 8, wide)
    rest_t[...] = jnp.transpose(jnp.concatenate([rest, jnp.zeros((wide - n_ma * 8, wide), f32)], axis=0))
    end_lane = lax.broadcasted_iota(jnp.int32, rest.shape, 1)
    end_sign = (1 - 2 * (pltpu.roll(rest, n_ma * 8 - pairs, 0).astype(jnp.int32) & 1)).astype(f32)
    north_end = jnp.where(end_lane < lat, pltpu.roll(rest, side, 1), 0.0)
    south_end = jnp.where((end_lane >= side) & (end_lane < side + lat), rest * end_sign, 0.0)
    end_op[...] = north_end + south_end
    for d in range(n_ma):
        place(d)
    hot = onehot[...].astype(bf16)
    to_grid = jnp.concatenate(
        [
            lax.dot_general(tab_t_ref[c], hot, (((1,), (1,)), ((), ())), preferred_element_type=f32)
            for c in range(2)
        ],
        axis=1,
    ).astype(bf16)
    to_spec = jnp.concatenate(
        [jnp.dot(hot, tab_ref[c], preferred_element_type=f32) for c in range(2)], axis=0
    ).astype(bf16)
    for d in range(n_ma):
        for p in range(pairs):
            i = 8 * d + p
            end_spec[d * pairs + p] = rest_t[0:groups, i : i + 1] * end_op[i : i + 1, :]
    held = [coef_ref[c, 0:fields2].astype(f32) for c in range(chunks)]
    held = jnp.concatenate(held + [rest_t[0:fields2, :]], axis=1)
    held = held.reshape(6, levels, held.shape[1])
    held = [held[:, k, :] for k in range(levels)]
    block = 6 * levels // 2
    lower = jnp.concatenate([held[k][:, c * wide : (c + 1) * wide] for c in range(chunks) for k in (0, 1)], axis=0)
    upper = jnp.concatenate([held[k][:, c * wide : (c + 1) * wide] for c in range(chunks) for k in (2, 3)], axis=0)
    own_end = jnp.concatenate([h[:, main:] for h in held] + [jnp.zeros((wide - fields2, wide), f32)], axis=0)
    own_end = jnp.where(lax.broadcasted_iota(jnp.int32, own_end.shape, 1) < pairs, own_end, 0.0)
    own_velocity = jnp.concatenate([lower, jnp.transpose(own_end)[0:8], upper], axis=0)
    build(0)
    synth(0)
    legs(0)
    for s in leg_groups[0]:
        build(s)
    for s in passed:
        synth(s)
    legs(1)
    for s in leg_groups[1]:
        build(s)
    for group in range(len(passed), len(coef_groups)):
        wait_blocks(coef_all, len(coef_groups[group]), coef_recv.at[group])
        for s in coef_groups[group]:
            synth(s)

    def middle(j):
        grids = []
        for f in range(6):
            blocks = []
            for i in range(2):
                k = 2 * j + i
                parts = [
                    spec[pl.ds(((f * 2 + c) * levels + k) * full, full), :] for c in range(2)
                ]
                blocks.append(jnp.concatenate(parts, axis=0))
            block = jnp.concatenate(blocks, axis=1).astype(bf16)
            grids.append(jnp.dot(to_grid, block, preferred_element_type=f32))
        u, w = grids[:3], grids[3:]
        lamb = [
            u[1] * w[2] - u[2] * w[1],
            u[2] * w[0] - u[0] * w[2],
            u[0] * w[1] - u[1] * w[0],
        ]
        for f in range(3):
            made = jnp.dot(to_spec, lamb[f].astype(bf16), preferred_element_type=f32) * weight
            for i in range(2):
                k = 2 * j + i
                for c in range(2):
                    at = (k * 6 + f * 2 + c) * full
                    wgt[pl.ds(at, full), :] = made[c * full : (c + 1) * full, i * wide : (i + 1) * wide]

    for j in range(levels // 2):
        middle(j)

    def part_copy(d):
        return remote(part.at[d], part_in.at[d], part_send.at[0], part_recv.at[0], (origin(d), row))

    def rows_of(slot):
        return wgt[pl.ds(slot, fields2, stride=full), :]

    def analyse(d):
        heads = []
        for c in range(chunks):
            picked = [rows_of(d * slots + i) for i in range(2 * c * per_chunk, 2 * (c + 1) * per_chunk)]
            lhs = jnp.concatenate(picked, axis=1).astype(bf16)
            first = c * per_chunk * 2 * wide
            heads.append(
                jnp.dot(lhs, ops[d, first : first + per_chunk * 2 * wide, :], preferred_element_type=f32)
            )
        lower = jnp.concatenate([h[:block] for h in heads], axis=0)
        upper = jnp.concatenate([h[block:] for h in heads], axis=0)
        return lower, upper

    body = chunks * block
    sent = pl.ds(pl.multiple_of(half * body, 8), body + 8)

    def far_copy(d):
        return remote(part.at[d, sent], far_in.at[d], far_send.at[0], far_recv.at[0], (origin(d), far_row))

    @pl.when(has_far)
    def _():
        pl.semaphore_wait(ready, 1)

    upper_z = z // (n_z // 2)

    def project(steps):
        made = []
        for i in steps:
            d = upper_z * (n_ma - i) + (1 - upper_z) * (1 + lax.rem(i, n_ma - 1))
            made.append((d, analyse(d)))
        return made

    def send(made):
        for d, (lower, upper) in made:
            part[d, 0:body] = lower.astype(bf16)
            part[d, body + 8 :] = upper.astype(bf16)
        for d, _ in made:
            part_copy(d).start()

        @pl.when(has_far)
        def _():
            for d, _ in made:
                far_copy(d).start()

    made = project([1, 2])
    highs = jnp.concatenate([rows_of(2 * i + 1) for i in range(n_ma * pairs)], axis=0).astype(bf16)
    ends = lax.dot_general(
        highs, end_op[...].astype(bf16), (((1,), (1,)), ((), ())), preferred_element_type=f32
    )
    end_column = lax.broadcasted_iota(jnp.int32, (fields2, n_ma * 8), 1)
    end_sum = jnp.zeros((fields2, n_ma * 8), f32)
    for i in range(n_ma * pairs):
        at = i // pairs * 8 + i % pairs
        end_sum = jnp.where(end_column == at, ends[i * fields2 : (i + 1) * fields2], end_sum)
    end_sum = jnp.concatenate([end_sum, jnp.zeros((fields2, wide - n_ma * 8), f32)], axis=1)
    end_sum = jnp.transpose(jnp.concatenate([end_sum, jnp.zeros((wide - fields2, wide), f32)], axis=0))
    for d in range(n_ma):
        part[d, body : body + 8] = end_sum[8 * d : 8 * (d + 1)].astype(bf16)

    send(made)
    for i in range(3, n_ma - 1, 2):
        send(project([i, i + 1]))
    made = project([n_ma - 1])
    lower, upper = analyse(0)
    send(made)
    source = jnp.concatenate([lower, end_sum[0:8], upper], axis=0) + own_velocity
    part[0] = source.astype(bf16)

    @pl.when(has_far)
    def _():
        far_copy(0).start()

    wait_blocks(part_in, n_ma - 1, part_recv.at[0])
    for d in range(1, n_ma):
        source = source + part_in[d].astype(f32)

    def end_rows(values):
        turned = jnp.transpose(jnp.concatenate([values, jnp.zeros((wide - 8, wide), f32)], axis=0))[0:fields2]
        return jnp.where(lax.broadcasted_iota(jnp.int32, turned.shape, 1) < pairs, turned, 0.0)

    def level_pair(values, ends):
        made = []
        for k in range(2):
            heads = [values[c * block + 6 * k : c * block + 6 * (k + 1)] for c in range(chunks)]
            made.append(jnp.concatenate(heads + [ends[6 * k : 6 * (k + 1)]], axis=1))
        return made

    turned = end_rows(source[body : body + 8])
    own_levels = level_pair(source[0:body], turned[0:block]) + level_pair(source[body + 8 :], turned[block:fields2])
    for i in range(2):
        near_out[i] = jnp.where(half == 0, own_levels[levels - 2 + i], own_levels[i]).astype(bf16)
    near_copy = remote(near_out, near_in, near_send.at[0], near_recv.at[0], (me, mate_row))
    near_copy.start()

    @pl.when(has_far)
    def _():
        wait_blocks(far_in, n_ma, far_recv.at[0])
        total = far_in[0].astype(f32)
        for d in range(1, n_ma):
            total = total + far_in[d].astype(f32)
        far_sum[...] = total

    @pl.when(jnp.logical_not(has_far))
    def _():
        far_sum[...] = jnp.zeros(far_sum.shape, f32)

    far_body = far_sum[pl.ds(pl.multiple_of((1 - half) * 8, 8), body), :]
    turned = end_rows(far_sum[pl.ds(pl.multiple_of(half * body, 8), 8), :])
    far_levels = level_pair(far_body, jnp.where(half == 0, turned[block:fields2], turned[0:block]))

    wait_blocks(coef_all, n_ma - 1, coef_send.at[0])
    wait_blocks(rest_all, n_ma - 1, rest_send.at[0])
    wait_blocks(part_in, n_ma - 1, part_send.at[0])

    @pl.when(half == 1)
    def _():
        wait_blocks(leg_all, n_ma - 1, leg_send.at[0])
        wait_blocks(leg_all, n_ma - 1, swap_send.at[0])

    @pl.when(has_far)
    def _():
        wait_blocks(far_in, n_ma, far_send.at[0])

    near_copy.wait_recv()

    shape = own_levels[0].shape
    has_left = (row > 0).astype(f32)
    has_right = (row < n_row - 1).astype(f32)
    near_levels = [near_in[i].astype(f32) for i in range(2)]
    before = [jnp.where(half == 0, a, b) for a, b in zip(far_levels, near_levels)]
    after = [jnp.where(half == 0, b, a) for a, b in zip(far_levels, near_levels)]
    wide_levels = before + own_levels + after
    coupling = [jnp.full(shape, dif_ref[lax.rem((row + n_row) * levels + i - 2, n_row * levels)]) for i in range(levels + 4)]
    inverse = [1.0 / (1.0 + 2.0 * c) for c in coupling]
    first = [
        (wide_levels[i] + coupling[i] * (wide_levels[i - 1] + wide_levels[i + 1])) * inverse[i]
        for i in range(1, levels + 3)
    ]
    first[0] = first[0] * has_left
    first[-1] = first[-1] * has_right
    for k in range(levels):
        done = (wide_levels[k + 2] + coupling[k + 2] * (first[k] + first[k + 2])) * inverse[k + 2]
        for p in range(pairs):
            line = jnp.concatenate(
                [done[:, p * orders : (p + 1) * orders], done[:, main + p : main + p + 1]], axis=1
            )
            for i in range(fields2 // levels):
                out_ref[i * levels + k, p : p + 1, :] = line[i : i + 1]
    near_copy.wait_send()


def fused(velocity, vorticity, legendre, pair_order, lat_weight, diffusivity):
    n_ma = lax.axis_size("ma")
    n_row = lax.axis_size("row")
    pairs, rows, half_lat = legendre.shape
    levels = velocity.shape[2]
    orders = rows - 1
    main = pairs * orders
    chunks = main // 128
    lanes = main + 128
    lat = half_lat // n_ma
    slots = 2 * pairs
    full = n_ma * slots
    points = lon_count(orders)
    bf16 = jnp.bfloat16
    f32 = jnp.float32
    groups = 12 * levels
    scale = (NLON / points) / math.sqrt(NLON) / orders
    angle = np.outer(np.arange(orders), np.arange(points)) % points * (2.0 * math.pi / points)
    table = np.stack([np.cos(angle), -np.sin(angle)])
    tab = jnp.asarray(table, bf16)
    tab_t = jnp.asarray(np.transpose(table, (0, 2, 1)), bf16)
    vmem = pl.BlockSpec(memory_space=pltpu.VMEM)
    away = pl.BlockSpec(memory_space=pltpu.HBM)
    operands = (
        velocity.reshape(6 * levels, pairs, rows),
        vorticity.reshape(6 * levels, pairs, rows),
        jnp.transpose(legendre, (1, 0, 2)),
        pair_order,
        lat_weight,
        diffusivity,
        tab,
        tab_t,
    )
    out = pl.pallas_call(
        functools.partial(fused_kernel, n_ma, n_row, pairs, rows, levels, scale),
        out_shape=jax.ShapeDtypeStruct((6 * levels, pairs, rows), f32),
        in_specs=[away] * 8,
        out_specs=vmem,
        scratch_shapes=[
            pltpu.VMEM((6 * levels, pairs, rows), bf16),
            pltpu.VMEM((6 * levels, pairs, rows), bf16),
            pltpu.VMEM((rows, pairs, half_lat), bf16),
            pltpu.SMEM((pairs,), jnp.int32),
            pltpu.VMEM((half_lat,), f32),
            pltpu.SMEM(diffusivity.shape, f32),
            pltpu.VMEM(tab.shape, bf16),
            pltpu.VMEM(tab_t.shape, bf16),
            pltpu.SemaphoreType.DMA((8,)),
            pltpu.VMEM((half_lat // 128, rows * pairs + 4, 128), f32),
            pltpu.VMEM((n_ma, chunks, lat, 128), bf16),
            pltpu.VMEM((n_ma, 8, 128), bf16),
            pltpu.VMEM((n_ma, chunks, groups, 128), bf16),
            pltpu.VMEM((n_ma, chunks, lat, 128), bf16),
            pltpu.VMEM((n_ma, 8, 128), bf16),
            pltpu.VMEM((128, 128), f32),
            pltpu.VMEM((n_ma * 8, 128), f32),
            pltpu.VMEM((n_ma * pairs, groups, 128), f32),
            pltpu.VMEM((full, orders), f32),
            pltpu.VMEM((n_ma, pairs * 256, 128), bf16),
            pltpu.VMEM((groups * full, 128), f32),
            pltpu.VMEM((groups // 2 * full, 128), f32),
            pltpu.VMEM((n_ma, chunks * groups // 2 + 8, 128), bf16),
            pltpu.VMEM((n_ma, chunks * groups // 2 + 8, 128), bf16),
            pltpu.VMEM((n_ma, chunks * groups // 4 + 8, 128), bf16),
            pltpu.VMEM((chunks * groups // 4 + 8, 128), f32),
            pltpu.VMEM((2, 6, lanes), bf16),
            pltpu.VMEM((2, 6, lanes), bf16),
        ]
        + [pltpu.SemaphoreType.DMA((count,)) for count in (1, 6, 1, n_ma - 1, 1, 2, 1, 1, 1, 1, 1, 1, 1, 1)]
        + [pltpu.SemaphoreType.REGULAR],
        compiler_params=pltpu.CompilerParams(
            collective_id=0, has_side_effects=True, vmem_limit_bytes=48 * 1024 * 1024
        ),
    )(*(pltpu.with_memory_space_constraint(x, pltpu.HBM) for x in operands))
    return out.reshape(velocity.shape)


def fits(velocity, legendre):
    n_ma = lax.axis_size("ma")
    n_row = lax.axis_size("row")
    pairs, rows, half_lat = legendre.shape
    levels = velocity.shape[2]
    lat = half_lat // n_ma
    tiles = pairs == 4 and pairs * (rows - 1) == 256 and n_ma % 2 == 0 and n_ma <= 8 and n_row % 2 == 0
    whole = half_lat % n_ma == 0 and half_lat % 128 == 0 and lat % 16 == 0 and lat <= 64 and levels == 4
    return tiles and whole and n_row > 2 and n_ma > 1


def step(velocity, vorticity, legendre, pair_order, lat_weight, diffusivity):
    chosen = fused if fits(velocity, legendre) else local
    return chosen(velocity, vorticity, legendre, pair_order, lat_weight, diffusivity)


def solution(mesh):
    in_specs = (
        P(None, None, "row", "ma", None),
        P(None, None, "row", "ma", None),
        P("ma", None, None),
        P("ma"),
        P(),
        P(),
    )
    out_specs = P(None, None, "row", "ma", None)
    return jax.shard_map(step, mesh=mesh, in_specs=in_specs, out_specs=out_specs, check_vma=False)
```

```python
import functools
import math

import jax
import jax.numpy as jnp
import numpy as np
from jax import lax
from jax.experimental import pallas as pl
from jax.experimental.pallas import tpu as pltpu
from jax.sharding import PartitionSpec as P

NLON = 2048


STEP_SIZE = 1.0


def with_halo(cells, sides, width):
    for axis, dim in sides:
        count = lax.axis_size(axis)
        ends = count - 1
        head = lax.slice_in_dim(cells, 0, width, axis=dim)
        tail = lax.slice_in_dim(cells, cells.shape[dim] - width, cells.shape[dim], axis=dim)
        cells = jnp.concatenate(
            [
                lax.ppermute(tail, axis, [(i, (i + 1) % count) for i in range(ends)]),
                cells,
                lax.ppermute(head, axis, [((i + 1) % count, i) for i in range(ends)]),
            ],
            axis=dim,
        )
    return cells


def row_masks(low_order, pack_rows):
    orders_all = pack_rows - 1
    row_index = jnp.arange(pack_rows, dtype=jnp.int32)[None, :]
    low_column = low_order[:, None]
    is_lower = row_index < orders_all - low_column
    not_lower = jnp.logical_not(is_lower)
    even_low = row_index % 2 == 0
    even_high = (row_index + low_column) % 2 == 0
    low_pair = jnp.stack([is_lower & even_low, is_lower & jnp.logical_not(even_low)])
    high_pair = jnp.stack([not_lower & even_high, not_lower & jnp.logical_not(even_high)])
    return jnp.stack([low_pair, high_pair])


def cross_product(velocity_grid, vorticity_grid):
    return jnp.stack(
        [
            velocity_grid[1] * vorticity_grid[2] - velocity_grid[2] * vorticity_grid[1],
            velocity_grid[2] * vorticity_grid[0] - velocity_grid[0] * vorticity_grid[2],
            velocity_grid[0] * vorticity_grid[1] - velocity_grid[1] * vorticity_grid[0],
        ]
    )


def lon_table(column_order, is_imag, lon_start, lon_count):
    lon_index = lon_start + jnp.arange(lon_count, dtype=jnp.int32)
    angle_index = column_order[:, None] * lon_index[None, :] % NLON
    angle_value = angle_index.astype(jnp.float32) * (2.0 * math.pi / NLON)
    return jnp.where(is_imag[:, None], -jnp.sin(angle_value), jnp.cos(angle_value))


def local(velocity, vorticity, legendre, pair_order, lat_weight, diffusivity):
    pair_count = pair_order.shape[0]
    pack_rows = legendre.shape[1]
    half_lat = legendre.shape[2]
    nlat_all = 2 * half_lat
    levels_dev = velocity.shape[2]
    orders_all = pack_rows - 1
    inv_orders = 1.0 / math.sqrt(orders_all)
    inv_lon = 1.0 / math.sqrt(NLON)
    lon_width = NLON // 4
    mask_bool = row_masks(pair_order, pack_rows)
    fields = jnp.concatenate([velocity, vorticity], axis=0)
    masked = fields[None, None] * mask_bool.astype(jnp.bfloat16)[:, :, None, None, None]
    halves = jnp.einsum(
        "oqfilsr,srj->qfliosj", masked, legendre, preferred_element_type=jnp.float32
    )
    north_part = halves[0] + halves[1]
    south_part = halves[0] - halves[1]
    both_parts = jnp.concatenate([north_part, south_part], axis=-1)
    spectral = jnp.transpose(both_parts, (0, 1, 5, 2, 3, 4))
    spectral = spectral.reshape(6, levels_dev, nlat_all, 4 * pair_count).astype(jnp.bfloat16)
    gathered_ids = lax.all_gather(pair_order, "ma", axis=0, tiled=True)
    pair_slots = gathered_ids.reshape(-1, 1, 1, pair_count)
    both_orders = jnp.concatenate([pair_slots, orders_all - 1 - pair_slots], axis=2)
    full_shape = (both_orders.shape[0], 2, 2, pair_count)
    column_order = jnp.broadcast_to(both_orders, full_shape).reshape(-1)
    part_index = jnp.arange(2, dtype=jnp.int32)[None, :, None, None]
    is_imag = jnp.broadcast_to(part_index, full_shape).reshape(-1) == 1
    tables = [
        lon_table(column_order, is_imag, lon_block * lon_width, lon_width).astype(jnp.bfloat16)
        for lon_block in range(4)
    ]
    spec_block = lax.all_to_all(spectral, "ma", split_axis=2, concat_axis=3, tiled=True)
    accumulated = jnp.zeros((3,) + spec_block.shape[1:], jnp.float32)
    for lon_block in range(4):
        table_block = tables[lon_block]
        grid_values = (
            jnp.einsum("flac,cb->flab", spec_block, table_block, preferred_element_type=jnp.float32)
            * inv_orders
        )
        lamb_vector = cross_product(grid_values[:3], grid_values[3:])
        accumulated = accumulated + jnp.einsum(
            "flab,cb->flac",
            lamb_vector,
            table_block.astype(jnp.float32),
            precision=lax.Precision.HIGH,
            preferred_element_type=jnp.float32,
        )
    lamb_spec = (accumulated * inv_lon).astype(jnp.bfloat16)
    selector = jnp.transpose(mask_bool.astype(jnp.float32), (1, 0, 2, 3))[:, None, None, None]
    lamb_block = lax.all_to_all(lamb_spec, "ma", split_axis=3, concat_axis=2, tiled=True)
    item_count = lamb_block.shape[0]
    shaped = lamb_block.astype(jnp.float32).reshape(
        item_count, levels_dev, nlat_all, 2, 2, pair_count
    )
    shaped = jnp.transpose(shaped, (0, 1, 3, 4, 5, 2))
    north_side = shaped[..., :half_lat]
    south_side = shaped[..., half_lat:]
    weighted = jnp.stack(
        [lat_weight * (north_side + south_side), lat_weight * (north_side - south_side)]
    )
    weighted = weighted.astype(jnp.bfloat16)
    projected = jnp.einsum(
        "qfliosj,srj->qfliosr", weighted, legendre, preferred_element_type=jnp.float32
    )
    picked = jnp.sum(projected * selector, axis=(0, 4))
    tendency = jnp.transpose(picked, (0, 2, 1, 3, 4))
    source = velocity.astype(jnp.float32) + STEP_SIZE * tendency
    row_start = lax.axis_index("row") * levels_dev
    level_total = levels_dev * lax.axis_size("row")
    extended = with_halo(source.astype(jnp.bfloat16), (("row", 2),), 2).astype(source.dtype)
    padded_coupling = jnp.pad(diffusivity, (2, 2))
    wide_coupling = lax.dynamic_slice_in_dim(padded_coupling, row_start, levels_dev + 4)[
        None, None, :, None, None
    ]
    inner_coupling = wide_coupling[:, :, 1:-1]
    first_wide = (
        extended[:, :, 1:-1] + inner_coupling * (extended[:, :, :-2] + extended[:, :, 2:])
    ) / (1.0 + 2.0 * inner_coupling)
    global_level = row_start - 1 + jnp.arange(levels_dev + 2, dtype=jnp.int32)
    inside = ((global_level >= 0) & (global_level < level_total)).astype(jnp.float32)
    first_wide = first_wide * inside[None, None, :, None, None]
    own_coupling = wide_coupling[:, :, 2:-2]
    return (source + own_coupling * (first_wide[:, :, :-2] + first_wide[:, :, 2:])) / (
        1.0 + 2.0 * own_coupling
    )

def lon_count(orders_all):
    need = 3 * (orders_all - 1) + 1
    return min(NLON, -(-need // 64) * 64)


def remote(src, dst, send_sem, recv_sem, device_id):
    return pltpu.make_async_remote_copy(
        src_ref=src,
        dst_ref=dst,
        send_sem=send_sem,
        recv_sem=recv_sem,
        device_id=device_id,
        device_id_type=pl.DeviceIdType.MESH,
    )


def fused_kernel(
    n_ma, n_row, pairs, rows, levels, scale,
    velocity_hbm, vorticity_hbm, legendre_hbm, order_hbm, weight_hbm, dif_hbm, tab_hbm, tab_t_hbm,
    out_ref,
    velocity_ref, vorticity_ref, legendre_ref, order_ref, weight_ref, dif_ref, tab_ref, tab_t_ref, load_sem,
    leg_rows, leg_ref, rest_ref, coef_all, leg_all, rest_all, rest_t, end_op, end_spec, onehot, ops, spec, wgt, part, part_in, far_in, far_sum, near_out, near_in,
    coef_send, coef_recv, leg_send, leg_recv, swap_send, swap_recv, rest_send, rest_recv, part_send, part_recv, far_send, far_recv, near_send, near_recv, ready,
):
    me = lax.axis_index("ma")
    row = lax.axis_index("row")
    _, chunks, groups, wide = coef_all.shape
    coef_ref = coef_all.at[0]
    fields2 = groups // 2
    orders = rows - 1
    slots = 2 * pairs
    full = n_ma * slots
    lat = leg_ref.shape[2]
    side = wide // 2
    main = pairs * orders
    per_chunk = pairs // chunks
    f32 = jnp.float32
    bf16 = jnp.bfloat16
    n_z = n_ma // 2
    z, y = me // 2, lax.rem(me, 2)
    mate = me + 1 - 2 * y
    half = lax.rem(row, 2)
    mate_row = row + 1 - 2 * half

    def target(s):
        return lax.rem(z + s // 2, n_z) * 2 + lax.rem(y + lax.rem(s, 2), 2)

    def origin(s):
        return lax.rem(z + n_z - s // 2, n_z) * 2 + lax.rem(y + lax.rem(s, 2), 2)

    far_row = row + 2 * half - 1
    has_far = (far_row >= 0) & (far_row < n_row)

    barrier = pltpu.get_barrier_semaphore()
    for d in range(1, n_ma):
        pl.semaphore_signal(
            barrier, inc=1, device_id=(lax.rem(me + d, n_ma), row), device_id_type=pl.DeviceIdType.MESH
        )
    pl.semaphore_signal(barrier, inc=1, device_id=(me, mate_row), device_id_type=pl.DeviceIdType.MESH)

    @pl.when(has_far)
    def _():
        pl.semaphore_signal(barrier, inc=1, device_id=(me, far_row), device_id_type=pl.DeviceIdType.MESH)

    loads = [
        pltpu.make_async_copy(src, dst, load_sem.at[i])
        for i, (src, dst) in enumerate(
            [
                (legendre_hbm, legendre_ref),
                (velocity_hbm, velocity_ref),
                (vorticity_hbm, vorticity_ref),
                (order_hbm, order_ref),
                (weight_hbm, weight_ref),
                (dif_hbm, dif_ref),
                (tab_hbm, tab_ref),
                (tab_t_hbm, tab_t_ref),
            ]
        )
    ]
    for load in loads:
        load.start()
    for load in loads[:4]:
        load.wait()

    for r in range(rows):
        values = legendre_ref[r].astype(f32)
        for t in range(leg_rows.shape[0]):
            leg_rows[t, r * pairs : (r + 1) * pairs, :] = values[:, t * wide : (t + 1) * wide]
    packs = [
        jnp.concatenate([velocity_ref[...].astype(f32)[:, p], vorticity_ref[...].astype(f32)[:, p]], axis=0)
        for p in range(pairs)
    ]
    column = lax.broadcasted_iota(jnp.int32, (groups, wide), 1)
    ends = jnp.zeros((groups, wide), f32)
    for p in range(pairs):
        ends = jnp.where(column == p, packs[p][:, orders:], ends)
    ends = jnp.concatenate([ends, jnp.zeros((wide - groups, wide), f32)], axis=0)
    ends = jnp.transpose(ends)[0:pairs, 0:side]
    tails = jnp.concatenate([leg_rows[t, main : main + pairs, :] for t in range(leg_rows.shape[0])], axis=1)
    order_rows = [jnp.full((1, side - lat), order_ref[p].astype(f32)) for p in range(pairs)]
    filler = jnp.concatenate(order_rows, axis=0)
    for b in range(n_ma):
        data_rows = jnp.concatenate([ends, tails[:, b * lat : (b + 1) * lat], filler], axis=1)
        rest_ref[b] = data_rows.astype(bf16)
    for c in range(chunks):
        members = range(c * per_chunk, (c + 1) * per_chunk)
        coef_all[0, c] = jnp.concatenate([packs[p][:, :orders] for p in members], axis=1).astype(bf16)
        turned = jnp.concatenate(
            [
                jnp.transpose(
                    jnp.concatenate([leg_rows[t, pl.ds(p, orders, stride=pairs), :] for p in members], axis=0)
                )
                for t in range(leg_rows.shape[0])
            ],
            axis=0,
        ).astype(bf16)
        for b in range(n_ma):
            leg_ref[b, c] = turned[b * lat : (b + 1) * lat]

    pl.semaphore_wait(barrier, n_ma + has_far.astype(jnp.int32))

    passed = [s for s in (4,) if s < n_ma]
    gained = [s + 1 for s in passed]
    far_first = sorted(range(1, n_ma), key=lambda s: (-min(s // 2, n_z - s // 2), -(s // 2), s % 2))
    direct = [s for s in (7, 3, 6, 2, 1) if s < n_ma]
    coef_groups = [[s] for s in passed] + [direct[:2], direct[2:], gained]
    leg_groups = [far_first[: n_ma // 2], far_first[n_ma // 2 :]]

    def wait_blocks(ref, count, sem):
        blocks = ref.at[pl.ds(0, count)]
        pltpu.make_async_copy(blocks, blocks, sem).wait()

    def coef_copy(s):
        group = [s in g for g in coef_groups].index(True)
        if s in gained:
            return remote(coef_all.at[s - 1], coef_all.at[s], coef_send.at[0], coef_recv.at[group], (mate, row))
        return remote(coef_ref, coef_all.at[s], coef_send.at[0], coef_recv.at[group], (target(s), row))

    def leg_copy(s):
        peer = target(s)
        return remote(leg_ref.at[peer], leg_all.at[s], leg_send.at[0], leg_recv.at[s - 1], (peer, row))

    def share_copy(s):
        group = [s in g for g in leg_groups].index(True)
        return remote(leg_all.at[s], leg_all.at[s], swap_send.at[0], swap_recv.at[group], (me, mate_row))

    def rest_copy(s):
        peer = target(s)
        return remote(rest_ref.at[peer], rest_all.at[s], rest_send.at[0], rest_recv.at[0], (peer, row))

    for s in far_first:
        rest_copy(s).start()
    for s in passed:
        coef_copy(s).start()

    @pl.when(half == 1)
    def _():
        for s in far_first:
            leg_copy(s).start()

    for s in direct:
        coef_copy(s).start()

    @pl.when(has_far)
    def _():
        pl.semaphore_signal(ready, inc=1, device_id=(me, far_row), device_id_type=pl.DeviceIdType.MESH)

    leg_all[0] = leg_ref[me]
    rest_all[0] = rest_ref[me]

    def clear(d, carry):
        ops[d] = jnp.zeros(ops.shape[1:], bf16)
        return carry

    lax.fori_loop(0, n_ma, clear, 0)
    for load in loads[4:]:
        load.wait()
    weight = jnp.zeros((1, lat), f32)
    for b in range(n_ma):
        weight = jnp.where(me == b, weight_ref[...].reshape(1, -1)[:, b * lat : (b + 1) * lat], weight)
    weight = weight * scale
    gap = jnp.zeros((1, side - lat), f32)
    weight = jnp.concatenate([weight, gap, weight, gap] * 2, axis=1)

    lane = lax.broadcasted_iota(jnp.int32, (pairs, wide), 1)
    sub = lax.broadcasted_iota(jnp.int32, (pairs, wide), 0)
    m_lane = lax.broadcasted_iota(jnp.int32, (slots, orders), 1)
    m_sub = lax.broadcasted_iota(jnp.int32, (slots, orders), 0)
    lane_row = lane % orders
    own = lane // orders == sub % per_chunk

    def low_orders(d):
        held_order = rest_all[d].astype(f32)[:, side + lat : side + lat + 1]
        return jnp.broadcast_to(held_order, (pairs, wide)).astype(jnp.int32)

    def place(d):
        low = low_orders(d)
        order = jnp.zeros((slots, orders), jnp.int32)
        for p in range(pairs):
            value = low[p : p + 1, 0:1]
            order = jnp.where(m_sub == 2 * p, value, order)
            order = jnp.where(m_sub == 2 * p + 1, orders - 1 - value, order)
        onehot[d * slots : (d + 1) * slots, :] = (m_lane == order).astype(f32)

    def build(d):
        low = low_orders(d)
        lower = lane_row < orders - low
        north_low = (own & lower).astype(f32)
        north_high = (own & jnp.logical_not(lower)).astype(f32)
        south_low = north_low * (1 - 2 * (lane_row & 1)).astype(f32)
        south_high = north_high * (1 - 2 * ((lane_row + low) & 1)).astype(f32)
        for p in range(pairs):
            c = p // per_chunk
            table = leg_all[d, c].astype(f32)
            at = p * 2 * wide
            for i, factor in enumerate((north_low, south_low, north_high, south_high)):
                ops[d, at + i * side : at + i * side + lat, :] = (table * factor[p : p + 1]).astype(bf16)

    def synth(d):
        for p in range(pairs):
            at = p * 2 * wide
            made = lax.dot_general(
                coef_all[d, p // per_chunk],
                ops[d, at : at + 2 * wide, :],
                (((1,), (1,)), ((), ())),
                preferred_element_type=f32,
            )
            spec[pl.ds(d * slots + 2 * p, groups, stride=full), :] = made[:, :wide]
            spec[pl.ds(d * slots + 2 * p + 1, groups, stride=full), :] = made[:, wide:] + end_spec[d * pairs + p]

    for i, s in enumerate(passed):
        wait_blocks(coef_all, 1, coef_recv.at[i])
        coef_copy(s + 1).start()
    wait_blocks(rest_all, n_ma - 1, rest_recv.at[0])

    def legs(group):
        @pl.when(half == 1)
        def _():
            for s in leg_groups[group]:
                leg_copy(s).wait_recv()
                share_copy(s).start()

        @pl.when(half == 0)
        def _():
            wait_blocks(leg_all, len(leg_groups[group]), swap_recv.at[group])

    rest = []
    for d in range(n_ma):
        rest += [rest_all[d].astype(f32), low_orders(d).astype(f32)]
    rest = jnp.concatenate(rest, axis=0)
    rest_t[...] = jnp.transpose(jnp.concatenate([rest, jnp.zeros((wide - n_ma * 8, wide), f32)], axis=0))
    end_lane = lax.broadcasted_iota(jnp.int32, rest.shape, 1)
    end_sign = (1 - 2 * (pltpu.roll(rest, n_ma * 8 - pairs, 0).astype(jnp.int32) & 1)).astype(f32)
    north_end = jnp.where(end_lane < lat, pltpu.roll(rest, side, 1), 0.0)
    south_end = jnp.where((end_lane >= side) & (end_lane < side + lat), rest * end_sign, 0.0)
    end_op[...] = north_end + south_end
    for d in range(n_ma):
        place(d)
    hot = onehot[...].astype(bf16)
    to_grid = jnp.concatenate(
        [
            lax.dot_general(tab_t_ref[c], hot, (((1,), (1,)), ((), ())), preferred_element_type=f32)
            for c in range(2)
        ],
        axis=1,
    ).astype(bf16)
    to_spec = jnp.concatenate(
        [jnp.dot(hot, tab_ref[c], preferred_element_type=f32) for c in range(2)], axis=0
    ).astype(bf16)
    for d in range(n_ma):
        for p in range(pairs):
            i = 8 * d + p
            end_spec[d * pairs + p] = rest_t[0:groups, i : i + 1] * end_op[i : i + 1, :]
    held = [coef_ref[c, 0:fields2].astype(f32) for c in range(chunks)]
    held = jnp.concatenate(held + [rest_t[0:fields2, :]], axis=1)
    held = held.reshape(6, levels, held.shape[1])
    held = [held[:, k, :] for k in range(levels)]
    block = 6 * levels // 2
    lower = jnp.concatenate([held[k][:, c * wide : (c + 1) * wide] for c in range(chunks) for k in (0, 1)], axis=0)
    upper = jnp.concatenate([held[k][:, c * wide : (c + 1) * wide] for c in range(chunks) for k in (2, 3)], axis=0)
    own_end = jnp.concatenate([h[:, main:] for h in held] + [jnp.zeros((wide - fields2, wide), f32)], axis=0)
    own_end = jnp.where(lax.broadcasted_iota(jnp.int32, own_end.shape, 1) < pairs, own_end, 0.0)
    own_velocity = jnp.concatenate([lower, jnp.transpose(own_end)[0:8], upper], axis=0)
    build(0)
    synth(0)
    legs(0)
    for s in leg_groups[0]:
        build(s)
    for s in passed:
        synth(s)
    legs(1)
    for s in leg_groups[1]:
        build(s)
    for group in range(len(passed), len(coef_groups)):
        wait_blocks(coef_all, len(coef_groups[group]), coef_recv.at[group])
        for s in coef_groups[group]:
            synth(s)

    def middle(j):
        grids = []
        for f in range(6):
            blocks = []
            for i in range(2):
                k = 2 * j + i
                parts = [
                    spec[pl.ds(((f * 2 + c) * levels + k) * full, full), :] for c in range(2)
                ]
                blocks.append(jnp.concatenate(parts, axis=0))
            block = jnp.concatenate(blocks, axis=1).astype(bf16)
            grids.append(jnp.dot(to_grid, block, preferred_element_type=f32))
        u, w = grids[:3], grids[3:]
        lamb = [
            u[1] * w[2] - u[2] * w[1],
            u[2] * w[0] - u[0] * w[2],
            u[0] * w[1] - u[1] * w[0],
        ]
        for f in range(3):
            made = jnp.dot(to_spec, lamb[f].astype(bf16), preferred_element_type=f32) * weight
            for i in range(2):
                k = 2 * j + i
                for c in range(2):
                    at = (k * 6 + f * 2 + c) * full
                    wgt[pl.ds(at, full), :] = made[c * full : (c + 1) * full, i * wide : (i + 1) * wide]

    for j in range(levels // 2):
        middle(j)

    def part_copy(d):
        return remote(part.at[d], part_in.at[d], part_send.at[0], part_recv.at[0], (origin(d), row))

    def rows_of(slot):
        return wgt[pl.ds(slot, fields2, stride=full), :]

    def analyse(d):
        heads = []
        for c in range(chunks):
            picked = [rows_of(d * slots + i) for i in range(2 * c * per_chunk, 2 * (c + 1) * per_chunk)]
            lhs = jnp.concatenate(picked, axis=1).astype(bf16)
            first = c * per_chunk * 2 * wide
            heads.append(
                jnp.dot(lhs, ops[d, first : first + per_chunk * 2 * wide, :], preferred_element_type=f32)
            )
        lower = jnp.concatenate([h[:block] for h in heads], axis=0)
        upper = jnp.concatenate([h[block:] for h in heads], axis=0)
        return lower, upper

    body = chunks * block
    sent = pl.ds(pl.multiple_of(half * body, 8), body + 8)

    def far_copy(d):
        return remote(part.at[d, sent], far_in.at[d], far_send.at[0], far_recv.at[0], (origin(d), far_row))

    @pl.when(has_far)
    def _():
        pl.semaphore_wait(ready, 1)

    upper_z = z // (n_z // 2)

    def project(steps):
        made = []
        for i in steps:
            d = upper_z * (n_ma - i) + (1 - upper_z) * (1 + lax.rem(i, n_ma - 1))
            made.append((d, analyse(d)))
        return made

    def send(made):
        for d, (lower, upper) in made:
            part[d, 0:body] = lower.astype(bf16)
            part[d, body + 8 :] = upper.astype(bf16)
        @pl.when(has_far)
        def _():
            for d, _ in made:
                far_copy(d).start()

        for d, _ in made:
            part_copy(d).start()

    made = project([1, 2])
    highs = jnp.concatenate([rows_of(2 * i + 1) for i in range(n_ma * pairs)], axis=0).astype(bf16)
    ends = lax.dot_general(
        highs, end_op[...].astype(bf16), (((1,), (1,)), ((), ())), preferred_element_type=f32
    )
    end_column = lax.broadcasted_iota(jnp.int32, (fields2, n_ma * 8), 1)
    end_sum = jnp.zeros((fields2, n_ma * 8), f32)
    for i in range(n_ma * pairs):
        at = i // pairs * 8 + i % pairs
        end_sum = jnp.where(end_column == at, ends[i * fields2 : (i + 1) * fields2], end_sum)
    end_sum = jnp.concatenate([end_sum, jnp.zeros((fields2, wide - n_ma * 8), f32)], axis=1)
    end_sum = jnp.transpose(jnp.concatenate([end_sum, jnp.zeros((wide - fields2, wide), f32)], axis=0))
    for d in range(n_ma):
        part[d, body : body + 8] = end_sum[8 * d : 8 * (d + 1)].astype(bf16)

    send(made)
    for i in range(3, n_ma - 1, 2):
        send(project([i, i + 1]))
    made = project([n_ma - 1])
    lower, upper = analyse(0)
    send(made)
    source = jnp.concatenate([lower, end_sum[0:8], upper], axis=0) + own_velocity
    part[0] = source.astype(bf16)

    @pl.when(has_far)
    def _():
        far_copy(0).start()

    wait_blocks(part_in, n_ma - 1, part_recv.at[0])
    for d in range(1, n_ma):
        source = source + part_in[d].astype(f32)

    def end_rows(values):
        turned = jnp.transpose(jnp.concatenate([values, jnp.zeros((wide - 8, wide), f32)], axis=0))[0:fields2]
        return jnp.where(lax.broadcasted_iota(jnp.int32, turned.shape, 1) < pairs, turned, 0.0)

    def level_pair(values, ends):
        made = []
        for k in range(2):
            heads = [values[c * block + 6 * k : c * block + 6 * (k + 1)] for c in range(chunks)]
            made.append(jnp.concatenate(heads + [ends[6 * k : 6 * (k + 1)]], axis=1))
        return made

    turned = end_rows(source[body : body + 8])
    own_levels = level_pair(source[0:body], turned[0:block]) + level_pair(source[body + 8 :], turned[block:fields2])
    for i in range(2):
        near_out[i] = jnp.where(half == 0, own_levels[levels - 2 + i], own_levels[i]).astype(bf16)
    near_copy = remote(near_out, near_in, near_send.at[0], near_recv.at[0], (me, mate_row))
    near_copy.start()

    @pl.when(has_far)
    def _():
        wait_blocks(far_in, n_ma, far_recv.at[0])
        total = far_in[0].astype(f32)
        for d in range(1, n_ma):
            total = total + far_in[d].astype(f32)
        far_sum[...] = total

    @pl.when(jnp.logical_not(has_far))
    def _():
        far_sum[...] = jnp.zeros(far_sum.shape, f32)

    far_body = far_sum[pl.ds(pl.multiple_of((1 - half) * 8, 8), body), :]
    turned = end_rows(far_sum[pl.ds(pl.multiple_of(half * body, 8), 8), :])
    far_levels = level_pair(far_body, jnp.where(half == 0, turned[block:fields2], turned[0:block]))

    wait_blocks(coef_all, n_ma - 1, coef_send.at[0])
    wait_blocks(rest_all, n_ma - 1, rest_send.at[0])
    wait_blocks(part_in, n_ma - 1, part_send.at[0])

    @pl.when(half == 1)
    def _():
        wait_blocks(leg_all, n_ma - 1, leg_send.at[0])
        wait_blocks(leg_all, n_ma - 1, swap_send.at[0])

    @pl.when(has_far)
    def _():
        wait_blocks(far_in, n_ma, far_send.at[0])

    near_copy.wait_recv()

    shape = own_levels[0].shape
    has_left = (row > 0).astype(f32)
    has_right = (row < n_row - 1).astype(f32)
    near_levels = [near_in[i].astype(f32) for i in range(2)]
    before = [jnp.where(half == 0, a, b) for a, b in zip(far_levels, near_levels)]
    after = [jnp.where(half == 0, b, a) for a, b in zip(far_levels, near_levels)]
    wide_levels = before + own_levels + after
    coupling = [jnp.full(shape, dif_ref[lax.rem((row + n_row) * levels + i - 2, n_row * levels)]) for i in range(levels + 4)]
    inverse = [1.0 / (1.0 + 2.0 * c) for c in coupling]
    first = [
        (wide_levels[i] + coupling[i] * (wide_levels[i - 1] + wide_levels[i + 1])) * inverse[i]
        for i in range(1, levels + 3)
    ]
    first[0] = first[0] * has_left
    first[-1] = first[-1] * has_right
    for k in range(levels):
        done = (wide_levels[k + 2] + coupling[k + 2] * (first[k] + first[k + 2])) * inverse[k + 2]
        for p in range(pairs):
            line = jnp.concatenate(
                [done[:, p * orders : (p + 1) * orders], done[:, main + p : main + p + 1]], axis=1
            )
            for i in range(fields2 // levels):
                out_ref[i * levels + k, p : p + 1, :] = line[i : i + 1]
    near_copy.wait_send()


def fused(velocity, vorticity, legendre, pair_order, lat_weight, diffusivity):
    n_ma = lax.axis_size("ma")
    n_row = lax.axis_size("row")
    pairs, rows, half_lat = legendre.shape
    levels = velocity.shape[2]
    orders = rows - 1
    main = pairs * orders
    chunks = main // 128
    lanes = main + 128
    lat = half_lat // n_ma
    slots = 2 * pairs
    full = n_ma * slots
    points = lon_count(orders)
    bf16 = jnp.bfloat16
    f32 = jnp.float32
    groups = 12 * levels
    scale = (NLON / points) / math.sqrt(NLON) / orders
    angle = np.outer(np.arange(orders), np.arange(points)) % points * (2.0 * math.pi / points)
    table = np.stack([np.cos(angle), -np.sin(angle)])
    tab = jnp.asarray(table, bf16)
    tab_t = jnp.asarray(np.transpose(table, (0, 2, 1)), bf16)
    vmem = pl.BlockSpec(memory_space=pltpu.VMEM)
    away = pl.BlockSpec(memory_space=pltpu.HBM)
    operands = (
        velocity.reshape(6 * levels, pairs, rows),
        vorticity.reshape(6 * levels, pairs, rows),
        jnp.transpose(legendre, (1, 0, 2)),
        pair_order,
        lat_weight,
        diffusivity,
        tab,
        tab_t,
    )
    out = pl.pallas_call(
        functools.partial(fused_kernel, n_ma, n_row, pairs, rows, levels, scale),
        out_shape=jax.ShapeDtypeStruct((6 * levels, pairs, rows), f32),
        in_specs=[away] * 8,
        out_specs=vmem,
        scratch_shapes=[
            pltpu.VMEM((6 * levels, pairs, rows), bf16),
            pltpu.VMEM((6 * levels, pairs, rows), bf16),
            pltpu.VMEM((rows, pairs, half_lat), bf16),
            pltpu.SMEM((pairs,), jnp.int32),
            pltpu.VMEM((half_lat,), f32),
            pltpu.SMEM(diffusivity.shape, f32),
            pltpu.VMEM(tab.shape, bf16),
            pltpu.VMEM(tab_t.shape, bf16),
            pltpu.SemaphoreType.DMA((8,)),
            pltpu.VMEM((half_lat // 128, rows * pairs + 4, 128), f32),
            pltpu.VMEM((n_ma, chunks, lat, 128), bf16),
            pltpu.VMEM((n_ma, pairs, 128), bf16),
            pltpu.VMEM((n_ma, chunks, groups, 128), bf16),
            pltpu.VMEM((n_ma, chunks, lat, 128), bf16),
            pltpu.VMEM((n_ma, pairs, 128), bf16),
            pltpu.VMEM((128, 128), f32),
            pltpu.VMEM((n_ma * 8, 128), f32),
            pltpu.VMEM((n_ma * pairs, groups, 128), f32),
            pltpu.VMEM((full, orders), f32),
            pltpu.VMEM((n_ma, pairs * 256, 128), bf16),
            pltpu.VMEM((groups * full, 128), f32),
            pltpu.VMEM((groups // 2 * full, 128), f32),
            pltpu.VMEM((n_ma, chunks * groups // 2 + 8, 128), bf16),
            pltpu.VMEM((n_ma, chunks * groups // 2 + 8, 128), bf16),
            pltpu.VMEM((n_ma, chunks * groups // 4 + 8, 128), bf16),
            pltpu.VMEM((chunks * groups // 4 + 8, 128), f32),
            pltpu.VMEM((2, 6, lanes), bf16),
            pltpu.VMEM((2, 6, lanes), bf16),
        ]
        + [pltpu.SemaphoreType.DMA((count,)) for count in (1, 4, 1, n_ma - 1, 1, 2, 1, 1, 1, 1, 1, 1, 1, 1)]
        + [pltpu.SemaphoreType.REGULAR],
        compiler_params=pltpu.CompilerParams(
            collective_id=0, has_side_effects=True, vmem_limit_bytes=48 * 1024 * 1024
        ),
    )(*(pltpu.with_memory_space_constraint(x, pltpu.HBM) for x in operands))
    return out.reshape(velocity.shape)


def fits(velocity, legendre):
    n_ma = lax.axis_size("ma")
    n_row = lax.axis_size("row")
    pairs, rows, half_lat = legendre.shape
    levels = velocity.shape[2]
    lat = half_lat // n_ma
    tiles = pairs == 4 and pairs * (rows - 1) == 256 and n_ma == 8 and n_row % 2 == 0
    whole = half_lat % n_ma == 0 and half_lat % 128 == 0 and lat % 16 == 0 and lat < 64 and levels == 4
    return tiles and whole and n_row > 2 and n_ma > 1


def step(velocity, vorticity, legendre, pair_order, lat_weight, diffusivity):
    chosen = fused if fits(velocity, legendre) else local
    return chosen(velocity, vorticity, legendre, pair_order, lat_weight, diffusivity)


def solution(mesh):
    in_specs = (
        P(None, None, "row", "ma", None),
        P(None, None, "row", "ma", None),
        P("ma", None, None),
        P("ma"),
        P(),
        P(),
    )
    out_specs = P(None, None, "row", "ma", None)
    return jax.shard_map(step, mesh=mesh, in_specs=in_specs, out_specs=out_specs, check_vma=False)
```

```python
import functools
import math

import jax
import jax.numpy as jnp
import numpy as np
from jax import lax
from jax.experimental import pallas as pl
from jax.experimental.pallas import tpu as pltpu
from jax.sharding import PartitionSpec as P

NLON = 2048


STEP_SIZE = 1.0


def with_halo(cells, sides, width):
    for axis, dim in sides:
        count = lax.axis_size(axis)
        ends = count - 1
        head = lax.slice_in_dim(cells, 0, width, axis=dim)
        tail = lax.slice_in_dim(cells, cells.shape[dim] - width, cells.shape[dim], axis=dim)
        cells = jnp.concatenate(
            [
                lax.ppermute(tail, axis, [(i, (i + 1) % count) for i in range(ends)]),
                cells,
                lax.ppermute(head, axis, [((i + 1) % count, i) for i in range(ends)]),
            ],
            axis=dim,
        )
    return cells


def row_masks(low_order, pack_rows):
    orders_all = pack_rows - 1
    row_index = jnp.arange(pack_rows, dtype=jnp.int32)[None, :]
    low_column = low_order[:, None]
    is_lower = row_index < orders_all - low_column
    not_lower = jnp.logical_not(is_lower)
    even_low = row_index % 2 == 0
    even_high = (row_index + low_column) % 2 == 0
    low_pair = jnp.stack([is_lower & even_low, is_lower & jnp.logical_not(even_low)])
    high_pair = jnp.stack([not_lower & even_high, not_lower & jnp.logical_not(even_high)])
    return jnp.stack([low_pair, high_pair])


def cross_product(velocity_grid, vorticity_grid):
    return jnp.stack(
        [
            velocity_grid[1] * vorticity_grid[2] - velocity_grid[2] * vorticity_grid[1],
            velocity_grid[2] * vorticity_grid[0] - velocity_grid[0] * vorticity_grid[2],
            velocity_grid[0] * vorticity_grid[1] - velocity_grid[1] * vorticity_grid[0],
        ]
    )


def lon_table(column_order, is_imag, lon_start, lon_count):
    lon_index = lon_start + jnp.arange(lon_count, dtype=jnp.int32)
    angle_index = column_order[:, None] * lon_index[None, :] % NLON
    angle_value = angle_index.astype(jnp.float32) * (2.0 * math.pi / NLON)
    return jnp.where(is_imag[:, None], -jnp.sin(angle_value), jnp.cos(angle_value))


def local(velocity, vorticity, legendre, pair_order, lat_weight, diffusivity):
    pair_count = pair_order.shape[0]
    pack_rows = legendre.shape[1]
    half_lat = legendre.shape[2]
    nlat_all = 2 * half_lat
    levels_dev = velocity.shape[2]
    orders_all = pack_rows - 1
    inv_orders = 1.0 / math.sqrt(orders_all)
    inv_lon = 1.0 / math.sqrt(NLON)
    lon_width = NLON // 4
    mask_bool = row_masks(pair_order, pack_rows)
    fields = jnp.concatenate([velocity, vorticity], axis=0)
    masked = fields[None, None] * mask_bool.astype(jnp.bfloat16)[:, :, None, None, None]
    halves = jnp.einsum(
        "oqfilsr,srj->qfliosj", masked, legendre, preferred_element_type=jnp.float32
    )
    north_part = halves[0] + halves[1]
    south_part = halves[0] - halves[1]
    both_parts = jnp.concatenate([north_part, south_part], axis=-1)
    spectral = jnp.transpose(both_parts, (0, 1, 5, 2, 3, 4))
    spectral = spectral.reshape(6, levels_dev, nlat_all, 4 * pair_count).astype(jnp.bfloat16)
    gathered_ids = lax.all_gather(pair_order, "ma", axis=0, tiled=True)
    pair_slots = gathered_ids.reshape(-1, 1, 1, pair_count)
    both_orders = jnp.concatenate([pair_slots, orders_all - 1 - pair_slots], axis=2)
    full_shape = (both_orders.shape[0], 2, 2, pair_count)
    column_order = jnp.broadcast_to(both_orders, full_shape).reshape(-1)
    part_index = jnp.arange(2, dtype=jnp.int32)[None, :, None, None]
    is_imag = jnp.broadcast_to(part_index, full_shape).reshape(-1) == 1
    tables = [
        lon_table(column_order, is_imag, lon_block * lon_width, lon_width).astype(jnp.bfloat16)
        for lon_block in range(4)
    ]
    spec_block = lax.all_to_all(spectral, "ma", split_axis=2, concat_axis=3, tiled=True)
    accumulated = jnp.zeros((3,) + spec_block.shape[1:], jnp.float32)
    for lon_block in range(4):
        table_block = tables[lon_block]
        grid_values = (
            jnp.einsum("flac,cb->flab", spec_block, table_block, preferred_element_type=jnp.float32)
            * inv_orders
        )
        lamb_vector = cross_product(grid_values[:3], grid_values[3:])
        accumulated = accumulated + jnp.einsum(
            "flab,cb->flac",
            lamb_vector,
            table_block.astype(jnp.float32),
            precision=lax.Precision.HIGH,
            preferred_element_type=jnp.float32,
        )
    lamb_spec = (accumulated * inv_lon).astype(jnp.bfloat16)
    selector = jnp.transpose(mask_bool.astype(jnp.float32), (1, 0, 2, 3))[:, None, None, None]
    lamb_block = lax.all_to_all(lamb_spec, "ma", split_axis=3, concat_axis=2, tiled=True)
    item_count = lamb_block.shape[0]
    shaped = lamb_block.astype(jnp.float32).reshape(
        item_count, levels_dev, nlat_all, 2, 2, pair_count
    )
    shaped = jnp.transpose(shaped, (0, 1, 3, 4, 5, 2))
    north_side = shaped[..., :half_lat]
    south_side = shaped[..., half_lat:]
    weighted = jnp.stack(
        [lat_weight * (north_side + south_side), lat_weight * (north_side - south_side)]
    )
    weighted = weighted.astype(jnp.bfloat16)
    projected = jnp.einsum(
        "qfliosj,srj->qfliosr", weighted, legendre, preferred_element_type=jnp.float32
    )
    picked = jnp.sum(projected * selector, axis=(0, 4))
    tendency = jnp.transpose(picked, (0, 2, 1, 3, 4))
    source = velocity.astype(jnp.float32) + STEP_SIZE * tendency
    row_start = lax.axis_index("row") * levels_dev
    level_total = levels_dev * lax.axis_size("row")
    extended = with_halo(source.astype(jnp.bfloat16), (("row", 2),), 2).astype(source.dtype)
    padded_coupling = jnp.pad(diffusivity, (2, 2))
    wide_coupling = lax.dynamic_slice_in_dim(padded_coupling, row_start, levels_dev + 4)[
        None, None, :, None, None
    ]
    inner_coupling = wide_coupling[:, :, 1:-1]
    first_wide = (
        extended[:, :, 1:-1] + inner_coupling * (extended[:, :, :-2] + extended[:, :, 2:])
    ) / (1.0 + 2.0 * inner_coupling)
    global_level = row_start - 1 + jnp.arange(levels_dev + 2, dtype=jnp.int32)
    inside = ((global_level >= 0) & (global_level < level_total)).astype(jnp.float32)
    first_wide = first_wide * inside[None, None, :, None, None]
    own_coupling = wide_coupling[:, :, 2:-2]
    return (source + own_coupling * (first_wide[:, :, :-2] + first_wide[:, :, 2:])) / (
        1.0 + 2.0 * own_coupling
    )

def lon_count(orders_all):
    need = 3 * (orders_all - 1) + 1
    return min(NLON, -(-need // 64) * 64)


def remote(src, dst, send_sem, recv_sem, device_id):
    return pltpu.make_async_remote_copy(
        src_ref=src,
        dst_ref=dst,
        send_sem=send_sem,
        recv_sem=recv_sem,
        device_id=device_id,
        device_id_type=pl.DeviceIdType.MESH,
    )


def fused_kernel(
    n_ma, n_row, pairs, rows, levels, scale,
    velocity_hbm, vorticity_hbm, legendre_hbm, order_hbm, weight_hbm, dif_hbm, tab_hbm, tab_t_hbm,
    out_ref,
    velocity_ref, vorticity_ref, legendre_ref, order_ref, weight_ref, dif_ref, tab_ref, tab_t_ref, load_sem,
    leg_rows, leg_ref, rest_ref, coef_all, leg_all, rest_all, rest_t, end_op, end_spec, onehot, ops, spec, wgt, part, part_in, far_in, far_sum, near_out, near_in,
    coef_send, coef_recv, leg_send, leg_recv, swap_send, swap_recv, rest_send, rest_recv, part_send, part_recv, far_send, far_recv, near_send, near_recv, ready,
):
    me = lax.axis_index("ma")
    row = lax.axis_index("row")
    _, chunks, groups, wide = coef_all.shape
    coef_ref = coef_all.at[0]
    fields2 = groups // 2
    orders = rows - 1
    slots = 2 * pairs
    full = n_ma * slots
    lat = leg_ref.shape[2]
    side = wide // 2
    main = pairs * orders
    per_chunk = pairs // chunks
    f32 = jnp.float32
    bf16 = jnp.bfloat16
    n_z = n_ma // 2
    z, y = me // 2, lax.rem(me, 2)
    mate = me + 1 - 2 * y
    upper_z = z // (n_z // 2)
    half = lax.rem(row, 2)
    mate_row = row + 1 - 2 * half

    def target(s):
        return lax.rem(z + s // 2, n_z) * 2 + lax.rem(y + lax.rem(s, 2), 2)

    def origin(s):
        return lax.rem(z + n_z - s // 2, n_z) * 2 + lax.rem(y + lax.rem(s, 2), 2)

    far_row = row + 2 * half - 1
    has_far = (far_row >= 0) & (far_row < n_row)

    barrier = pltpu.get_barrier_semaphore()
    for d in range(1, n_ma):
        pl.semaphore_signal(
            barrier, inc=1, device_id=(lax.rem(me + d, n_ma), row), device_id_type=pl.DeviceIdType.MESH
        )
    pl.semaphore_signal(barrier, inc=1, device_id=(me, mate_row), device_id_type=pl.DeviceIdType.MESH)

    @pl.when(has_far)
    def _():
        pl.semaphore_signal(barrier, inc=1, device_id=(me, far_row), device_id_type=pl.DeviceIdType.MESH)

    loads = [
        pltpu.make_async_copy(src, dst, load_sem.at[i])
        for i, (src, dst) in enumerate(
            [
                (legendre_hbm, legendre_ref),
                (velocity_hbm, velocity_ref),
                (vorticity_hbm, vorticity_ref),
                (order_hbm, order_ref),
                (weight_hbm, weight_ref),
                (dif_hbm, dif_ref),
                (tab_hbm, tab_ref),
                (tab_t_hbm, tab_t_ref),
            ]
        )
    ]
    for load in loads:
        load.start()
    for load in loads[:4]:
        load.wait()

    for r in range(rows):
        values = legendre_ref[r].astype(f32)
        for t in range(leg_rows.shape[0]):
            leg_rows[t, r * pairs : (r + 1) * pairs, :] = values[:, t * wide : (t + 1) * wide]
    packs = [
        jnp.concatenate([velocity_ref[...].astype(f32)[:, p], vorticity_ref[...].astype(f32)[:, p]], axis=0)
        for p in range(pairs)
    ]
    column = lax.broadcasted_iota(jnp.int32, (groups, wide), 1)
    ends = jnp.zeros((groups, wide), f32)
    for p in range(pairs):
        ends = jnp.where(column == p, packs[p][:, orders:], ends)
    ends = jnp.concatenate([ends, jnp.zeros((wide - groups, wide), f32)], axis=0)
    ends = jnp.transpose(ends)[0:pairs, 0:side]
    tails = jnp.concatenate([leg_rows[t, main : main + pairs, :] for t in range(leg_rows.shape[0])], axis=1)
    order_rows = [jnp.full((1, side - lat), order_ref[p].astype(f32)) for p in range(pairs)]
    filler = jnp.concatenate(order_rows, axis=0)
    for b in range(n_ma):
        data_rows = jnp.concatenate([ends, tails[:, b * lat : (b + 1) * lat], filler], axis=1)
        rest_ref[b] = data_rows.astype(bf16)
    for c in range(chunks):
        members = range(c * per_chunk, (c + 1) * per_chunk)
        coef_all[0, c] = jnp.concatenate([packs[p][:, :orders] for p in members], axis=1).astype(bf16)
        turned = jnp.concatenate(
            [
                jnp.transpose(
                    jnp.concatenate([leg_rows[t, pl.ds(p, orders, stride=pairs), :] for p in members], axis=0)
                )
                for t in range(leg_rows.shape[0])
            ],
            axis=0,
        ).astype(bf16)
        for b in range(n_ma):
            leg_ref[b, c] = turned[b * lat : (b + 1) * lat]

    pl.semaphore_wait(barrier, n_ma + has_far.astype(jnp.int32))

    passed = [s for s in (4,) if s < n_ma]
    gained = [s + 1 for s in passed]
    far_first = sorted(range(1, n_ma), key=lambda s: (-min(s // 2, n_z - s // 2), -(s // 2), s % 2))
    direct = [s for s in (7, 3, 6, 2, 1) if s < n_ma]
    coef_groups = [[s] for s in passed] + [direct[:2], direct[2:], gained]
    leg_groups = [far_first[: n_ma // 2], far_first[n_ma // 2 :]]

    def wait_blocks(ref, count, sem):
        blocks = ref.at[pl.ds(0, count)]
        pltpu.make_async_copy(blocks, blocks, sem).wait()

    def coef_copy(s):
        group = [s in g for g in coef_groups].index(True)
        if s in gained:
            return remote(coef_all.at[s - 1], coef_all.at[s], coef_send.at[0], coef_recv.at[group], (mate, row))
        return remote(coef_ref, coef_all.at[s], coef_send.at[0], coef_recv.at[group], (target(s), row))

    def leg_copy(s):
        peer = target(s)
        return remote(leg_ref.at[peer], leg_all.at[s], leg_send.at[0], leg_recv.at[s - 1], (peer, row))

    def share_copy(s):
        group = [s in g for g in leg_groups].index(True)
        return remote(leg_all.at[s], leg_all.at[s], swap_send.at[0], swap_recv.at[group], (me, mate_row))

    def rest_copy(s):
        peer = target(s)
        return remote(rest_ref.at[peer], rest_all.at[s], rest_send.at[0], rest_recv.at[0], (peer, row))

    for s in far_first:
        rest_copy(s).start()
    for s in passed:
        coef_copy(s).start()

    @pl.when(half == 1)
    def _():
        for j in range(n_z - 1):
            delta = upper_z * (1 + j) + (1 - upper_z) * (n_z - 1 - j)
            leg_copy(2 * delta).start()
            leg_copy(2 * delta + 1).start()
        leg_copy(1).start()

    for s in direct:
        coef_copy(s).start()

    @pl.when(has_far)
    def _():
        pl.semaphore_signal(ready, inc=1, device_id=(me, far_row), device_id_type=pl.DeviceIdType.MESH)

    leg_all[0] = leg_ref[me]
    rest_all[0] = rest_ref[me]

    def clear(d, carry):
        ops[d] = jnp.zeros(ops.shape[1:], bf16)
        return carry

    lax.fori_loop(0, n_ma, clear, 0)
    for load in loads[4:]:
        load.wait()
    weight = jnp.zeros((1, lat), f32)
    for b in range(n_ma):
        weight = jnp.where(me == b, weight_ref[...].reshape(1, -1)[:, b * lat : (b + 1) * lat], weight)
    weight = weight * scale
    gap = jnp.zeros((1, side - lat), f32)
    weight = jnp.concatenate([weight, gap, weight, gap] * 2, axis=1)

    lane = lax.broadcasted_iota(jnp.int32, (pairs, wide), 1)
    sub = lax.broadcasted_iota(jnp.int32, (pairs, wide), 0)
    m_lane = lax.broadcasted_iota(jnp.int32, (slots, orders), 1)
    m_sub = lax.broadcasted_iota(jnp.int32, (slots, orders), 0)
    lane_row = lane % orders
    own = lane // orders == sub % per_chunk

    def low_orders(d):
        held_order = rest_all[d].astype(f32)[:, side + lat : side + lat + 1]
        return jnp.broadcast_to(held_order, (pairs, wide)).astype(jnp.int32)

    def place(d):
        low = low_orders(d)
        order = jnp.zeros((slots, orders), jnp.int32)
        for p in range(pairs):
            value = low[p : p + 1, 0:1]
            order = jnp.where(m_sub == 2 * p, value, order)
            order = jnp.where(m_sub == 2 * p + 1, orders - 1 - value, order)
        onehot[d * slots : (d + 1) * slots, :] = (m_lane == order).astype(f32)

    def build(d):
        low = low_orders(d)
        lower = lane_row < orders - low
        north_low = (own & lower).astype(f32)
        north_high = (own & jnp.logical_not(lower)).astype(f32)
        south_low = north_low * (1 - 2 * (lane_row & 1)).astype(f32)
        south_high = north_high * (1 - 2 * ((lane_row + low) & 1)).astype(f32)
        for p in range(pairs):
            c = p // per_chunk
            table = leg_all[d, c].astype(f32)
            at = p * 2 * wide
            for i, factor in enumerate((north_low, south_low, north_high, south_high)):
                ops[d, at + i * side : at + i * side + lat, :] = (table * factor[p : p + 1]).astype(bf16)

    def synth(d):
        for p in range(pairs):
            at = p * 2 * wide
            made = lax.dot_general(
                coef_all[d, p // per_chunk],
                ops[d, at : at + 2 * wide, :],
                (((1,), (1,)), ((), ())),
                preferred_element_type=f32,
            )
            spec[pl.ds(d * slots + 2 * p, groups, stride=full), :] = made[:, :wide]
            spec[pl.ds(d * slots + 2 * p + 1, groups, stride=full), :] = made[:, wide:] + end_spec[d * pairs + p]

    for i, s in enumerate(passed):
        wait_blocks(coef_all, 1, coef_recv.at[i])
        coef_copy(s + 1).start()
    wait_blocks(rest_all, n_ma - 1, rest_recv.at[0])

    def legs(group):
        @pl.when(half == 1)
        def _():
            for s in leg_groups[group]:
                leg_copy(s).wait_recv()
                share_copy(s).start()

        @pl.when(half == 0)
        def _():
            wait_blocks(leg_all, len(leg_groups[group]), swap_recv.at[group])

    rest = []
    for d in range(n_ma):
        rest += [rest_all[d].astype(f32), low_orders(d).astype(f32)]
    rest = jnp.concatenate(rest, axis=0)
    rest_t[...] = jnp.transpose(jnp.concatenate([rest, jnp.zeros((wide - n_ma * 8, wide), f32)], axis=0))
    end_lane = lax.broadcasted_iota(jnp.int32, rest.shape, 1)
    end_sign = (1 - 2 * (pltpu.roll(rest, n_ma * 8 - pairs, 0).astype(jnp.int32) & 1)).astype(f32)
    north_end = jnp.where(end_lane < lat, pltpu.roll(rest, side, 1), 0.0)
    south_end = jnp.where((end_lane >= side) & (end_lane < side + lat), rest * end_sign, 0.0)
    end_op[...] = north_end + south_end
    for d in range(n_ma):
        place(d)
    hot = onehot[...].astype(bf16)
    to_grid = jnp.concatenate(
        [
            lax.dot_general(tab_t_ref[c], hot, (((1,), (1,)), ((), ())), preferred_element_type=f32)
            for c in range(2)
        ],
        axis=1,
    ).astype(bf16)
    to_spec = jnp.concatenate(
        [jnp.dot(hot, tab_ref[c], preferred_element_type=f32) for c in range(2)], axis=0
    ).astype(bf16)
    for d in range(n_ma):
        for p in range(pairs):
            i = 8 * d + p
            end_spec[d * pairs + p] = rest_t[0:groups, i : i + 1] * end_op[i : i + 1, :]
    held = [coef_ref[c, 0:fields2].astype(f32) for c in range(chunks)]
    held = jnp.concatenate(held + [rest_t[0:fields2, :]], axis=1)
    held = held.reshape(6, levels, held.shape[1])
    held = [held[:, k, :] for k in range(levels)]
    block = 6 * levels // 2
    lower = jnp.concatenate([held[k][:, c * wide : (c + 1) * wide] for c in range(chunks) for k in (0, 1)], axis=0)
    upper = jnp.concatenate([held[k][:, c * wide : (c + 1) * wide] for c in range(chunks) for k in (2, 3)], axis=0)
    own_end = jnp.concatenate([h[:, main:] for h in held] + [jnp.zeros((wide - fields2, wide), f32)], axis=0)
    own_end = jnp.where(lax.broadcasted_iota(jnp.int32, own_end.shape, 1) < pairs, own_end, 0.0)
    own_velocity = jnp.concatenate([lower, jnp.transpose(own_end)[0:8], upper], axis=0)
    build(0)
    synth(0)
    legs(0)
    for s in leg_groups[0]:
        build(s)
    for s in passed:
        synth(s)
    legs(1)
    for s in leg_groups[1]:
        build(s)
    for group in range(len(passed), len(coef_groups)):
        wait_blocks(coef_all, len(coef_groups[group]), coef_recv.at[group])
        for s in coef_groups[group]:
            synth(s)

    def middle(j):
        grids = []
        for f in range(6):
            blocks = []
            for i in range(2):
                k = 2 * j + i
                parts = [
                    spec[pl.ds(((f * 2 + c) * levels + k) * full, full), :] for c in range(2)
                ]
                blocks.append(jnp.concatenate(parts, axis=0))
            block = jnp.concatenate(blocks, axis=1).astype(bf16)
            grids.append(jnp.dot(to_grid, block, preferred_element_type=f32))
        u, w = grids[:3], grids[3:]
        lamb = [
            u[1] * w[2] - u[2] * w[1],
            u[2] * w[0] - u[0] * w[2],
            u[0] * w[1] - u[1] * w[0],
        ]
        for f in range(3):
            made = jnp.dot(to_spec, lamb[f].astype(bf16), preferred_element_type=f32) * weight
            for i in range(2):
                k = 2 * j + i
                for c in range(2):
                    at = (k * 6 + f * 2 + c) * full
                    wgt[pl.ds(at, full), :] = made[c * full : (c + 1) * full, i * wide : (i + 1) * wide]

    for j in range(levels // 2):
        middle(j)

    def part_copy(d):
        return remote(part.at[d], part_in.at[d], part_send.at[0], part_recv.at[0], (origin(d), row))

    def rows_of(slot):
        return wgt[pl.ds(slot, fields2, stride=full), :]

    def analyse(d):
        heads = []
        for c in range(chunks):
            picked = [rows_of(d * slots + i) for i in range(2 * c * per_chunk, 2 * (c + 1) * per_chunk)]
            lhs = jnp.concatenate(picked, axis=1).astype(bf16)
            first = c * per_chunk * 2 * wide
            heads.append(
                jnp.dot(lhs, ops[d, first : first + per_chunk * 2 * wide, :], preferred_element_type=f32)
            )
        lower = jnp.concatenate([h[:block] for h in heads], axis=0)
        upper = jnp.concatenate([h[block:] for h in heads], axis=0)
        return lower, upper

    body = chunks * block
    sent = pl.ds(pl.multiple_of(half * body, 8), body + 8)

    def far_copy(d):
        return remote(part.at[d, sent], far_in.at[d], far_send.at[0], far_recv.at[0], (origin(d), far_row))

    @pl.when(has_far)
    def _():
        pl.semaphore_wait(ready, 1)

    def project(steps):
        made = []
        for i in steps:
            d = upper_z * (n_ma - i) + (1 - upper_z) * (1 + lax.rem(i, n_ma - 1))
            made.append((d, analyse(d)))
        return made

    def send(made):
        for d, (lower, upper) in made:
            part[d, 0:body] = lower.astype(bf16)
            part[d, body + 8 :] = upper.astype(bf16)
        @pl.when(has_far)
        def _():
            for d, _ in made:
                far_copy(d).start()

        for d, _ in made:
            part_copy(d).start()

    made = project([1, 2])
    highs = jnp.concatenate([rows_of(2 * i + 1) for i in range(n_ma * pairs)], axis=0).astype(bf16)
    ends = lax.dot_general(
        highs, end_op[...].astype(bf16), (((1,), (1,)), ((), ())), preferred_element_type=f32
    )
    end_column = lax.broadcasted_iota(jnp.int32, (fields2, n_ma * 8), 1)
    end_sum = jnp.zeros((fields2, n_ma * 8), f32)
    for i in range(n_ma * pairs):
        at = i // pairs * 8 + i % pairs
        end_sum = jnp.where(end_column == at, ends[i * fields2 : (i + 1) * fields2], end_sum)
    end_sum = jnp.concatenate([end_sum, jnp.zeros((fields2, wide - n_ma * 8), f32)], axis=1)
    end_sum = jnp.transpose(jnp.concatenate([end_sum, jnp.zeros((wide - fields2, wide), f32)], axis=0))
    for d in range(n_ma):
        part[d, body : body + 8] = end_sum[8 * d : 8 * (d + 1)].astype(bf16)

    send(made)
    for i in range(3, n_ma - 1, 2):
        send(project([i, i + 1]))
    made = project([n_ma - 1])
    lower, upper = analyse(0)
    send(made)
    source = jnp.concatenate([lower, end_sum[0:8], upper], axis=0) + own_velocity
    part[0] = source.astype(bf16)

    @pl.when(has_far)
    def _():
        far_copy(0).start()

    wait_blocks(part_in, n_ma - 1, part_recv.at[0])
    for d in range(1, n_ma):
        source = source + part_in[d].astype(f32)

    def end_rows(values):
        turned = jnp.transpose(jnp.concatenate([values, jnp.zeros((wide - 8, wide), f32)], axis=0))[0:fields2]
        return jnp.where(lax.broadcasted_iota(jnp.int32, turned.shape, 1) < pairs, turned, 0.0)

    def level_pair(values, ends):
        made = []
        for k in range(2):
            heads = [values[c * block + 6 * k : c * block + 6 * (k + 1)] for c in range(chunks)]
            made.append(jnp.concatenate(heads + [ends[6 * k : 6 * (k + 1)]], axis=1))
        return made

    turned = end_rows(source[body : body + 8])
    own_levels = level_pair(source[0:body], turned[0:block]) + level_pair(source[body + 8 :], turned[block:fields2])
    for i in range(2):
        near_out[i] = jnp.where(half == 0, own_levels[levels - 2 + i], own_levels[i]).astype(bf16)
    near_copy = remote(near_out, near_in, near_send.at[0], near_recv.at[0], (me, mate_row))
    near_copy.start()

    @pl.when(has_far)
    def _():
        wait_blocks(far_in, n_ma, far_recv.at[0])
        total = far_in[0].astype(f32)
        for d in range(1, n_ma):
            total = total + far_in[d].astype(f32)
        far_sum[...] = total

    @pl.when(jnp.logical_not(has_far))
    def _():
        far_sum[...] = jnp.zeros(far_sum.shape, f32)

    far_body = far_sum[pl.ds(pl.multiple_of((1 - half) * 8, 8), body), :]
    turned = end_rows(far_sum[pl.ds(pl.multiple_of(half * body, 8), 8), :])
    far_levels = level_pair(far_body, jnp.where(half == 0, turned[block:fields2], turned[0:block]))

    wait_blocks(coef_all, n_ma - 1, coef_send.at[0])
    wait_blocks(rest_all, n_ma - 1, rest_send.at[0])
    wait_blocks(part_in, n_ma - 1, part_send.at[0])

    @pl.when(half == 1)
    def _():
        wait_blocks(leg_all, n_ma - 1, leg_send.at[0])
        wait_blocks(leg_all, n_ma - 1, swap_send.at[0])

    @pl.when(has_far)
    def _():
        wait_blocks(far_in, n_ma, far_send.at[0])

    near_copy.wait_recv()

    shape = own_levels[0].shape
    has_left = (row > 0).astype(f32)
    has_right = (row < n_row - 1).astype(f32)
    near_levels = [near_in[i].astype(f32) for i in range(2)]
    before = [jnp.where(half == 0, a, b) for a, b in zip(far_levels, near_levels)]
    after = [jnp.where(half == 0, b, a) for a, b in zip(far_levels, near_levels)]
    wide_levels = before + own_levels + after
    coupling = [jnp.full(shape, dif_ref[lax.rem((row + n_row) * levels + i - 2, n_row * levels)]) for i in range(levels + 4)]
    inverse = [1.0 / (1.0 + 2.0 * c) for c in coupling]
    first = [
        (wide_levels[i] + coupling[i] * (wide_levels[i - 1] + wide_levels[i + 1])) * inverse[i]
        for i in range(1, levels + 3)
    ]
    first[0] = first[0] * has_left
    first[-1] = first[-1] * has_right
    for k in range(levels):
        done = (wide_levels[k + 2] + coupling[k + 2] * (first[k] + first[k + 2])) * inverse[k + 2]
        for p in range(pairs):
            line = jnp.concatenate(
                [done[:, p * orders : (p + 1) * orders], done[:, main + p : main + p + 1]], axis=1
            )
            for i in range(fields2 // levels):
                out_ref[i * levels + k, p : p + 1, :] = line[i : i + 1]
    near_copy.wait_send()


def fused(velocity, vorticity, legendre, pair_order, lat_weight, diffusivity):
    n_ma = lax.axis_size("ma")
    n_row = lax.axis_size("row")
    pairs, rows, half_lat = legendre.shape
    levels = velocity.shape[2]
    orders = rows - 1
    main = pairs * orders
    chunks = main // 128
    lanes = main + 128
    lat = half_lat // n_ma
    slots = 2 * pairs
    full = n_ma * slots
    points = lon_count(orders)
    bf16 = jnp.bfloat16
    f32 = jnp.float32
    groups = 12 * levels
    scale = (NLON / points) / math.sqrt(NLON) / orders
    angle = np.outer(np.arange(orders), np.arange(points)) % points * (2.0 * math.pi / points)
    table = np.stack([np.cos(angle), -np.sin(angle)])
    tab = jnp.asarray(table, bf16)
    tab_t = jnp.asarray(np.transpose(table, (0, 2, 1)), bf16)
    vmem = pl.BlockSpec(memory_space=pltpu.VMEM)
    away = pl.BlockSpec(memory_space=pltpu.HBM)
    operands = (
        velocity.reshape(6 * levels, pairs, rows),
        vorticity.reshape(6 * levels, pairs, rows),
        jnp.transpose(legendre, (1, 0, 2)),
        pair_order,
        lat_weight,
        diffusivity,
        tab,
        tab_t,
    )
    out = pl.pallas_call(
        functools.partial(fused_kernel, n_ma, n_row, pairs, rows, levels, scale),
        out_shape=jax.ShapeDtypeStruct((6 * levels, pairs, rows), f32),
        in_specs=[away] * 8,
        out_specs=vmem,
        scratch_shapes=[
            pltpu.VMEM((6 * levels, pairs, rows), bf16),
            pltpu.VMEM((6 * levels, pairs, rows), bf16),
            pltpu.VMEM((rows, pairs, half_lat), bf16),
            pltpu.SMEM((pairs,), jnp.int32),
            pltpu.VMEM((half_lat,), f32),
            pltpu.SMEM(diffusivity.shape, f32),
            pltpu.VMEM(tab.shape, bf16),
            pltpu.VMEM(tab_t.shape, bf16),
            pltpu.SemaphoreType.DMA((8,)),
            pltpu.VMEM((half_lat // 128, rows * pairs + 4, 128), f32),
            pltpu.VMEM((n_ma, chunks, lat, 128), bf16),
            pltpu.VMEM((n_ma, pairs, 128), bf16),
            pltpu.VMEM((n_ma, chunks, groups, 128), bf16),
            pltpu.VMEM((n_ma, chunks, lat, 128), bf16),
            pltpu.VMEM((n_ma, pairs, 128), bf16),
            pltpu.VMEM((128, 128), f32),
            pltpu.VMEM((n_ma * 8, 128), f32),
            pltpu.VMEM((n_ma * pairs, groups, 128), f32),
            pltpu.VMEM((full, orders), f32),
            pltpu.VMEM((n_ma, pairs * 256, 128), bf16),
            pltpu.VMEM((groups * full, 128), f32),
            pltpu.VMEM((groups // 2 * full, 128), f32),
            pltpu.VMEM((n_ma, chunks * groups // 2 + 8, 128), bf16),
            pltpu.VMEM((n_ma, chunks * groups // 2 + 8, 128), bf16),
            pltpu.VMEM((n_ma, chunks * groups // 4 + 8, 128), bf16),
            pltpu.VMEM((chunks * groups // 4 + 8, 128), f32),
            pltpu.VMEM((2, 6, lanes), bf16),
            pltpu.VMEM((2, 6, lanes), bf16),
        ]
        + [pltpu.SemaphoreType.DMA((count,)) for count in (1, 4, 1, n_ma - 1, 1, 2, 1, 1, 1, 1, 1, 1, 1, 1)]
        + [pltpu.SemaphoreType.REGULAR],
        compiler_params=pltpu.CompilerParams(
            collective_id=0, has_side_effects=True, vmem_limit_bytes=48 * 1024 * 1024
        ),
    )(*(pltpu.with_memory_space_constraint(x, pltpu.HBM) for x in operands))
    return out.reshape(velocity.shape)


def fits(velocity, legendre):
    n_ma = lax.axis_size("ma")
    n_row = lax.axis_size("row")
    pairs, rows, half_lat = legendre.shape
    levels = velocity.shape[2]
    lat = half_lat // n_ma
    tiles = pairs == 4 and pairs * (rows - 1) == 256 and n_ma == 8 and n_row % 2 == 0
    whole = half_lat % n_ma == 0 and half_lat % 128 == 0 and lat % 16 == 0 and lat < 64 and levels == 4
    return tiles and whole and n_row > 2 and n_ma > 1


def step(velocity, vorticity, legendre, pair_order, lat_weight, diffusivity):
    chosen = fused if fits(velocity, legendre) else local
    return chosen(velocity, vorticity, legendre, pair_order, lat_weight, diffusivity)


def solution(mesh):
    in_specs = (
        P(None, None, "row", "ma", None),
        P(None, None, "row", "ma", None),
        P("ma", None, None),
        P("ma"),
        P(),
        P(),
    )
    out_specs = P(None, None, "row", "ma", None)
    return jax.shard_map(step, mesh=mesh, in_specs=in_specs, out_specs=out_specs, check_vma=False)
```

```python
import functools
import math

import jax
import jax.numpy as jnp
import numpy as np
from jax import lax
from jax.experimental import pallas as pl
from jax.experimental.pallas import tpu as pltpu
from jax.sharding import PartitionSpec as P

NLON = 2048


STEP_SIZE = 1.0


def with_halo(cells, sides, width):
    for axis, dim in sides:
        count = lax.axis_size(axis)
        ends = count - 1
        head = lax.slice_in_dim(cells, 0, width, axis=dim)
        tail = lax.slice_in_dim(cells, cells.shape[dim] - width, cells.shape[dim], axis=dim)
        cells = jnp.concatenate(
            [
                lax.ppermute(tail, axis, [(i, (i + 1) % count) for i in range(ends)]),
                cells,
                lax.ppermute(head, axis, [((i + 1) % count, i) for i in range(ends)]),
            ],
            axis=dim,
        )
    return cells


def row_masks(low_order, pack_rows):
    orders_all = pack_rows - 1
    row_index = jnp.arange(pack_rows, dtype=jnp.int32)[None, :]
    low_column = low_order[:, None]
    is_lower = row_index < orders_all - low_column
    not_lower = jnp.logical_not(is_lower)
    even_low = row_index % 2 == 0
    even_high = (row_index + low_column) % 2 == 0
    low_pair = jnp.stack([is_lower & even_low, is_lower & jnp.logical_not(even_low)])
    high_pair = jnp.stack([not_lower & even_high, not_lower & jnp.logical_not(even_high)])
    return jnp.stack([low_pair, high_pair])


def cross_product(velocity_grid, vorticity_grid):
    return jnp.stack(
        [
            velocity_grid[1] * vorticity_grid[2] - velocity_grid[2] * vorticity_grid[1],
            velocity_grid[2] * vorticity_grid[0] - velocity_grid[0] * vorticity_grid[2],
            velocity_grid[0] * vorticity_grid[1] - velocity_grid[1] * vorticity_grid[0],
        ]
    )


def lon_table(column_order, is_imag, lon_start, lon_count):
    lon_index = lon_start + jnp.arange(lon_count, dtype=jnp.int32)
    angle_index = column_order[:, None] * lon_index[None, :] % NLON
    angle_value = angle_index.astype(jnp.float32) * (2.0 * math.pi / NLON)
    return jnp.where(is_imag[:, None], -jnp.sin(angle_value), jnp.cos(angle_value))


def local(velocity, vorticity, legendre, pair_order, lat_weight, diffusivity):
    pair_count = pair_order.shape[0]
    pack_rows = legendre.shape[1]
    half_lat = legendre.shape[2]
    nlat_all = 2 * half_lat
    levels_dev = velocity.shape[2]
    orders_all = pack_rows - 1
    inv_orders = 1.0 / math.sqrt(orders_all)
    inv_lon = 1.0 / math.sqrt(NLON)
    lon_width = NLON // 4
    mask_bool = row_masks(pair_order, pack_rows)
    fields = jnp.concatenate([velocity, vorticity], axis=0)
    masked = fields[None, None] * mask_bool.astype(jnp.bfloat16)[:, :, None, None, None]
    halves = jnp.einsum(
        "oqfilsr,srj->qfliosj", masked, legendre, preferred_element_type=jnp.float32
    )
    north_part = halves[0] + halves[1]
    south_part = halves[0] - halves[1]
    both_parts = jnp.concatenate([north_part, south_part], axis=-1)
    spectral = jnp.transpose(both_parts, (0, 1, 5, 2, 3, 4))
    spectral = spectral.reshape(6, levels_dev, nlat_all, 4 * pair_count).astype(jnp.bfloat16)
    gathered_ids = lax.all_gather(pair_order, "ma", axis=0, tiled=True)
    pair_slots = gathered_ids.reshape(-1, 1, 1, pair_count)
    both_orders = jnp.concatenate([pair_slots, orders_all - 1 - pair_slots], axis=2)
    full_shape = (both_orders.shape[0], 2, 2, pair_count)
    column_order = jnp.broadcast_to(both_orders, full_shape).reshape(-1)
    part_index = jnp.arange(2, dtype=jnp.int32)[None, :, None, None]
    is_imag = jnp.broadcast_to(part_index, full_shape).reshape(-1) == 1
    tables = [
        lon_table(column_order, is_imag, lon_block * lon_width, lon_width).astype(jnp.bfloat16)
        for lon_block in range(4)
    ]
    spec_block = lax.all_to_all(spectral, "ma", split_axis=2, concat_axis=3, tiled=True)
    accumulated = jnp.zeros((3,) + spec_block.shape[1:], jnp.float32)
    for lon_block in range(4):
        table_block = tables[lon_block]
        grid_values = (
            jnp.einsum("flac,cb->flab", spec_block, table_block, preferred_element_type=jnp.float32)
            * inv_orders
        )
        lamb_vector = cross_product(grid_values[:3], grid_values[3:])
        accumulated = accumulated + jnp.einsum(
            "flab,cb->flac",
            lamb_vector,
            table_block.astype(jnp.float32),
            precision=lax.Precision.HIGH,
            preferred_element_type=jnp.float32,
        )
    lamb_spec = (accumulated * inv_lon).astype(jnp.bfloat16)
    selector = jnp.transpose(mask_bool.astype(jnp.float32), (1, 0, 2, 3))[:, None, None, None]
    lamb_block = lax.all_to_all(lamb_spec, "ma", split_axis=3, concat_axis=2, tiled=True)
    item_count = lamb_block.shape[0]
    shaped = lamb_block.astype(jnp.float32).reshape(
        item_count, levels_dev, nlat_all, 2, 2, pair_count
    )
    shaped = jnp.transpose(shaped, (0, 1, 3, 4, 5, 2))
    north_side = shaped[..., :half_lat]
    south_side = shaped[..., half_lat:]
    weighted = jnp.stack(
        [lat_weight * (north_side + south_side), lat_weight * (north_side - south_side)]
    )
    weighted = weighted.astype(jnp.bfloat16)
    projected = jnp.einsum(
        "qfliosj,srj->qfliosr", weighted, legendre, preferred_element_type=jnp.float32
    )
    picked = jnp.sum(projected * selector, axis=(0, 4))
    tendency = jnp.transpose(picked, (0, 2, 1, 3, 4))
    source = velocity.astype(jnp.float32) + STEP_SIZE * tendency
    row_start = lax.axis_index("row") * levels_dev
    level_total = levels_dev * lax.axis_size("row")
    extended = with_halo(source.astype(jnp.bfloat16), (("row", 2),), 2).astype(source.dtype)
    padded_coupling = jnp.pad(diffusivity, (2, 2))
    wide_coupling = lax.dynamic_slice_in_dim(padded_coupling, row_start, levels_dev + 4)[
        None, None, :, None, None
    ]
    inner_coupling = wide_coupling[:, :, 1:-1]
    first_wide = (
        extended[:, :, 1:-1] + inner_coupling * (extended[:, :, :-2] + extended[:, :, 2:])
    ) / (1.0 + 2.0 * inner_coupling)
    global_level = row_start - 1 + jnp.arange(levels_dev + 2, dtype=jnp.int32)
    inside = ((global_level >= 0) & (global_level < level_total)).astype(jnp.float32)
    first_wide = first_wide * inside[None, None, :, None, None]
    own_coupling = wide_coupling[:, :, 2:-2]
    return (source + own_coupling * (first_wide[:, :, :-2] + first_wide[:, :, 2:])) / (
        1.0 + 2.0 * own_coupling
    )

def lon_count(orders_all):
    need = 3 * (orders_all - 1) + 1
    return min(NLON, -(-need // 64) * 64)


def remote(src, dst, send_sem, recv_sem, device_id):
    return pltpu.make_async_remote_copy(
        src_ref=src,
        dst_ref=dst,
        send_sem=send_sem,
        recv_sem=recv_sem,
        device_id=device_id,
        device_id_type=pl.DeviceIdType.MESH,
    )


def fused_kernel(
    n_ma, n_row, pairs, rows, levels, scale,
    velocity_hbm, vorticity_hbm, legendre_hbm, order_hbm, weight_hbm, dif_hbm, tab_hbm, tab_t_hbm,
    out_ref,
    velocity_ref, vorticity_ref, legendre_ref, order_ref, weight_ref, dif_ref, tab_ref, tab_t_ref, load_sem,
    leg_rows, leg_ref, rest_ref, coef_all, leg_all, rest_all, rest_t, end_op, end_spec, onehot, ops, spec, wgt, part, part_in, far_in, far_sum, near_out, near_in,
    coef_send, coef_recv, leg_send, leg_recv, swap_send, swap_recv, rest_send, rest_recv, part_send, part_recv, far_send, far_recv, near_send, near_recv, ready,
):
    me = lax.axis_index("ma")
    row = lax.axis_index("row")
    _, chunks, groups, wide = coef_all.shape
    coef_ref = coef_all.at[0]
    fields2 = groups // 2
    orders = rows - 1
    slots = 2 * pairs
    full = n_ma * slots
    lat = leg_ref.shape[2]
    side = wide // 2
    main = pairs * orders
    per_chunk = pairs // chunks
    f32 = jnp.float32
    bf16 = jnp.bfloat16
    n_z = n_ma // 2
    z, y = me // 2, lax.rem(me, 2)
    mate = me + 1 - 2 * y
    upper_z = z // (n_z // 2)
    half = lax.rem(row, 2)
    mate_row = row + 1 - 2 * half

    def target(s):
        return lax.rem(z + s // 2, n_z) * 2 + lax.rem(y + lax.rem(s, 2), 2)

    def origin(s):
        return lax.rem(z + n_z - s // 2, n_z) * 2 + lax.rem(y + lax.rem(s, 2), 2)

    far_row = row + 2 * half - 1
    has_far = (far_row >= 0) & (far_row < n_row)

    barrier = pltpu.get_barrier_semaphore()
    for d in range(1, n_ma):
        pl.semaphore_signal(
            barrier, inc=1, device_id=(lax.rem(me + d, n_ma), row), device_id_type=pl.DeviceIdType.MESH
        )
    pl.semaphore_signal(barrier, inc=1, device_id=(me, mate_row), device_id_type=pl.DeviceIdType.MESH)

    @pl.when(has_far)
    def _():
        pl.semaphore_signal(barrier, inc=1, device_id=(me, far_row), device_id_type=pl.DeviceIdType.MESH)

    loads = [
        pltpu.make_async_copy(src, dst, load_sem.at[i])
        for i, (src, dst) in enumerate(
            [
                (legendre_hbm, legendre_ref),
                (velocity_hbm, velocity_ref),
                (vorticity_hbm, vorticity_ref),
                (order_hbm, order_ref),
                (weight_hbm, weight_ref),
                (dif_hbm, dif_ref),
                (tab_hbm, tab_ref),
                (tab_t_hbm, tab_t_ref),
            ]
        )
    ]
    for load in loads:
        load.start()
    for load in loads[:4]:
        load.wait()

    for r in range(rows):
        values = legendre_ref[r].astype(f32)
        for t in range(leg_rows.shape[0]):
            leg_rows[t, r * pairs : (r + 1) * pairs, :] = values[:, t * wide : (t + 1) * wide]
    packs = [
        jnp.concatenate([velocity_ref[...].astype(f32)[:, p], vorticity_ref[...].astype(f32)[:, p]], axis=0)
        for p in range(pairs)
    ]
    column = lax.broadcasted_iota(jnp.int32, (groups, wide), 1)
    ends = jnp.zeros((groups, wide), f32)
    for p in range(pairs):
        ends = jnp.where(column == p, packs[p][:, orders:], ends)
    ends = jnp.concatenate([ends, jnp.zeros((wide - groups, wide), f32)], axis=0)
    ends = jnp.transpose(ends)[0:pairs, 0:side]
    tails = jnp.concatenate([leg_rows[t, main : main + pairs, :] for t in range(leg_rows.shape[0])], axis=1)
    order_rows = [jnp.full((1, side - lat), order_ref[p].astype(f32)) for p in range(pairs)]
    filler = jnp.concatenate(order_rows, axis=0)
    for b in range(n_ma):
        data_rows = jnp.concatenate([ends, tails[:, b * lat : (b + 1) * lat], filler], axis=1)
        rest_ref[b] = data_rows.astype(bf16)
    for c in range(chunks):
        members = range(c * per_chunk, (c + 1) * per_chunk)
        coef_all[0, c] = jnp.concatenate([packs[p][:, :orders] for p in members], axis=1).astype(bf16)
        turned = jnp.concatenate(
            [
                jnp.transpose(
                    jnp.concatenate([leg_rows[t, pl.ds(p, orders, stride=pairs), :] for p in members], axis=0)
                )
                for t in range(leg_rows.shape[0])
            ],
            axis=0,
        ).astype(bf16)
        for b in range(n_ma):
            leg_ref[b, c] = turned[b * lat : (b + 1) * lat]

    pl.semaphore_wait(barrier, n_ma + has_far.astype(jnp.int32))

    passed = [s for s in (4,) if s < n_ma]
    gained = [s + 1 for s in passed]
    far_first = sorted(range(1, n_ma), key=lambda s: (-min(s // 2, n_z - s // 2), -(s // 2), s % 2))
    direct = [s for s in (7, 3, 6, 2, 1) if s < n_ma]
    coef_groups = [[s] for s in passed] + [direct[:2], direct[2:], gained]
    leg_groups = [far_first[: n_ma // 2], far_first[n_ma // 2 :]]

    def wait_blocks(ref, count, sem):
        blocks = ref.at[pl.ds(0, count)]
        pltpu.make_async_copy(blocks, blocks, sem).wait()

    def coef_copy(s, group=None):
        if group is None:
            group = [s in g for g in coef_groups].index(True)
        if group == len(coef_groups) - 1:
            return remote(coef_all.at[s - 1], coef_all.at[s], coef_send.at[0], coef_recv.at[group], (mate, row))
        return remote(coef_ref, coef_all.at[s], coef_send.at[0], coef_recv.at[group], (target(s), row))

    def leg_copy(s):
        peer = target(s)
        return remote(leg_ref.at[peer], leg_all.at[s], leg_send.at[0], leg_recv.at[s - 1], (peer, row))

    def share_copy(s):
        group = [s in g for g in leg_groups].index(True)
        return remote(leg_all.at[s], leg_all.at[s], swap_send.at[0], swap_recv.at[group], (me, mate_row))

    def rest_copy(s):
        peer = target(s)
        return remote(rest_ref.at[peer], rest_all.at[s], rest_send.at[0], rest_recv.at[0], (peer, row))

    for s in far_first:
        rest_copy(s).start()
    for s in passed:
        coef_copy(s).start()

    @pl.when(half == 1)
    def _():
        for j in range(n_z - 1):
            delta = upper_z * (1 + j) + (1 - upper_z) * (n_z - 1 - j)
            leg_copy(2 * delta).start()
            leg_copy(2 * delta + 1).start()
        leg_copy(1).start()

    for dy in (1, 0):
        coef_copy(upper_z * (2 + dy) + (1 - upper_z) * (6 + dy), group=1 + (1 - dy)).start()
        coef_copy(upper_z * (6 + dy) + (1 - upper_z) * (2 + dy), group=1 + (1 - dy)).start()
    coef_copy(1, group=2).start()

    @pl.when(has_far)
    def _():
        pl.semaphore_signal(ready, inc=1, device_id=(me, far_row), device_id_type=pl.DeviceIdType.MESH)

    leg_all[0] = leg_ref[me]
    rest_all[0] = rest_ref[me]

    def clear(d, carry):
        ops[d] = jnp.zeros(ops.shape[1:], bf16)
        return carry

    lax.fori_loop(0, n_ma, clear, 0)
    for load in loads[4:]:
        load.wait()
    weight = jnp.zeros((1, lat), f32)
    for b in range(n_ma):
        weight = jnp.where(me == b, weight_ref[...].reshape(1, -1)[:, b * lat : (b + 1) * lat], weight)
    weight = weight * scale
    gap = jnp.zeros((1, side - lat), f32)
    weight = jnp.concatenate([weight, gap, weight, gap] * 2, axis=1)

    lane = lax.broadcasted_iota(jnp.int32, (pairs, wide), 1)
    sub = lax.broadcasted_iota(jnp.int32, (pairs, wide), 0)
    m_lane = lax.broadcasted_iota(jnp.int32, (slots, orders), 1)
    m_sub = lax.broadcasted_iota(jnp.int32, (slots, orders), 0)
    lane_row = lane % orders
    own = lane // orders == sub % per_chunk

    def low_orders(d):
        held_order = rest_all[d].astype(f32)[:, side + lat : side + lat + 1]
        return jnp.broadcast_to(held_order, (pairs, wide)).astype(jnp.int32)

    def place(d):
        low = low_orders(d)
        order = jnp.zeros((slots, orders), jnp.int32)
        for p in range(pairs):
            value = low[p : p + 1, 0:1]
            order = jnp.where(m_sub == 2 * p, value, order)
            order = jnp.where(m_sub == 2 * p + 1, orders - 1 - value, order)
        onehot[d * slots : (d + 1) * slots, :] = (m_lane == order).astype(f32)

    def build(d):
        low = low_orders(d)
        lower = lane_row < orders - low
        north_low = (own & lower).astype(f32)
        north_high = (own & jnp.logical_not(lower)).astype(f32)
        south_low = north_low * (1 - 2 * (lane_row & 1)).astype(f32)
        south_high = north_high * (1 - 2 * ((lane_row + low) & 1)).astype(f32)
        for p in range(pairs):
            c = p // per_chunk
            table = leg_all[d, c].astype(f32)
            at = p * 2 * wide
            for i, factor in enumerate((north_low, south_low, north_high, south_high)):
                ops[d, at + i * side : at + i * side + lat, :] = (table * factor[p : p + 1]).astype(bf16)

    def synth(d):
        for p in range(pairs):
            at = p * 2 * wide
            made = lax.dot_general(
                coef_all[d, p // per_chunk],
                ops[d, at : at + 2 * wide, :],
                (((1,), (1,)), ((), ())),
                preferred_element_type=f32,
            )
            spec[pl.ds(d * slots + 2 * p, groups, stride=full), :] = made[:, :wide]
            spec[pl.ds(d * slots + 2 * p + 1, groups, stride=full), :] = made[:, wide:] + end_spec[d * pairs + p]

    for i, s in enumerate(passed):
        wait_blocks(coef_all, 1, coef_recv.at[i])
        coef_copy(s + 1).start()
    wait_blocks(rest_all, n_ma - 1, rest_recv.at[0])

    def legs(group):
        @pl.when(half == 1)
        def _():
            for s in leg_groups[group]:
                leg_copy(s).wait_recv()
                share_copy(s).start()

        @pl.when(half == 0)
        def _():
            wait_blocks(leg_all, len(leg_groups[group]), swap_recv.at[group])

    rest = []
    for d in range(n_ma):
        rest += [rest_all[d].astype(f32), low_orders(d).astype(f32)]
    rest = jnp.concatenate(rest, axis=0)
    rest_t[...] = jnp.transpose(jnp.concatenate([rest, jnp.zeros((wide - n_ma * 8, wide), f32)], axis=0))
    end_lane = lax.broadcasted_iota(jnp.int32, rest.shape, 1)
    end_sign = (1 - 2 * (pltpu.roll(rest, n_ma * 8 - pairs, 0).astype(jnp.int32) & 1)).astype(f32)
    north_end = jnp.where(end_lane < lat, pltpu.roll(rest, side, 1), 0.0)
    south_end = jnp.where((end_lane >= side) & (end_lane < side + lat), rest * end_sign, 0.0)
    end_op[...] = north_end + south_end
    for d in range(n_ma):
        place(d)
    hot = onehot[...].astype(bf16)
    to_grid = jnp.concatenate(
        [
            lax.dot_general(tab_t_ref[c], hot, (((1,), (1,)), ((), ())), preferred_element_type=f32)
            for c in range(2)
        ],
        axis=1,
    ).astype(bf16)
    to_spec = jnp.concatenate(
        [jnp.dot(hot, tab_ref[c], preferred_element_type=f32) for c in range(2)], axis=0
    ).astype(bf16)
    for d in range(n_ma):
        for p in range(pairs):
            i = 8 * d + p
            end_spec[d * pairs + p] = rest_t[0:groups, i : i + 1] * end_op[i : i + 1, :]
    held = [coef_ref[c, 0:fields2].astype(f32) for c in range(chunks)]
    held = jnp.concatenate(held + [rest_t[0:fields2, :]], axis=1)
    held = held.reshape(6, levels, held.shape[1])
    held = [held[:, k, :] for k in range(levels)]
    block = 6 * levels // 2
    lower = jnp.concatenate([held[k][:, c * wide : (c + 1) * wide] for c in range(chunks) for k in (0, 1)], axis=0)
    upper = jnp.concatenate([held[k][:, c * wide : (c + 1) * wide] for c in range(chunks) for k in (2, 3)], axis=0)
    own_end = jnp.concatenate([h[:, main:] for h in held] + [jnp.zeros((wide - fields2, wide), f32)], axis=0)
    own_end = jnp.where(lax.broadcasted_iota(jnp.int32, own_end.shape, 1) < pairs, own_end, 0.0)
    own_velocity = jnp.concatenate([lower, jnp.transpose(own_end)[0:8], upper], axis=0)
    build(0)
    synth(0)
    legs(0)
    for s in leg_groups[0]:
        build(s)
    for s in passed:
        synth(s)
    legs(1)
    for s in leg_groups[1]:
        build(s)
    for group in range(len(passed), len(coef_groups)):
        wait_blocks(coef_all, len(coef_groups[group]), coef_recv.at[group])
        for s in coef_groups[group]:
            synth(s)

    def middle(j):
        grids = []
        for f in range(6):
            blocks = []
            for i in range(2):
                k = 2 * j + i
                parts = [
                    spec[pl.ds(((f * 2 + c) * levels + k) * full, full), :] for c in range(2)
                ]
                blocks.append(jnp.concatenate(parts, axis=0))
            block = jnp.concatenate(blocks, axis=1).astype(bf16)
            grids.append(jnp.dot(to_grid, block, preferred_element_type=f32))
        u, w = grids[:3], grids[3:]
        lamb = [
            u[1] * w[2] - u[2] * w[1],
            u[2] * w[0] - u[0] * w[2],
            u[0] * w[1] - u[1] * w[0],
        ]
        for f in range(3):
            made = jnp.dot(to_spec, lamb[f].astype(bf16), preferred_element_type=f32) * weight
            for i in range(2):
                k = 2 * j + i
                for c in range(2):
                    at = (k * 6 + f * 2 + c) * full
                    wgt[pl.ds(at, full), :] = made[c * full : (c + 1) * full, i * wide : (i + 1) * wide]

    for j in range(levels // 2):
        middle(j)

    def part_copy(d):
        return remote(part.at[d], part_in.at[d], part_send.at[0], part_recv.at[0], (origin(d), row))

    def rows_of(slot):
        return wgt[pl.ds(slot, fields2, stride=full), :]

    def analyse(d):
        heads = []
        for c in range(chunks):
            picked = [rows_of(d * slots + i) for i in range(2 * c * per_chunk, 2 * (c + 1) * per_chunk)]
            lhs = jnp.concatenate(picked, axis=1).astype(bf16)
            first = c * per_chunk * 2 * wide
            heads.append(
                jnp.dot(lhs, ops[d, first : first + per_chunk * 2 * wide, :], preferred_element_type=f32)
            )
        lower = jnp.concatenate([h[:block] for h in heads], axis=0)
        upper = jnp.concatenate([h[block:] for h in heads], axis=0)
        return lower, upper

    body = chunks * block
    sent = pl.ds(pl.multiple_of(half * body, 8), body + 8)

    def far_copy(d):
        return remote(part.at[d, sent], far_in.at[d], far_send.at[0], far_recv.at[0], (origin(d), far_row))

    @pl.when(has_far)
    def _():
        pl.semaphore_wait(ready, 1)

    def project(steps):
        made = []
        for i in steps:
            d = upper_z * (n_ma - i) + (1 - upper_z) * (1 + lax.rem(i, n_ma - 1))
            made.append((d, analyse(d)))
        return made

    def send(made):
        for d, (lower, upper) in made:
            part[d, 0:body] = lower.astype(bf16)
            part[d, body + 8 :] = upper.astype(bf16)
        @pl.when(has_far)
        def _():
            for d, _ in made:
                far_copy(d).start()

        for d, _ in made:
            part_copy(d).start()

    made = project([1, 2])
    highs = jnp.concatenate([rows_of(2 * i + 1) for i in range(n_ma * pairs)], axis=0).astype(bf16)
    ends = lax.dot_general(
        highs, end_op[...].astype(bf16), (((1,), (1,)), ((), ())), preferred_element_type=f32
    )
    end_column = lax.broadcasted_iota(jnp.int32, (fields2, n_ma * 8), 1)
    end_sum = jnp.zeros((fields2, n_ma * 8), f32)
    for i in range(n_ma * pairs):
        at = i // pairs * 8 + i % pairs
        end_sum = jnp.where(end_column == at, ends[i * fields2 : (i + 1) * fields2], end_sum)
    end_sum = jnp.concatenate([end_sum, jnp.zeros((fields2, wide - n_ma * 8), f32)], axis=1)
    end_sum = jnp.transpose(jnp.concatenate([end_sum, jnp.zeros((wide - fields2, wide), f32)], axis=0))
    for d in range(n_ma):
        part[d, body : body + 8] = end_sum[8 * d : 8 * (d + 1)].astype(bf16)

    send(made)
    for i in range(3, n_ma - 1, 2):
        send(project([i, i + 1]))
    made = project([n_ma - 1])
    lower, upper = analyse(0)
    send(made)
    source = jnp.concatenate([lower, end_sum[0:8], upper], axis=0) + own_velocity
    part[0] = source.astype(bf16)

    @pl.when(has_far)
    def _():
        far_copy(0).start()

    wait_blocks(part_in, n_ma - 1, part_recv.at[0])
    for d in range(1, n_ma):
        source = source + part_in[d].astype(f32)

    def end_rows(values):
        turned = jnp.transpose(jnp.concatenate([values, jnp.zeros((wide - 8, wide), f32)], axis=0))[0:fields2]
        return jnp.where(lax.broadcasted_iota(jnp.int32, turned.shape, 1) < pairs, turned, 0.0)

    def level_pair(values, ends):
        made = []
        for k in range(2):
            heads = [values[c * block + 6 * k : c * block + 6 * (k + 1)] for c in range(chunks)]
            made.append(jnp.concatenate(heads + [ends[6 * k : 6 * (k + 1)]], axis=1))
        return made

    turned = end_rows(source[body : body + 8])
    own_levels = level_pair(source[0:body], turned[0:block]) + level_pair(source[body + 8 :], turned[block:fields2])
    for i in range(2):
        near_out[i] = jnp.where(half == 0, own_levels[levels - 2 + i], own_levels[i]).astype(bf16)
    near_copy = remote(near_out, near_in, near_send.at[0], near_recv.at[0], (me, mate_row))
    near_copy.start()

    @pl.when(has_far)
    def _():
        wait_blocks(far_in, n_ma, far_recv.at[0])
        total = far_in[0].astype(f32)
        for d in range(1, n_ma):
            total = total + far_in[d].astype(f32)
        far_sum[...] = total

    @pl.when(jnp.logical_not(has_far))
    def _():
        far_sum[...] = jnp.zeros(far_sum.shape, f32)

    far_body = far_sum[pl.ds(pl.multiple_of((1 - half) * 8, 8), body), :]
    turned = end_rows(far_sum[pl.ds(pl.multiple_of(half * body, 8), 8), :])
    far_levels = level_pair(far_body, jnp.where(half == 0, turned[block:fields2], turned[0:block]))

    wait_blocks(coef_all, n_ma - 1, coef_send.at[0])
    wait_blocks(rest_all, n_ma - 1, rest_send.at[0])
    wait_blocks(part_in, n_ma - 1, part_send.at[0])

    @pl.when(half == 1)
    def _():
        wait_blocks(leg_all, n_ma - 1, leg_send.at[0])
        wait_blocks(leg_all, n_ma - 1, swap_send.at[0])

    @pl.when(has_far)
    def _():
        wait_blocks(far_in, n_ma, far_send.at[0])

    near_copy.wait_recv()

    shape = own_levels[0].shape
    has_left = (row > 0).astype(f32)
    has_right = (row < n_row - 1).astype(f32)
    near_levels = [near_in[i].astype(f32) for i in range(2)]
    before = [jnp.where(half == 0, a, b) for a, b in zip(far_levels, near_levels)]
    after = [jnp.where(half == 0, b, a) for a, b in zip(far_levels, near_levels)]
    wide_levels = before + own_levels + after
    coupling = [jnp.full(shape, dif_ref[lax.rem((row + n_row) * levels + i - 2, n_row * levels)]) for i in range(levels + 4)]
    inverse = [1.0 / (1.0 + 2.0 * c) for c in coupling]
    first = [
        (wide_levels[i] + coupling[i] * (wide_levels[i - 1] + wide_levels[i + 1])) * inverse[i]
        for i in range(1, levels + 3)
    ]
    first[0] = first[0] * has_left
    first[-1] = first[-1] * has_right
    for k in range(levels):
        done = (wide_levels[k + 2] + coupling[k + 2] * (first[k] + first[k + 2])) * inverse[k + 2]
        for p in range(pairs):
            line = jnp.concatenate(
                [done[:, p * orders : (p + 1) * orders], done[:, main + p : main + p + 1]], axis=1
            )
            for i in range(fields2 // levels):
                out_ref[i * levels + k, p : p + 1, :] = line[i : i + 1]
    near_copy.wait_send()


def fused(velocity, vorticity, legendre, pair_order, lat_weight, diffusivity):
    n_ma = lax.axis_size("ma")
    n_row = lax.axis_size("row")
    pairs, rows, half_lat = legendre.shape
    levels = velocity.shape[2]
    orders = rows - 1
    main = pairs * orders
    chunks = main // 128
    lanes = main + 128
    lat = half_lat // n_ma
    slots = 2 * pairs
    full = n_ma * slots
    points = lon_count(orders)
    bf16 = jnp.bfloat16
    f32 = jnp.float32
    groups = 12 * levels
    scale = (NLON / points) / math.sqrt(NLON) / orders
    angle = np.outer(np.arange(orders), np.arange(points)) % points * (2.0 * math.pi / points)
    table = np.stack([np.cos(angle), -np.sin(angle)])
    tab = jnp.asarray(table, bf16)
    tab_t = jnp.asarray(np.transpose(table, (0, 2, 1)), bf16)
    vmem = pl.BlockSpec(memory_space=pltpu.VMEM)
    away = pl.BlockSpec(memory_space=pltpu.HBM)
    operands = (
        velocity.reshape(6 * levels, pairs, rows),
        vorticity.reshape(6 * levels, pairs, rows),
        jnp.transpose(legendre, (1, 0, 2)),
        pair_order,
        lat_weight,
        diffusivity,
        tab,
        tab_t,
    )
    out = pl.pallas_call(
        functools.partial(fused_kernel, n_ma, n_row, pairs, rows, levels, scale),
        out_shape=jax.ShapeDtypeStruct((6 * levels, pairs, rows), f32),
        in_specs=[away] * 8,
        out_specs=vmem,
        scratch_shapes=[
            pltpu.VMEM((6 * levels, pairs, rows), bf16),
            pltpu.VMEM((6 * levels, pairs, rows), bf16),
            pltpu.VMEM((rows, pairs, half_lat), bf16),
            pltpu.SMEM((pairs,), jnp.int32),
            pltpu.VMEM((half_lat,), f32),
            pltpu.SMEM(diffusivity.shape, f32),
            pltpu.VMEM(tab.shape, bf16),
            pltpu.VMEM(tab_t.shape, bf16),
            pltpu.SemaphoreType.DMA((8,)),
            pltpu.VMEM((half_lat // 128, rows * pairs + 4, 128), f32),
            pltpu.VMEM((n_ma, chunks, lat, 128), bf16),
            pltpu.VMEM((n_ma, pairs, 128), bf16),
            pltpu.VMEM((n_ma, chunks, groups, 128), bf16),
            pltpu.VMEM((n_ma, chunks, lat, 128), bf16),
            pltpu.VMEM((n_ma, pairs, 128), bf16),
            pltpu.VMEM((128, 128), f32),
            pltpu.VMEM((n_ma * 8, 128), f32),
            pltpu.VMEM((n_ma * pairs, groups, 128), f32),
            pltpu.VMEM((full, orders), f32),
            pltpu.VMEM((n_ma, pairs * 256, 128), bf16),
            pltpu.VMEM((groups * full, 128), f32),
            pltpu.VMEM((groups // 2 * full, 128), f32),
            pltpu.VMEM((n_ma, chunks * groups // 2 + 8, 128), bf16),
            pltpu.VMEM((n_ma, chunks * groups // 2 + 8, 128), bf16),
            pltpu.VMEM((n_ma, chunks * groups // 4 + 8, 128), bf16),
            pltpu.VMEM((chunks * groups // 4 + 8, 128), f32),
            pltpu.VMEM((2, 6, lanes), bf16),
            pltpu.VMEM((2, 6, lanes), bf16),
        ]
        + [pltpu.SemaphoreType.DMA((count,)) for count in (1, 4, 1, n_ma - 1, 1, 2, 1, 1, 1, 1, 1, 1, 1, 1)]
        + [pltpu.SemaphoreType.REGULAR],
        compiler_params=pltpu.CompilerParams(
            collective_id=0, has_side_effects=True, vmem_limit_bytes=48 * 1024 * 1024
        ),
    )(*(pltpu.with_memory_space_constraint(x, pltpu.HBM) for x in operands))
    return out.reshape(velocity.shape)


def fits(velocity, legendre):
    n_ma = lax.axis_size("ma")
    n_row = lax.axis_size("row")
    pairs, rows, half_lat = legendre.shape
    levels = velocity.shape[2]
    lat = half_lat // n_ma
    tiles = pairs == 4 and pairs * (rows - 1) == 256 and n_ma == 8 and n_row % 2 == 0
    whole = half_lat % n_ma == 0 and half_lat % 128 == 0 and lat % 16 == 0 and lat < 64 and levels == 4
    return tiles and whole and n_row > 2 and n_ma > 1


def step(velocity, vorticity, legendre, pair_order, lat_weight, diffusivity):
    chosen = fused if fits(velocity, legendre) else local
    return chosen(velocity, vorticity, legendre, pair_order, lat_weight, diffusivity)


def solution(mesh):
    in_specs = (
        P(None, None, "row", "ma", None),
        P(None, None, "row", "ma", None),
        P("ma", None, None),
        P("ma"),
        P(),
        P(),
    )
    out_specs = P(None, None, "row", "ma", None)
    return jax.shard_map(step, mesh=mesh, in_specs=in_specs, out_specs=out_specs, check_vma=False)
```
